32 devices in a mesh: expert: 8 (over y, x, core), replica: 4 (over z).
Axes of the slice: x: 2, y: 2, z: 4, core: 2. Of those that a mesh axis runs over, the one named last changes fastest.
Arguments:
- tokens: bfloat16 [8192, 7168], P(('expert', 'replica')), may hold values from -40 to 40
- routes: int32 [8192, 8], P(('expert', 'replica')), may hold values from 0 to 255, all different within a row
- gate_weight: bfloat16 [7168, 4096], P(None, 'expert'), may hold values from -0.0625 to 0.0625
- up_weight: bfloat16 [7168, 4096], P(None, 'expert'), may hold values from -0.0625 to 0.0625
Outputs:
- calibrated: bfloat16 [512, 4096], P(('expert', 'replica'))
The draws below stay inside these ranges and needn't reach their ends.
Inputs may be any that keep to these rules, and one draw needn't show every extreme that they name: `routes`: each row names 8 different experts of the layer, and every expert is named by some row.
All inputs are finite; a program needn't handle non-finite values.
Results may differ from the reference program's by a relative error of at most 0.001.
Values may be sent and summed in bfloat16 or wider, within the bound.
A program may use at most 128 MiB of HBM per device.

```python
import math
import jax
import jax.numpy as jnp
from jax import lax

D = 7168
FF = 2048
ROUTED = 256
TOP = 8
CAP = 16
KMOM = 12
QITERS = 4
TOK_DEV = 256
EXPERTS = 2
TOKENS = 8192
N_EXPERT = 8
N_REPLICA = 4


def draw_tokens(key, part):
    key_base = jax.random.fold_in(key, 0)
    key_scale = jax.random.fold_in(key, 2)
    source = jnp.arange(TOKENS, dtype=jnp.int32) // TOK_DEV
    replica_pos = (source % N_REPLICA).astype(jnp.float32)
    replica_ramp = jnp.sqrt(1.0 + 2.0 * replica_pos / max(N_REPLICA - 1, 1))
    values = jax.random.truncated_normal(key_base, -6.0, 6.0, (TOKENS, D), jnp.float32)
    spread = jnp.exp(jax.random.uniform(key_scale, (TOKENS,), jnp.float32, -0.5, 0.5) * math.log(10.0))
    return (values * (spread * replica_ramp)[:, None]).astype(jnp.bfloat16)


def block_scale(stream_key, extent, pieces, low, high):
    loudness, own = 1.0, jax.random.fold_in(stream_key, 6)
    for dim, shards_of in pieces:
        draws = jnp.exp(jax.random.uniform(jax.random.fold_in(own, dim), (shards_of,), jnp.float32, low / len(pieces), high / len(pieces)))
        loudness = loudness * jnp.repeat(draws, extent[dim] // shards_of).reshape([-1 if axis == dim else 1 for axis in range(len(extent))])
    return loudness


def choose_distinct(stream_key, rows, amount, top, lift):
    ranking = jax.random.permutation(jax.random.fold_in(stream_key, 1), amount)
    pull = ranking
    for power in range(3):
        pull = pull * pull // amount
    pull = pull * lift // amount
    chance = jax.random.randint(jax.random.fold_in(stream_key, 2), (rows, amount), 0, 4096) + pull
    sure = jax.random.permutation(jax.random.fold_in(stream_key, 3), rows)[jnp.arange(amount) % rows]
    chance = jnp.where(jnp.arange(rows)[:, None] == sure[None, :], 1 << 14, chance)
    priority = chance * amount + jnp.arange(amount)
    return lax.top_k(priority.astype(jnp.int32), top)[1].astype(jnp.int32)


def noise(key, dims, deviation, limit, cuts=(), held_as=jnp.bfloat16):
    values = deviation * jax.random.normal(key, dims, jnp.float32)
    if cuts:
        values = values * block_scale(key, dims, cuts, -0.22, 0.18)
    return jnp.clip(values, -limit, limit).astype(held_as)


def setup_inputs(seed: int = 0) -> dict:
    splits = jax.random.split(jax.random.key(seed), 5)
    return {
        "tokens": draw_tokens(jax.random.fold_in(splits[4], 71), 0),
        "routes": choose_distinct(splits[1], TOKENS, ROUTED, TOP, 256),
        "gate_weight": noise(splits[2], (D, EXPERTS * FF), D ** -0.5, 0.0625, ((1, 8),)),
        "up_weight": noise(splits[3], (D, EXPERTS * FF), D ** -0.5, 0.0625, ((1, 8),)),
    }


QUANTILE_LEVEL = 0.99
EPSILON = 1e-6


def slot_table(route_block):
    window = jnp.arange(EXPERTS, dtype=jnp.int32)
    naming = jnp.sum((route_block[:, :, None] == window[None, None, :]).astype(jnp.int32), axis=1)
    before = jnp.cumsum(naming, axis=0) - naming
    positions = jnp.arange(CAP, dtype=jnp.int32)
    chosen = naming[:, :, None] * (before[:, :, None] == positions[None, None, :]).astype(jnp.int32)
    token_ids = jnp.arange(route_block.shape[0], dtype=jnp.int32)
    picked = jnp.sum(chosen * token_ids[:, None, None], axis=0)
    filled = jnp.sum(chosen, axis=0)
    return picked, filled


def chebyshev_sums(scaled, occupied):
    previous = jnp.ones_like(scaled)
    current = scaled
    totals = [jnp.sum(occupied[:, None] * previous, axis=0), jnp.sum(occupied[:, None] * current, axis=0)]
    for degree in range(2, KMOM):
        previous, current = current, 2.0 * scaled * current - previous
        totals.append(jnp.sum(occupied[:, None] * current, axis=0))
    return jnp.stack(totals[:KMOM])


def clip_fraction(moments, counted):
    coefficient = moments[1:] / counted[None, :]
    orders = jnp.arange(1, KMOM, dtype=jnp.float32)[:, None]
    angles = jnp.full(moments.shape[1:], 0.5 * math.pi, jnp.float32)
    for iteration in range(QITERS):
        lower_mass = 1.0 - angles / math.pi - (2.0 / math.pi) * jnp.sum(coefficient * jnp.sin(orders * angles[None, :]) / orders, axis=0)
        angles = angles + math.pi * (lower_mass - QUANTILE_LEVEL)
    return 0.5 * (1.0 + jnp.cos(angles))


def take_block(packed):
    tok_block, slot_ids, occupied = packed
    gathered = jnp.take(tok_block, slot_ids.reshape(-1), axis=0).reshape(EXPERTS, CAP, D)
    return jnp.where(occupied[:, :, None] > 0, gathered, jnp.zeros_like(gathered))


def reference(tokens, routes, gate_weight, up_weight):
    sources = N_EXPERT * N_REPLICA
    tok_blocks = tokens.reshape(sources, TOK_DEV, D)
    route_blocks = routes.reshape(sources, TOK_DEV, TOP)
    picked, filled = lax.map(slot_table, route_blocks)
    dispatched = lax.map(take_block, (tok_blocks, picked, filled))

    def one_expert(expert_id):
        slab = lax.dynamic_index_in_dim(dispatched, expert_id, 1, keepdims=False).reshape(sources * CAP, D)
        occupied = lax.dynamic_index_in_dim(filled, expert_id, 1, keepdims=False).reshape(sources * CAP).astype(jnp.float32)
        gate_cols = lax.dynamic_slice_in_dim(gate_weight, expert_id * FF, FF, 1)
        up_cols = lax.dynamic_slice_in_dim(up_weight, expert_id * FF, FF, 1)
        gate_act = jnp.dot(slab, gate_cols, preferred_element_type=jnp.float32)
        up_act = jnp.dot(slab, up_cols, preferred_element_type=jnp.float32)
        hidden = jax.nn.silu(gate_act) * up_act
        magnitude = jnp.abs(hidden)
        ceiling = jnp.max(magnitude, axis=0) + EPSILON
        scaled = 2.0 * magnitude / ceiling - 1.0
        moments = chebyshev_sums(scaled, occupied)
        clip_level = ceiling * clip_fraction(moments, moments[0])
        result = jnp.clip(hidden, -clip_level, clip_level) / ceiling
        return result.astype(jnp.bfloat16).reshape(sources, CAP, FF)

    results = lax.map(one_expert, jnp.arange(EXPERTS, dtype=jnp.int32))
    return results.transpose(1, 2, 0, 3).reshape(sources * CAP, EXPERTS * FF)
```

```python
import functools
import math

import jax
import jax.numpy as jnp
from jax import lax
from jax.experimental import pallas as pl
from jax.experimental.pallas import tpu as pltpu
from jax.sharding import PartitionSpec as P

HSPLIT = 4
CAP = 16
KMOM = 12
QITERS = 4
LANES = 128
UNIT = 512
ROWS = 32
SKETCH = 12

QUANTILE_LEVEL = 0.99
EPSILON = 1e-06
MESH = pl.DeviceIdType.MESH

PI_HIGH = 3.140625
PI_LOW = math.pi - PI_HIGH
SIN_TERMS = [(-1.0) ** i / math.factorial(2 * i + 1) for i in range(7)]
COS_TERMS = [(-1.0) ** i / math.factorial(2 * i) for i in range(8)]


def horner(square, terms):
    total = jnp.full_like(square, terms[-1])
    for term in terms[-2::-1]:
        total = total * square + term
    return total


def sin_cos(angle):
    turns = jnp.floor(angle * (1.0 / math.pi) + 0.5)
    rest = (angle - turns * PI_HIGH) - turns * PI_LOW
    sign = 1.0 - 2.0 * (turns - 2.0 * jnp.floor(turns * 0.5))
    square = rest * rest
    return sign * rest * horner(square, SIN_TERMS), sign * horner(square, COS_TERMS)


def clip_fraction(coefficient):
    start = (1.0 - QUANTILE_LEVEL) * math.pi
    total = jnp.zeros_like(coefficient[0])
    for k in range(1, KMOM, 2):
        total = total + coefficient[k - 1] * ((1.0 if k % 4 == 1 else -1.0) / k)
    angle = start - 2.0 * total
    for _ in range(QITERS - 1):
        sine, cosine = sin_cos(angle)
        double = 2.0 * cosine
        before, current = jnp.zeros_like(sine), sine
        total = jnp.zeros_like(sine)
        for k in range(1, KMOM):
            total = total + coefficient[k - 1] * (current * (1.0 / k))
            before, current = current, double * current - before
        angle = start - 2.0 * total
    return 0.5 * (1.0 + sin_cos(angle)[1])


def rebase(moments, ratio):
    shift = ratio - 1.0
    before = moments
    current = [
        0.5 * ratio * (before[j + 1] + before[abs(j - 1)]) + shift * before[j]
        for j in range(KMOM - 1)
    ]
    out = [current[0]]
    twice = 2.0 * shift
    for k in range(1, KMOM - 1):
        following = [
            ratio * (current[j + 1] + current[abs(j - 1)]) + twice * current[j] - before[j]
            for j in range(KMOM - 1 - k)
        ]
        before, current = current, following
        out.append(current[0])
    return out


def cuts(total, sizes):
    edges = [0]
    for size in sizes:
        edges.append(edges[-1] + size)
    return [(i, j - i) for i, j in zip(edges, edges[1:])]


def chunk_sizes(depth):
    units = depth // UNIT
    middle, odd = divmod(units - 2, 2)
    return [UNIT] + [2 * UNIT] * middle + [UNIT] * odd + [UNIT]


def groups_of(count, parts):
    edges = [count * i // parts for i in range(parts + 1)]
    return list(zip(edges, edges[1:]))


def kernel(
    devices, replicas, chunks, token_parts, weight_parts,
    tok, rt, wg, wu, out,
    T, RT, SEL, Y, X, W, AG, AU, H, HIN, CS, CN, SK, LV,
    rt_sem, tok_sem, w_sem,
    x_send, x_recv, f_send, f_recv,
    n_send, n_recv, s_send, s_recv, h_send, h_recv, l_send, l_recv, ready, go,
):
    groups = devices // HSPLIT
    half = devices // 2 * CAP
    width = W.shape[2]
    tiles = width // LANES
    rows = devices * CAP
    me = lax.axis_index("expert")
    z = lax.axis_index("replica")
    c = me % 2
    p = (me // 2) % 2
    a = me // HSPLIT
    partner = me + 1 - 2 * c
    last = len(chunks) - 1

    def pos(j):
        return (j % 2) * (devices // 2) + j // 2

    def other(dg, dp, dc):
        return HSPLIT * ((a + dg) % groups) + 2 * ((p + dp) % 2) + (c + dc) % 2

    combos = [(dg, dp) for dg in range(groups) for dp in range(2) if (dg, dp) != (0, 0)]
    combos = combos[::-1]
    alls = [
        (dg, dp, dc)
        for dg in range(groups) for dp in range(2) for dc in range(2)
        if (dg, dp, dc) != (0, 0, 0)
    ][::-1]
    peers = [(z + dz) % replicas for dz in range(1, replicas)]

    def block(j):
        return pl.ds(pl.multiple_of(pos(j) * CAP, CAP), CAP)

    def columns(ch):
        return pl.ds(chunks[ch][0], chunks[ch][1])

    def span(first, end):
        return pl.ds(chunks[first][0], chunks[end - 1][0] + chunks[end - 1][1] - chunks[first][0])

    def remote(src, dst, send_sem, recv_sem, device):
        return pltpu.make_async_remote_copy(
            src_ref=src, dst_ref=dst, send_sem=send_sem, recv_sem=recv_sem,
            device_id=device, device_id_type=MESH)

    def settle(ref, sem):
        pltpu.make_async_copy(ref, ref, sem).wait()

    def load_tokens(i):
        part = span(*token_parts[i])
        return pltpu.make_async_copy(tok.at[:, part], T.at[:, part], tok_sem.at[i])

    def load_weights(i):
        part = span(*weight_parts[i])
        return [
            pltpu.make_async_copy(w.at[part], W.at[k, part], w_sem.at[i])
            for k, w in enumerate((wg, wu))
        ]

    load_routes = pltpu.make_async_copy(rt, RT, rt_sem)
    load_routes.start()
    load_tokens(0).start()

    barrier = pltpu.get_barrier_semaphore()
    for combo in alls:
        pl.semaphore_signal(barrier, inc=1, device_id=(other(*combo), z), device_id_type=MESH)

    @pl.when(me == 0)
    def _():
        for peer in peers:
            pl.semaphore_signal(barrier, inc=1, device_id=(me, peer), device_id_type=MESH)

    for i in range(1, len(token_parts)):
        load_tokens(i).start()

    with jax.named_scope('p0_routes'):
        load_routes.wait()
    routes = RT[...]
    count = routes.shape[1]
    t_from = lax.broadcasted_iota(jnp.int32, (count, count), 0)
    t_to = lax.broadcasted_iota(jnp.int32, (count, count), 1)
    earlier = jnp.where(t_from < t_to, 1.0, 0.0).astype(jnp.bfloat16)
    named = [
        jnp.sum(jnp.where(routes == (a + dg) % groups, 1.0, 0.0), axis=0, keepdims=True)
        for dg in range(groups)
    ]
    table = jnp.concatenate(
        [jnp.broadcast_to(n, (CAP, count)) for n in named], axis=0)
    before = jnp.dot(table.astype(jnp.bfloat16), earlier, preferred_element_type=jnp.float32)
    slot = (lax.broadcasted_iota(jnp.int32, (groups * CAP, count), 0) % CAP).astype(jnp.float32)
    picks = jnp.where(before == slot, table, 0.0)
    SEL[...] = picks.astype(jnp.bfloat16)

    def gather(ch):
        part = columns(ch)
        picked = jnp.dot(
            SEL[...], T[:, part], preferred_element_type=jnp.float32).astype(jnp.bfloat16)
        Y[:, part] = picked
        X[block(me), part] = picked[:CAP]

    def send_rows(ch):
        part = columns(ch)
        for dg, dp in combos:
            remote(
                Y.at[pl.ds(dg * CAP, CAP), part], X.at[block(me), part],
                x_send, x_recv.at[ch], (other(dg, dp, 0), z)).start()

    with jax.named_scope('p1_tok0'):
        load_tokens(0).wait()
    gather(0)
    for i in range(len(weight_parts)):
        for copy in load_weights(i):
            copy.start()
    with jax.named_scope('p2_bar'):
        pl.semaphore_wait(barrier, len(alls) + jnp.where(me == 0, len(peers), 0))
    send_rows(0)

    with jax.named_scope('p3_sending'):
        for i, (first, end) in enumerate(token_parts):
            if i:
                load_tokens(i).wait()
            for ch in range(max(first, 1), end):
                gather(ch)
                send_rows(ch)

    @pl.when(me == 0)
    def _():
        for peer in peers:
            pl.semaphore_signal(ready, inc=1, device_id=(me, peer), device_id_type=MESH)

    with jax.named_scope('p4_count'):
        filled = jnp.sum(picks, axis=1, keepdims=True)
        for dg in range(groups):
            total = jnp.sum(filled[dg * CAP:(dg + 1) * CAP], axis=0, keepdims=True)
            CS[dg] = jnp.broadcast_to(total, (8, LANES))
        CN[me] = CS[0]
        for dg, dp, dc in alls:
            remote(CS.at[dg], CN.at[me], n_send, n_recv, (other(dg, dp, dc), z)).start()

    own = pl.ds(pl.multiple_of(c * half, half), half)

    def collect(ch):
        part = columns(ch)
        settle(X.at[pl.ds(0, len(combos) * CAP), part], x_recv.at[ch])
        remote(
            X.at[own, part], X.at[own, part], f_send, f_recv.at[ch], (partner, z)).start()

    def multiply(ch):
        part = columns(ch)
        settle(X.at[pl.ds(0, half), part], f_recv.at[ch])
        for i, (first, end) in enumerate(weight_parts):
            if first == ch:
                settle(W.at[:, span(first, end)], w_sem.at[i])
        x = X[:, part]
        for k, A in enumerate((AG, AU)):
            product = jnp.dot(x, W[k, part, :], preferred_element_type=jnp.float32)
            A[...] = A[...] + product if ch else product

    def share_count():
        @pl.when(me == 0)
        def _():
            pl.semaphore_wait(ready, len(peers))
            for combo in alls:
                pl.semaphore_signal(go, inc=1, device_id=(other(*combo), z), device_id_type=MESH)

        settle(CN.at[pl.ds(0, len(alls))], n_recv)
        total = functools.reduce(jnp.add, [CN[j] for j in range(devices)])
        SK[counts(z), :] = total

        @pl.when(me != 0)
        def _():
            pl.semaphore_wait(go, 1)

        for peer in peers:
            remote(SK.at[counts(z), :], SK.at[counts(z), :], s_send, s_recv, (me, peer)).start()

    def counts(r):
        start = replicas * SKETCH * tiles + r * 8
        return pl.ds(pl.multiple_of(start, 8), 8)

    with jax.named_scope('p5_c0'):
        collect(0)
    for ch in range(1, last + 1):
        with jax.named_scope('p7_c'):
            collect(ch)
        with jax.named_scope('p8_m'):
            multiply(ch - 1)
        if ch == last // 2 + 1:
            with jax.named_scope('p9_cnt'):
                share_count()
    with jax.named_scope('p9_mlast'):
        multiply(last)

    def activate(i, top):
        part = pl.ds(pl.multiple_of(i * ROWS, ROWS), ROWS)
        g = AG[part, :]
        h = g / (1.0 + jnp.exp(-g)) * AU[part, :]
        H[part, :] = h
        return jnp.maximum(top, jnp.max(jnp.abs(h).reshape(ROWS // 8, 8, width), axis=0))

    with jax.named_scope('q0_act'):
        top = lax.fori_loop(0, rows // ROWS, activate, jnp.zeros((8, width), jnp.float32))
    for dg, dp, dc in alls:
        j = other(dg, dp, dc)
        remote(H.at[block(j), :], HIN.at[me], h_send, h_recv, (j, z)).start()
    ceiling = jnp.max(top, axis=0, keepdims=True) + EPSILON
    scale = 2.0 / ceiling
    portion = max(tiles // 2, 1)

    def sketches(first):
        start = (z * tiles + first) * SKETCH
        return pl.ds(pl.multiple_of(start, 8), portion * SKETCH)

    for l in range(tiles):
        lanes = slice(l * LANES, (l + 1) * LANES)
        scale_l = scale[:, lanes]

        def sketch(i, sums):
            part = pl.ds(pl.multiple_of(i * ROWS, ROWS), ROWS)
            scaled = jnp.abs(H[part, lanes]) * scale_l - 1.0
            double = 2.0 * scaled
            previous, current = jnp.ones_like(scaled), scaled
            new = []
            for k in range(KMOM - 1):
                new.append(sums[k] + jnp.sum(current.reshape(ROWS // 8, 8, LANES), axis=0))
                previous, current = current, double * current - previous
            return tuple(new)

        zero = jnp.zeros((8, LANES), jnp.float32)
        with jax.named_scope('q1_sk'):
            sums = lax.fori_loop(0, rows // ROWS, sketch, (zero,) * (KMOM - 1))
        base = (z * tiles + l) * SKETCH
        SK[pl.ds(base, 1), :] = ceiling[:, lanes]
        for k in range(1, KMOM):
            SK[pl.ds(base + k, 1), :] = jnp.sum(sums[k - 1], axis=0, keepdims=True)
        if (l + 1) % portion == 0:
            part = sketches(l + 1 - portion)
            for peer in peers[1:] + peers[:1]:
                remote(SK.at[part, :], SK.at[part, :], s_send, s_recv, (me, peer)).start()

    HIN[me] = H[block(me), :]
    with jax.named_scope('q3_skwait'):
        settle(SK.at[pl.ds(0, len(peers) * (SKETCH * tiles + 8)), :], s_recv)

    def across(k):
        return SK[pl.ds(k, replicas * tiles, stride=SKETCH), :]

    def added(value):
        return functools.reduce(
            jnp.add, [value[r * tiles:(r + 1) * tiles] for r in range(replicas)])

    with jax.named_scope('q4_inv'):
        local = across(0)
        common = functools.reduce(
            jnp.maximum, [local[r * tiles:(r + 1) * tiles] for r in range(replicas)])
        ratio = local / jnp.concatenate([common] * replicas, axis=0)
        moments = [jnp.full_like(local, float(rows))] + [across(k) for k in range(1, KMOM)]
        named_rows = functools.reduce(jnp.add, [SK[counts(r), :] for r in range(replicas)])[:tiles]
        empty = float(rows * replicas) - named_rows
        weight = 1.0 / named_rows
        sums = [added(value) for value in rebase(moments, ratio)]
        level = clip_fraction([
            (total + empty if k % 2 else total - empty) * weight
            for k, total in enumerate(sums, 1)
        ])
        LV[me] = jnp.concatenate([common * level, 1.0 / common], axis=0)
    for dg, dp, dc in alls:
        remote(LV.at[me], LV.at[me], l_send, l_recv, (other(dg, dp, dc), z)).start()

    with jax.named_scope('q6_drain'):
        settle(X.at[pl.ds(0, len(combos) * CAP), :], x_send)
        settle(X.at[pl.ds(0, half), :], f_send)
        settle(CN.at[pl.ds(0, len(alls))], n_send)
        settle(SK.at[pl.ds(0, len(peers) * (SKETCH * tiles + 8)), :], s_send)
        settle(HIN.at[pl.ds(0, len(alls))], h_send)
        settle(HIN.at[pl.ds(0, len(alls))], h_recv)
    with jax.named_scope('q7_lvwait'):
        settle(LV.at[pl.ds(0, len(alls))], l_recv)

    def finish(i, _):
        for k in range(HSPLIT):
            e = i * HSPLIT + k
            for l in range(tiles):
                bound = LV[e, l:l + 1, :]
                factor = LV[e, tiles + l:tiles + l + 1, :]
                h = HIN[e, :, l * LANES:(l + 1) * LANES]
                h = jnp.minimum(jnp.maximum(h, -bound), bound) * factor
                lanes = pl.ds(pl.multiple_of(e * width + l * LANES, LANES), LANES)
                out[:, lanes] = h.astype(jnp.bfloat16)
        return 0

    with jax.named_scope('q8_fin'):
        lax.fori_loop(0, groups, finish, 0)
        settle(LV.at[pl.ds(0, len(alls))], l_send)


def shards(tokens, routes, gate_weight, up_weight):
    devices = lax.axis_size("expert")
    replicas = lax.axis_size("replica")
    groups = devices // HSPLIT
    count, depth = tokens.shape
    width = gate_weight.shape[1]
    chunks = cuts(depth, chunk_sizes(depth))
    token_parts = [(0, 1), (1, 3), (3, len(chunks))]
    weight_parts = groups_of(len(chunks), 4)
    rows = devices * CAP
    tiles = width // LANES
    bf16, f32 = jnp.bfloat16, jnp.float32
    dma = pltpu.SemaphoreType.DMA
    anywhere = pl.BlockSpec(memory_space=pl.ANY)
    return pl.pallas_call(
        functools.partial(kernel, devices, replicas, chunks, token_parts, weight_parts),
        out_shape=pltpu.VMEM((CAP, devices * width), bf16),
        in_specs=[anywhere] * 4,
        out_specs=pl.BlockSpec(memory_space=pltpu.VMEM),
        scratch_shapes=[
            pltpu.VMEM((count, depth), bf16),
            pltpu.VMEM((routes.shape[1], count), jnp.int32),
            pltpu.VMEM((groups * CAP, count), bf16),
            pltpu.VMEM((groups * CAP, depth), bf16),
            pltpu.VMEM((rows, depth), bf16),
            pltpu.VMEM((2, depth, width), bf16),
            pltpu.VMEM((rows, width), f32),
            pltpu.VMEM((rows, width), f32),
            pltpu.VMEM((rows, width), f32),
            pltpu.VMEM((devices, CAP, width), f32),
            pltpu.VMEM((groups, 8, LANES), f32),
            pltpu.VMEM((devices, 8, LANES), f32),
            pltpu.VMEM((replicas * (SKETCH * tiles + 8), LANES), f32),
            pltpu.VMEM((devices, 2 * tiles, LANES), f32),
            dma(()), dma((len(token_parts),)), dma((len(weight_parts),)),
            dma(()), dma((len(chunks),)), dma(()), dma((len(chunks),)),
            dma(()), dma(()), dma(()), dma(()), dma(()), dma(()), dma(()), dma(()),
            pltpu.SemaphoreType.REGULAR, pltpu.SemaphoreType.REGULAR,
        ],
        compiler_params=pltpu.CompilerParams(
            collective_id=0, has_side_effects=True, vmem_limit_bytes=56 * 1024 * 1024),
    )(tokens, pltpu.with_memory_space_constraint(routes.T, pltpu.HBM), gate_weight, up_weight)


def solution(mesh):
    in_specs = (
        P(("expert", "replica"), None),
        P(("expert", "replica"), None),
        P(None, "expert"),
        P(None, "expert"),
    )
    out_specs = P(("expert", "replica"), None)
    return jax.shard_map(shards, mesh=mesh, in_specs=in_specs, out_specs=out_specs, check_vma=False)
```

```python
import functools
import math

import jax
import jax.numpy as jnp
from jax import lax
from jax.experimental import pallas as pl
from jax.experimental.pallas import tpu as pltpu
from jax.sharding import PartitionSpec as P

HSPLIT = 4
CAP = 16
KMOM = 12
QITERS = 4
LANES = 128
UNIT = 512
DIRECT = 512
ROWS = 32
BATCH = 64
SKETCH = 12
STEPS = 32767.0

QUANTILE_LEVEL = 0.99
EPSILON = 1e-06
MESH = pl.DeviceIdType.MESH

PI_HIGH = 3.140625
PI_LOW = math.pi - PI_HIGH
SIN_TERMS = [(-1.0) ** i / math.factorial(2 * i + 1) for i in range(7)]
COS_TERMS = [(-1.0) ** i / math.factorial(2 * i) for i in range(8)]


def horner(square, terms):
    total = jnp.full_like(square, terms[-1])
    for term in terms[-2::-1]:
        total = total * square + term
    return total


def sin_cos(angle):
    turns = jnp.floor(angle * (1.0 / math.pi) + 0.5)
    rest = (angle - turns * PI_HIGH) - turns * PI_LOW
    sign = 1.0 - 2.0 * (turns - 2.0 * jnp.floor(turns * 0.5))
    square = rest * rest
    return sign * rest * horner(square, SIN_TERMS), sign * horner(square, COS_TERMS)


def tree(terms):
    while len(terms) > 1:
        terms = [functools.reduce(jnp.add, terms[i:i + 2]) for i in range(0, len(terms), 2)]
    return terms[0]


def clip_fraction(coefficient):
    start = (1.0 - QUANTILE_LEVEL) * math.pi
    total = jnp.zeros_like(coefficient[0])
    for k in range(1, KMOM, 2):
        total = total + coefficient[k - 1] * ((1.0 if k % 4 == 1 else -1.0) / k)
    angle = start - 2.0 * total
    for _ in range(QITERS - 1):
        sine, cosine = sin_cos(angle)
        double = 2.0 * cosine
        stride = double * double - 2.0
        waves = [-sine, jnp.zeros_like(sine), sine, double * sine]
        for k in range(3, KMOM):
            waves.append(stride * waves[k - 1] - waves[k - 3])
        angle = start - 2.0 * tree([
            coefficient[k - 1] * (waves[k + 1] * (1.0 / k)) for k in range(1, KMOM)])
    return 0.5 * (1.0 + sin_cos(angle)[1])


def rebase(moments, ratio):
    shift = ratio - 1.0
    before = moments
    current = [
        0.5 * ratio * (before[j + 1] + before[abs(j - 1)]) + shift * before[j]
        for j in range(KMOM - 1)
    ]
    out = [current[0]]
    twice = 2.0 * shift
    for k in range(1, KMOM - 1):
        following = [
            ratio * (current[j + 1] + current[abs(j - 1)]) + twice * current[j] - before[j]
            for j in range(KMOM - 1 - k)
        ]
        before, current = current, following
        out.append(current[0])
    return out


def cuts(total, sizes):
    edges = [0]
    for size in sizes:
        edges.append(edges[-1] + size)
    return [(i, j - i) for i, j in zip(edges, edges[1:])]


def chunk_sizes(depth):
    units = depth // UNIT - DIRECT // UNIT
    middle, odd = divmod(units - 2, 2)
    return [UNIT] + [2 * UNIT] * middle + [UNIT] * odd + [UNIT, DIRECT]


def groups_of(count, parts):
    edges = [count * i // parts for i in range(parts + 1)]
    return list(zip(edges, edges[1:]))


def kernel(
    devices, replicas, chunks, token_parts, weight_parts,
    tok, rt, wg, wu, out,
    T, RT, SEL, Y, X, W, AG, AU, H, HIN, CS, CN, SK, Q, F, Z, LV,
    rt_sem, tok_sem, w_sem,
    x_send, d_send, x_recv, f_send, f_recv,
    n_send, n_recv, q_send, q_recv, z_send, z_recv, h_send, h_recv, l_send, l_recv, ready, go,
):
    groups = devices // HSPLIT
    half = devices // 2 * CAP
    width = W.shape[2]
    tiles = width // LANES
    rows = devices * CAP
    me = lax.axis_index("expert")
    z = lax.axis_index("replica")
    c = me % 2
    p = (me // 2) % 2
    a = me // HSPLIT
    partner = me + 1 - 2 * c
    last = len(chunks) - 1

    def pos(j):
        return (j % 2) * (devices // 2) + j // 2

    def other(dg, dp, dc):
        return HSPLIT * ((a + dg) % groups) + 2 * ((p + dp) % 2) + (c + dc) % 2

    combos = [(dg, dp) for dg in range(groups) for dp in range(2) if (dg, dp) != (0, 0)]
    combos = combos[::-1]
    alls = [
        (dg, dp, dc)
        for dg in range(groups) for dp in range(2) for dc in range(2)
        if (dg, dp, dc) != (0, 0, 0)
    ][::-1]
    peers = [(z + dz) % replicas for dz in range(1, replicas)]

    def block(j):
        return pl.ds(pl.multiple_of(pos(j) * CAP, CAP), CAP)

    def columns(ch):
        return pl.ds(chunks[ch][0], chunks[ch][1])

    def span(first, end):
        return pl.ds(chunks[first][0], chunks[end - 1][0] + chunks[end - 1][1] - chunks[first][0])

    def remote(src, dst, send_sem, recv_sem, device):
        return pltpu.make_async_remote_copy(
            src_ref=src, dst_ref=dst, send_sem=send_sem, recv_sem=recv_sem,
            device_id=device, device_id_type=MESH)

    def settle(ref, sem):
        pltpu.make_async_copy(ref, ref, sem).wait()

    def load_tokens(i):
        part = span(*token_parts[i])
        return pltpu.make_async_copy(tok.at[:, part], T.at[:, part], tok_sem.at[i])

    def load_weights(i):
        part = span(*weight_parts[i])
        return [
            pltpu.make_async_copy(w.at[part], W.at[k, part], w_sem.at[i])
            for k, w in enumerate((wg, wu))
        ]

    load_routes = pltpu.make_async_copy(rt, RT, rt_sem)
    load_routes.start()
    load_tokens(0).start()

    barrier = pltpu.get_barrier_semaphore()
    for combo in alls:
        pl.semaphore_signal(barrier, inc=1, device_id=(other(*combo), z), device_id_type=MESH)

    @pl.when(me == 0)
    def _():
        for peer in peers:
            pl.semaphore_signal(barrier, inc=1, device_id=(me, peer), device_id_type=MESH)

    for i in range(1, len(token_parts)):
        load_tokens(i).start()

    load_routes.wait()
    routes = RT[...]
    count = routes.shape[1]
    t_from = lax.broadcasted_iota(jnp.int32, (count, count), 0)
    t_to = lax.broadcasted_iota(jnp.int32, (count, count), 1)
    earlier = jnp.where(t_from < t_to, 1.0, 0.0).astype(jnp.bfloat16)
    named = [
        jnp.sum(jnp.where(routes == (a + dg) % groups, 1.0, 0.0), axis=0, keepdims=True)
        for dg in range(groups)
    ]
    table = jnp.concatenate(
        [jnp.broadcast_to(n, (CAP, count)) for n in named], axis=0)
    before = jnp.dot(table.astype(jnp.bfloat16), earlier, preferred_element_type=jnp.float32)
    slot = (lax.broadcasted_iota(jnp.int32, (groups * CAP, count), 0) % CAP).astype(jnp.float32)
    picks = jnp.where(before == slot, table, 0.0)
    SEL[...] = picks.astype(jnp.bfloat16)

    def gather(ch):
        part = columns(ch)
        picked = jnp.dot(
            SEL[...], T[:, part], preferred_element_type=jnp.float32).astype(jnp.bfloat16)
        Y[:, part] = picked
        X[block(me), part] = picked[:CAP]

    def send_rows(ch):
        part = columns(ch)
        if ch == last:
            for dg, dp, dc in alls:
                remote(
                    Y.at[pl.ds(dg * CAP, CAP), part], X.at[block(me), part],
                    d_send, x_recv.at[ch], (other(dg, dp, dc), z)).start()
            return
        for dg, dp in combos:
            remote(
                Y.at[pl.ds(dg * CAP, CAP), part], X.at[block(me), part],
                x_send, x_recv.at[ch], (other(dg, dp, 0), z)).start()

    load_tokens(0).wait()
    gather(0)
    for i in range(len(weight_parts)):
        for copy in load_weights(i):
            copy.start()
    pl.semaphore_wait(barrier, len(alls) + jnp.where(me == 0, len(peers), 0))
    send_rows(0)

    filled = jnp.sum(picks, axis=1, keepdims=True)
    for dg in range(groups):
        total = jnp.sum(filled[dg * CAP:(dg + 1) * CAP], axis=0, keepdims=True)
        CS[dg] = jnp.broadcast_to(total, (8, LANES))
    CN[me] = CS[0]
    for dg, dp, dc in alls:
        remote(CS.at[dg], CN.at[me], n_send, n_recv, (other(dg, dp, dc), z)).start()

    for i, (first, end) in enumerate(token_parts):
        if i:
            load_tokens(i).wait()
        for ch in range(max(first, 1), end):
            gather(ch)
            send_rows(ch)

    @pl.when(me == 0)
    def _():
        for peer in peers:
            pl.semaphore_signal(ready, inc=1, device_id=(me, peer), device_id_type=MESH)

    own = pl.ds(pl.multiple_of(c * half, half), half)

    def collect(ch):
        part = columns(ch)
        settle(X.at[pl.ds(0, len(combos) * CAP), part], x_recv.at[ch])
        remote(
            X.at[own, part], X.at[own, part], f_send, f_recv.at[ch], (partner, z)).start()

    def multiply(ch):
        part = columns(ch)
        if ch < last:
            settle(X.at[pl.ds(0, half), part], f_recv.at[ch])
        else:
            settle(X.at[pl.ds(0, len(alls) * CAP), part], x_recv.at[ch])
        for i, (first, end) in enumerate(weight_parts):
            if first == ch:
                settle(W.at[:, span(first, end)], w_sem.at[i])
        x = X[:, part]
        for k, A in enumerate((AG, AU)):
            product = jnp.dot(x, W[k, part, :], preferred_element_type=jnp.float32)
            A[...] = A[...] + product if ch else product

    def release():
        @pl.when(me == 0)
        def _():
            pl.semaphore_wait(ready, len(peers))
            for combo in alls:
                pl.semaphore_signal(go, inc=1, device_id=(other(*combo), z), device_id_type=MESH)

    def share_count():
        settle(CN.at[pl.ds(0, len(alls))], n_recv)
        total = functools.reduce(jnp.add, [CN[j] for j in range(devices)])
        Z[z, 0] = total

        @pl.when(me != 0)
        def _():
            pl.semaphore_wait(go, 1)

        for peer in peers:
            remote(Z.at[z, 0], Z.at[z, 0], z_send, z_recv, (me, peer)).start()

    collect(0)
    for ch in range(1, last + 1):
        if ch < last:
            collect(ch)
        multiply(ch - 1)
        if ch == last // 2 - 1:
            release()
        if ch == last:
            share_count()
    multiply(last)

    def activate(i, top):
        part = pl.ds(pl.multiple_of(i * ROWS, ROWS), ROWS)
        g = AG[part, :]
        h = g / (1.0 + jnp.exp(-g)) * AU[part, :]
        H[part, :] = h
        return jnp.maximum(top, jnp.max(jnp.abs(h).reshape(ROWS // 8, 8, width), axis=0))

    top = lax.fori_loop(0, rows // ROWS, activate, jnp.zeros((8, width), jnp.float32))
    ceiling = jnp.max(top, axis=0, keepdims=True) + EPSILON
    for l in range(tiles):
        Z[z, 1, l:l + 1, :] = ceiling[:, l * LANES:(l + 1) * LANES]
    for peer in peers:
        remote(Z.at[z, 1], Z.at[z, 1], z_send, z_recv, (me, peer)).start()
    for dg, dp, dc in alls:
        j = other(dg, dp, dc)
        remote(H.at[block(j), :], HIN.at[me], h_send, h_recv, (j, z)).start()
    scale = 2.0 / ceiling
    here = Z[z, 0, 0:1, :]
    empty = float(rows) - here
    stretch = STEPS / jnp.maximum(here, 1.0)
    even = lax.broadcasted_iota(jnp.int32, (SKETCH * tiles, LANES), 0) % 2 == 0
    bounds = [SKETCH * tiles * 2 // 3 // 16 * 16, SKETCH * tiles]
    sent = 0

    for l in range(tiles):
        lanes = slice(l * LANES, (l + 1) * LANES)
        scale_l = scale[:, lanes]

        def sketch(i, sums):
            part = pl.ds(pl.multiple_of(i * BATCH, BATCH), BATCH)
            scaled = jnp.abs(H[part, lanes]) * scale_l - 1.0
            double = 2.0 * scaled
            previous, current = jnp.ones_like(scaled), scaled
            new = []
            for k in range(KMOM - 1):
                new.append(sums[k] + jnp.sum(current.reshape(BATCH // 8, 8, LANES), axis=0))
                previous, current = current, double * current - previous
            return tuple(new)

        zero = jnp.zeros((8, LANES), jnp.float32)
        sums = lax.fori_loop(0, rows // BATCH, sketch, (zero,) * (KMOM - 1), unroll=True)
        SK[l * SKETCH:l * SKETCH + 1, :] = jnp.zeros((1, LANES), jnp.float32)
        for k in range(1, KMOM):
            SK[l * SKETCH + k:l * SKETCH + k + 1, :] = jnp.sum(
                sums[k - 1], axis=0, keepdims=True)
        while bounds and bounds[0] <= (l + 1) * SKETCH:
            part = slice(sent, bounds[0])
            held = SK[part, :] + jnp.where(even[part], -empty, empty)
            code = jnp.minimum(jnp.maximum(held * stretch, -STEPS), STEPS)
            Q[z, part, :] = jnp.floor(code + 0.5).astype(jnp.int32).astype(jnp.int16)
            for peer in peers[1:] + peers[:1]:
                remote(Q.at[z, part, :], Q.at[z, part, :], q_send, q_recv, (me, peer)).start()
            sent = bounds.pop(0)

    HIN[me] = H[block(me), :]
    settle(Z.at[pl.ds(0, len(peers))], z_recv)

    def stacked(kind):
        return [Z[r, kind, 0:tiles, :] for r in range(replicas)]

    def added(value):
        return functools.reduce(
            jnp.add, [value[r * tiles:(r + 1) * tiles] for r in range(replicas)])

    local = stacked(1)
    common = functools.reduce(jnp.maximum, local)
    ratio = jnp.concatenate([value / common for value in local], axis=0)
    here = stacked(0)
    total = functools.reduce(jnp.add, here)
    share = jnp.concatenate([value / total for value in here], axis=0)
    settle(Q.at[pl.ds(0, len(peers))], q_recv)
    for r in range(replicas):
        F[r * SKETCH * tiles:(r + 1) * SKETCH * tiles, :] = (
            Q[r].astype(jnp.int32).astype(jnp.float32) * (1.0 / STEPS))
    moments = [jnp.ones_like(ratio)]
    moments += [F[pl.ds(k, replicas * tiles, stride=SKETCH), :] for k in range(1, KMOM)]
    level = clip_fraction([added(value * share) for value in rebase(moments, ratio)])
    LV[me] = jnp.concatenate([common * level, 1.0 / common], axis=0)
    for dg, dp, dc in alls:
        remote(LV.at[me], LV.at[me], l_send, l_recv, (other(dg, dp, dc), z)).start()

    settle(X.at[pl.ds(0, len(combos) * CAP), span(0, last)], x_send)
    settle(X.at[pl.ds(0, len(alls) * CAP), columns(last)], d_send)
    settle(X.at[pl.ds(0, half), span(0, last)], f_send)
    settle(CN.at[pl.ds(0, len(alls))], n_send)
    settle(Q.at[pl.ds(0, len(peers))], q_send)
    settle(Z.at[pl.ds(0, len(peers))], z_send)
    settle(HIN.at[pl.ds(0, len(alls))], h_send)
    settle(HIN.at[pl.ds(0, len(alls))], h_recv)
    settle(LV.at[pl.ds(0, len(alls))], l_recv)

    def finish(i, _):
        for k in range(HSPLIT):
            e = i * HSPLIT + k
            for l in range(tiles):
                bound = LV[e, l:l + 1, :]
                factor = LV[e, tiles + l:tiles + l + 1, :]
                h = HIN[e, :, l * LANES:(l + 1) * LANES]
                h = jnp.minimum(jnp.maximum(h, -bound), bound) * factor
                lanes = pl.ds(pl.multiple_of(e * width + l * LANES, LANES), LANES)
                out[:, lanes] = h.astype(jnp.bfloat16)
        return 0

    lax.fori_loop(0, groups, finish, 0)
    settle(LV.at[pl.ds(0, len(alls))], l_send)


def shards(tokens, routes, gate_weight, up_weight):
    devices = lax.axis_size("expert")
    replicas = lax.axis_size("replica")
    groups = devices // HSPLIT
    count, depth = tokens.shape
    width = gate_weight.shape[1]
    chunks = cuts(depth, chunk_sizes(depth))
    token_parts = [(0, 1), (1, 3), (3, len(chunks))]
    weight_parts = groups_of(len(chunks), 4)
    rows = devices * CAP
    tiles = width // LANES
    bf16, f32 = jnp.bfloat16, jnp.float32
    dma = pltpu.SemaphoreType.DMA
    anywhere = pl.BlockSpec(memory_space=pl.ANY)
    return pl.pallas_call(
        functools.partial(kernel, devices, replicas, chunks, token_parts, weight_parts),
        out_shape=pltpu.VMEM((CAP, devices * width), bf16),
        in_specs=[anywhere] * 4,
        out_specs=pl.BlockSpec(memory_space=pltpu.VMEM),
        scratch_shapes=[
            pltpu.VMEM((count, depth), bf16),
            pltpu.VMEM((routes.shape[1], count), jnp.int32),
            pltpu.VMEM((groups * CAP, count), bf16),
            pltpu.VMEM((groups * CAP, depth), bf16),
            pltpu.VMEM((rows, depth), bf16),
            pltpu.VMEM((2, depth, width), bf16),
            pltpu.VMEM((rows, width), f32),
            pltpu.VMEM((rows, width), f32),
            pltpu.VMEM((rows, width), f32),
            pltpu.VMEM((devices, CAP, width), f32),
            pltpu.VMEM((groups, 8, LANES), f32),
            pltpu.VMEM((devices, 8, LANES), f32),
            pltpu.VMEM((SKETCH * tiles, LANES), f32),
            pltpu.VMEM((replicas, SKETCH * tiles, LANES), jnp.int16),
            pltpu.VMEM((replicas * SKETCH * tiles, LANES), f32),
            pltpu.VMEM((replicas, 2, 8, LANES), f32),
            pltpu.VMEM((devices, 2 * tiles, LANES), f32),
            dma(()), dma((len(token_parts),)), dma((len(weight_parts),)),
            dma(()), dma(()), dma((len(chunks),)), dma(()), dma((len(chunks) - 1,)),
            dma(()), dma(()), dma(()), dma(()), dma(()), dma(()), dma(()), dma(()), dma(()), dma(()),
            pltpu.SemaphoreType.REGULAR, pltpu.SemaphoreType.REGULAR,
        ],
        compiler_params=pltpu.CompilerParams(
            collective_id=0, has_side_effects=True, vmem_limit_bytes=56 * 1024 * 1024),
    )(tokens, pltpu.with_memory_space_constraint(routes.T, pltpu.HBM), gate_weight, up_weight)


def solution(mesh):
    in_specs = (
        P(("expert", "replica"), None),
        P(("expert", "replica"), None),
        P(None, "expert"),
        P(None, "expert"),
    )
    out_specs = P(("expert", "replica"), None)
    return jax.shard_map(shards, mesh=mesh, in_specs=in_specs, out_specs=out_specs, check_vma=False)
```

```python
import functools
import math

import jax
import jax.numpy as jnp
from jax import lax
from jax.experimental import pallas as pl
from jax.experimental.pallas import tpu as pltpu
from jax.sharding import PartitionSpec as P

HSPLIT = 4
CAP = 16
KMOM = 12
QITERS = 4
LANES = 128
UNIT = 512
DIRECT = 512
ROWS = 32
BATCH = 64
SKETCH = 12
STEPS = 32767.0

QUANTILE_LEVEL = 0.99
EPSILON = 1e-06
MESH = pl.DeviceIdType.MESH

SIN_TERMS = [(-1.0) ** i / math.factorial(2 * i + 1) for i in range(7)]
COS_TERMS = [(-1.0) ** i / math.factorial(2 * i) for i in range(8)]


def polynomial(x, terms):
    terms = [jnp.full_like(x, term) for term in terms]
    while len(terms) > 1:
        pairs = [terms[i] + terms[i + 1] * x for i in range(0, len(terms) - 1, 2)]
        terms = pairs + terms[2 * len(pairs):]
        x = x * x
    return terms[0]


def sin_cos(half_turns):
    turns = jnp.floor(half_turns + 0.5)
    rest = (half_turns - turns) * math.pi
    sign = 1.0 - 2.0 * (turns - 2.0 * jnp.floor(turns * 0.5))
    square = rest * rest
    return sign * rest * polynomial(square, SIN_TERMS), sign * polynomial(square, COS_TERMS)


def tree(terms):
    while len(terms) > 1:
        terms = [functools.reduce(jnp.add, terms[i:i + 2]) for i in range(0, len(terms), 2)]
    return terms[0]


def clip_fraction(coefficient):
    start = 1.0 - QUANTILE_LEVEL
    total = jnp.zeros_like(coefficient[0])
    for k in range(1, KMOM, 2):
        total = total + coefficient[k - 1] * ((1.0 if k % 4 == 1 else -1.0) / k)
    angle = start - (2.0 / math.pi) * total
    for _ in range(QITERS - 1):
        sine, cosine = sin_cos(angle)
        double = 2.0 * cosine
        stride = double * double - 2.0
        waves = [-sine, jnp.zeros_like(sine), sine, double * sine]
        for k in range(3, KMOM):
            waves.append(stride * waves[k - 1] - waves[k - 3])
        angle = start - (2.0 / math.pi) * tree([
            coefficient[k - 1] * (waves[k + 1] * (1.0 / k)) for k in range(1, KMOM)])
    return 0.5 * (1.0 + sin_cos(angle)[1])


def rebase(moments, ratio):
    shift = ratio - 1.0
    before = moments
    current = [
        0.5 * ratio * (before[j + 1] + before[abs(j - 1)]) + shift * before[j]
        for j in range(KMOM - 1)
    ]
    out = [current[0]]
    twice = 2.0 * shift
    for k in range(1, KMOM - 1):
        following = [
            ratio * (current[j + 1] + current[abs(j - 1)]) + twice * current[j] - before[j]
            for j in range(KMOM - 1 - k)
        ]
        before, current = current, following
        out.append(current[0])
    return out


def cuts(total, sizes):
    edges = [0]
    for size in sizes:
        edges.append(edges[-1] + size)
    return [(i, j - i) for i, j in zip(edges, edges[1:])]


def chunk_sizes(depth):
    units = depth // UNIT - DIRECT // UNIT
    middle, odd = divmod(units - 2, 2)
    return [UNIT] + [2 * UNIT] * middle + [UNIT] * odd + [UNIT, DIRECT]


def groups_of(count, parts):
    edges = [count * i // parts for i in range(parts + 1)]
    return list(zip(edges, edges[1:]))


def kernel(
    devices, replicas, chunks, token_parts, weight_parts,
    tok, rt, wg, wu, out,
    T, RT, SEL, Y, X, W, AG, AU, H, HIN, CS, CN, SK, Q, F, Z, LV,
    rt_sem, tok_sem, w_sem,
    x_send, d_send, x_recv, f_send, f_recv,
    n_send, n_recv, q_send, q_recv, z_send, z_recv, h_send, h_recv, l_send, l_recv, ready, go,
):
    groups = devices // HSPLIT
    half = devices // 2 * CAP
    width = W.shape[2]
    tiles = width // LANES
    rows = devices * CAP
    me = lax.axis_index("expert")
    z = lax.axis_index("replica")
    c = me % 2
    p = (me // 2) % 2
    a = me // HSPLIT
    partner = me + 1 - 2 * c
    last = len(chunks) - 1

    def pos(j):
        return (j % 2) * (devices // 2) + j // 2

    def other(dg, dp, dc):
        return HSPLIT * ((a + dg) % groups) + 2 * ((p + dp) % 2) + (c + dc) % 2

    combos = [(dg, dp) for dg in range(groups) for dp in range(2) if (dg, dp) != (0, 0)]
    combos = combos[::-1]
    alls = [
        (dg, dp, dc)
        for dg in range(groups) for dp in range(2) for dc in range(2)
        if (dg, dp, dc) != (0, 0, 0)
    ][::-1]
    peers = []
    for i in range(replicas - 1):
        up, down = i + (i >= z), replicas - 1 - i - (replicas - 1 - i <= z)
        peers.append(jnp.where(z < replicas // 2, down, up))

    def block(j):
        return pl.ds(pl.multiple_of(pos(j) * CAP, CAP), CAP)

    def columns(ch):
        return pl.ds(chunks[ch][0], chunks[ch][1])

    def span(first, end):
        return pl.ds(chunks[first][0], chunks[end - 1][0] + chunks[end - 1][1] - chunks[first][0])

    def remote(src, dst, send_sem, recv_sem, device):
        return pltpu.make_async_remote_copy(
            src_ref=src, dst_ref=dst, send_sem=send_sem, recv_sem=recv_sem,
            device_id=device, device_id_type=MESH)

    def settle(ref, sem):
        pltpu.make_async_copy(ref, ref, sem).wait()

    def load_tokens(i):
        part = span(*token_parts[i])
        return pltpu.make_async_copy(tok.at[:, part], T.at[:, part], tok_sem.at[i])

    def load_weights(i):
        part = span(*weight_parts[i])
        return [
            pltpu.make_async_copy(w.at[part], W.at[k, part], w_sem.at[i])
            for k, w in enumerate((wg, wu))
        ]

    load_routes = pltpu.make_async_copy(rt, RT, rt_sem)
    load_routes.start()
    load_tokens(0).start()

    barrier = pltpu.get_barrier_semaphore()
    for combo in alls:
        pl.semaphore_signal(barrier, inc=1, device_id=(other(*combo), z), device_id_type=MESH)

    @pl.when(me == 0)
    def _():
        for peer in peers:
            pl.semaphore_signal(barrier, inc=1, device_id=(me, peer), device_id_type=MESH)

    for i in range(1, len(token_parts)):
        load_tokens(i).start()

    load_routes.wait()
    routes = RT[...]
    count = routes.shape[1]
    t_from = lax.broadcasted_iota(jnp.int32, (count, count), 0)
    t_to = lax.broadcasted_iota(jnp.int32, (count, count), 1)
    earlier = jnp.where(t_from < t_to, 1.0, 0.0).astype(jnp.bfloat16)
    named = [
        jnp.sum(jnp.where(routes == (a + dg) % groups, 1.0, 0.0), axis=0, keepdims=True)
        for dg in range(groups)
    ]
    table = jnp.concatenate(
        [jnp.broadcast_to(n, (CAP, count)) for n in named], axis=0)
    before = jnp.dot(table.astype(jnp.bfloat16), earlier, preferred_element_type=jnp.float32)
    slot = (lax.broadcasted_iota(jnp.int32, (groups * CAP, count), 0) % CAP).astype(jnp.float32)
    picks = jnp.where(before == slot, table, 0.0)
    SEL[...] = picks.astype(jnp.bfloat16)

    def gather(ch):
        part = columns(ch)
        picked = jnp.dot(
            SEL[...], T[:, part], preferred_element_type=jnp.float32).astype(jnp.bfloat16)
        Y[:, part] = picked
        X[block(me), part] = picked[:CAP]

    def send_rows(ch):
        part = columns(ch)
        if ch == last:
            for dg, dp, dc in alls:
                remote(
                    Y.at[pl.ds(dg * CAP, CAP), part], X.at[block(me), part],
                    d_send, x_recv.at[ch], (other(dg, dp, dc), z)).start()
            return
        for dg, dp in combos:
            remote(
                Y.at[pl.ds(dg * CAP, CAP), part], X.at[block(me), part],
                x_send, x_recv.at[ch], (other(dg, dp, 0), z)).start()

    load_tokens(0).wait()
    gather(0)
    for i in range(len(weight_parts)):
        for copy in load_weights(i):
            copy.start()
    pl.semaphore_wait(barrier, len(alls) + jnp.where(me == 0, len(peers), 0))
    send_rows(0)

    filled = jnp.sum(picks, axis=1, keepdims=True)
    for dg in range(groups):
        total = jnp.sum(filled[dg * CAP:(dg + 1) * CAP], axis=0, keepdims=True)
        CS[dg] = jnp.broadcast_to(total, (8, LANES))
    CN[me] = CS[0]
    for dg, dp, dc in alls:
        remote(CS.at[dg], CN.at[me], n_send, n_recv, (other(dg, dp, dc), z)).start()

    for i, (first, end) in enumerate(token_parts):
        if i:
            load_tokens(i).wait()
        for ch in range(max(first, 1), end):
            gather(ch)
            send_rows(ch)

    @pl.when(me == 0)
    def _():
        for peer in peers:
            pl.semaphore_signal(ready, inc=1, device_id=(me, peer), device_id_type=MESH)

    own = pl.ds(pl.multiple_of(c * half, half), half)

    def collect(ch):
        part = columns(ch)
        settle(X.at[pl.ds(0, len(combos) * CAP), part], x_recv.at[ch])
        remote(
            X.at[own, part], X.at[own, part], f_send, f_recv.at[ch], (partner, z)).start()

    def arrive(ch):
        part = columns(ch)
        if ch < last:
            settle(X.at[pl.ds(0, half), part], f_recv.at[ch])
        else:
            settle(X.at[pl.ds(0, len(alls) * CAP), part], x_recv.at[ch])
        for i, (first, end) in enumerate(weight_parts):
            if first == ch:
                settle(W.at[:, span(first, end)], w_sem.at[i])

    def multiply(ch):
        arrive(ch)
        part = columns(ch)
        x = X[:, part]
        for k, A in enumerate((AG, AU)):
            product = jnp.dot(x, W[k, part, :], preferred_element_type=jnp.float32)
            A[...] = A[...] + product if ch else product

    def release():
        @pl.when(me == 0)
        def _():
            pl.semaphore_wait(ready, len(peers))
            for combo in alls:
                pl.semaphore_signal(go, inc=1, device_id=(other(*combo), z), device_id_type=MESH)

    def share_count():
        settle(CN.at[pl.ds(0, len(alls))], n_recv)
        total = functools.reduce(jnp.add, [CN[j] for j in range(devices)])
        Z[z, 0] = total

        @pl.when(me != 0)
        def _():
            pl.semaphore_wait(go, 1)

        for peer in peers:
            remote(Z.at[z, 0], Z.at[z, 0], z_send, z_recv, (me, peer)).start()

    collect(0)
    for ch in range(1, last):
        collect(ch)
        multiply(ch - 1)
        if ch == last // 2 - 1:
            release()
        if ch == last - 1:
            share_count()
    arrive(last - 1)
    arrive(last)
    part = span(last - 1, last + 1)
    x = X[:, part]
    strip = min(2 * LANES, width)
    tops = []
    for n in range(0, width, strip):
        lanes = slice(n, n + strip)
        g, u = (
            A[:, lanes] + jnp.dot(x, W[k, part, lanes], preferred_element_type=jnp.float32)
            for k, A in enumerate((AG, AU)))
        h = g / (1.0 + jnp.exp(-g)) * u
        H[:, lanes] = h
        tops.append(jnp.max(jnp.abs(h), axis=0, keepdims=True))

    ceiling = jnp.concatenate(tops, axis=1) + EPSILON
    for l in range(tiles):
        Z[z, 1, l:l + 1, :] = ceiling[:, l * LANES:(l + 1) * LANES]
    for peer in peers:
        remote(Z.at[z, 1], Z.at[z, 1], z_send, z_recv, (me, peer)).start()
    scale = 2.0 / ceiling
    here = Z[z, 0, 0:1, :]
    empty = float(rows) - here
    stretch = STEPS / jnp.maximum(here, 1.0)
    even = lax.broadcasted_iota(jnp.int32, (SKETCH * tiles, LANES), 0) % 2 == 0
    bounds = [SKETCH * tiles * 2 // 3 // 16 * 16, SKETCH * tiles]
    sent = 0

    def send_codes(ref, peer):
        remote(ref, ref, q_send, q_recv, (me, peer)).start()

    for l in range(tiles):
        lanes = slice(l * LANES, (l + 1) * LANES)
        scale_l = scale[:, lanes]

        def sketch(i, sums):
            part = pl.ds(pl.multiple_of(i * BATCH, BATCH), BATCH)
            scaled = jnp.abs(H[part, lanes]) * scale_l - 1.0
            double = 2.0 * scaled
            previous, current = jnp.ones_like(scaled), scaled
            new = []
            for k in range(KMOM - 1):
                new.append(sums[k] + jnp.sum(current.reshape(BATCH // 8, 8, LANES), axis=0))
                previous, current = current, double * current - previous
            return tuple(new)

        zero = jnp.zeros((8, LANES), jnp.float32)
        sums = lax.fori_loop(0, rows // BATCH, sketch, (zero,) * (KMOM - 1), unroll=True)
        SK[l * SKETCH:l * SKETCH + 1, :] = jnp.zeros((1, LANES), jnp.float32)
        for k in range(1, KMOM):
            SK[l * SKETCH + k:l * SKETCH + k + 1, :] = jnp.sum(
                sums[k - 1], axis=0, keepdims=True)
        while bounds and bounds[0] <= (l + 1) * SKETCH:
            part = slice(sent, bounds[0])
            held = SK[part, :] + jnp.where(even[part], -empty, empty)
            code = jnp.minimum(jnp.maximum(held * stretch, -STEPS), STEPS)
            Q[z, part, :] = jnp.floor(code + 0.5).astype(jnp.int32).astype(jnp.int16)
            send_codes(Q.at[z, part, :], peers[0])
            sent = bounds.pop(0)
    for peer in peers[1:]:
        send_codes(Q.at[z], peer)
    for dg, dp, dc in alls:
        j = other(dg, dp, dc)
        remote(H.at[block(j), :], HIN.at[me], h_send, h_recv, (j, z)).start()

    HIN[me] = H[block(me), :]
    settle(Z.at[pl.ds(0, len(peers))], z_recv)

    def stacked(kind):
        return [Z[r, kind, 0:tiles, :] for r in range(replicas)]

    def added(value):
        return functools.reduce(
            jnp.add, [value[r * tiles:(r + 1) * tiles] for r in range(replicas)])

    local = stacked(1)
    common = functools.reduce(jnp.maximum, local)
    ratio = jnp.concatenate([value / common for value in local], axis=0)
    here = stacked(0)
    total = functools.reduce(jnp.add, here)
    share = jnp.concatenate([value / total for value in here], axis=0)
    settle(Q.at[pl.ds(0, len(peers))], q_recv)
    for r in range(replicas):
        F[r * SKETCH * tiles:(r + 1) * SKETCH * tiles, :] = (
            Q[r].astype(jnp.int32).astype(jnp.float32) * (1.0 / STEPS))
    moments = [jnp.ones_like(ratio)]
    moments += [F[pl.ds(k, replicas * tiles, stride=SKETCH), :] for k in range(1, KMOM)]
    level = clip_fraction([added(value * share) for value in rebase(moments, ratio)])
    LV[me] = jnp.concatenate([common * level, 1.0 / common], axis=0)
    for dg, dp, dc in alls:
        remote(LV.at[me], LV.at[me], l_send, l_recv, (other(dg, dp, dc), z)).start()

    settle(X.at[pl.ds(0, len(combos) * CAP), span(0, last)], x_send)
    settle(X.at[pl.ds(0, len(alls) * CAP), columns(last)], d_send)
    settle(X.at[pl.ds(0, half), span(0, last)], f_send)
    settle(CN.at[pl.ds(0, len(alls))], n_send)
    settle(Q.at[pl.ds(0, len(peers))], q_send)
    settle(Z.at[pl.ds(0, len(peers))], z_send)
    settle(HIN.at[pl.ds(0, len(alls))], h_send)
    settle(HIN.at[pl.ds(0, len(alls))], h_recv)
    settle(LV.at[pl.ds(0, len(alls))], l_recv)

    def finish(i, _):
        for k in range(HSPLIT):
            e = i * HSPLIT + k
            for l in range(tiles):
                bound = LV[e, l:l + 1, :]
                factor = LV[e, tiles + l:tiles + l + 1, :]
                h = HIN[e, :, l * LANES:(l + 1) * LANES]
                h = jnp.minimum(jnp.maximum(h, -bound), bound) * factor
                lanes = pl.ds(pl.multiple_of(e * width + l * LANES, LANES), LANES)
                out[:, lanes] = h.astype(jnp.bfloat16)
        return 0

    lax.fori_loop(0, groups, finish, 0)
    settle(LV.at[pl.ds(0, len(alls))], l_send)


def shards(tokens, routes, gate_weight, up_weight):
    devices = lax.axis_size("expert")
    replicas = lax.axis_size("replica")
    groups = devices // HSPLIT
    count, depth = tokens.shape
    width = gate_weight.shape[1]
    chunks = cuts(depth, chunk_sizes(depth))
    token_parts = [(0, 1), (1, 3), (3, len(chunks))]
    weight_parts = groups_of(len(chunks), 4)
    rows = devices * CAP
    tiles = width // LANES
    bf16, f32 = jnp.bfloat16, jnp.float32
    dma = pltpu.SemaphoreType.DMA
    anywhere = pl.BlockSpec(memory_space=pl.ANY)
    return pl.pallas_call(
        functools.partial(kernel, devices, replicas, chunks, token_parts, weight_parts),
        out_shape=pltpu.VMEM((CAP, devices * width), bf16),
        in_specs=[anywhere] * 4,
        out_specs=pl.BlockSpec(memory_space=pltpu.VMEM),
        scratch_shapes=[
            pltpu.VMEM((count, depth), bf16),
            pltpu.VMEM((routes.shape[1], count), jnp.int32),
            pltpu.VMEM((groups * CAP, count), bf16),
            pltpu.VMEM((groups * CAP, depth), bf16),
            pltpu.VMEM((rows, depth), bf16),
            pltpu.VMEM((2, depth, width), bf16),
            pltpu.VMEM((rows, width), f32),
            pltpu.VMEM((rows, width), f32),
            pltpu.VMEM((rows, width), f32),
            pltpu.VMEM((devices, CAP, width), f32),
            pltpu.VMEM((groups, 8, LANES), f32),
            pltpu.VMEM((devices, 8, LANES), f32),
            pltpu.VMEM((SKETCH * tiles, LANES), f32),
            pltpu.VMEM((replicas, SKETCH * tiles, LANES), jnp.int16),
            pltpu.VMEM((replicas * SKETCH * tiles, LANES), f32),
            pltpu.VMEM((replicas, 2, 8, LANES), f32),
            pltpu.VMEM((devices, 2 * tiles, LANES), f32),
            dma(()), dma((len(token_parts),)), dma((len(weight_parts),)),
            dma(()), dma(()), dma((len(chunks),)), dma(()), dma((len(chunks) - 1,)),
            dma(()), dma(()), dma(()), dma(()), dma(()), dma(()), dma(()), dma(()), dma(()), dma(()),
            pltpu.SemaphoreType.REGULAR, pltpu.SemaphoreType.REGULAR,
        ],
        compiler_params=pltpu.CompilerParams(
            collective_id=0, has_side_effects=True, vmem_limit_bytes=56 * 1024 * 1024),
    )(tokens, pltpu.with_memory_space_constraint(routes.T, pltpu.HBM), gate_weight, up_weight)


def solution(mesh):
    in_specs = (
        P(("expert", "replica"), None),
        P(("expert", "replica"), None),
        P(None, "expert"),
        P(None, "expert"),
    )
    out_specs = P(("expert", "replica"), None)
    return jax.shard_map(shards, mesh=mesh, in_specs=in_specs, out_specs=out_specs, check_vma=False)
```

```python
import functools
import math

import jax
import jax.numpy as jnp
from jax import lax
from jax.experimental import pallas as pl
from jax.experimental.pallas import tpu as pltpu
from jax.sharding import PartitionSpec as P

HSPLIT = 4
CAP = 16
KMOM = 12
QITERS = 4
LANES = 128
UNIT = 512
DIRECT = 512
ROWS = 32
BATCH = 64
SKETCH = 12
STEPS = 32767.0

QUANTILE_LEVEL = 0.99
EPSILON = 1e-06
MESH = pl.DeviceIdType.MESH

SIN_TERMS = [(-1.0) ** i / math.factorial(2 * i + 1) for i in range(7)]
COS_TERMS = [(-1.0) ** i / math.factorial(2 * i) for i in range(8)]


def polynomial(x, terms):
    terms = [jnp.full_like(x, term) for term in terms]
    while len(terms) > 1:
        pairs = [terms[i] + terms[i + 1] * x for i in range(0, len(terms) - 1, 2)]
        terms = pairs + terms[2 * len(pairs):]
        x = x * x
    return terms[0]


def sin_cos(half_turns):
    turns = jnp.floor(half_turns + 0.5)
    rest = (half_turns - turns) * math.pi
    sign = 1.0 - 2.0 * (turns - 2.0 * jnp.floor(turns * 0.5))
    square = rest * rest
    return sign * rest * polynomial(square, SIN_TERMS), sign * polynomial(square, COS_TERMS)


def tree(terms):
    while len(terms) > 1:
        terms = [functools.reduce(jnp.add, terms[i:i + 2]) for i in range(0, len(terms), 2)]
    return terms[0]


def clip_fraction(coefficient):
    start = 1.0 - QUANTILE_LEVEL
    total = jnp.zeros_like(coefficient[0])
    for k in range(1, KMOM, 2):
        total = total + coefficient[k - 1] * ((1.0 if k % 4 == 1 else -1.0) / k)
    angle = start - (2.0 / math.pi) * total
    for _ in range(QITERS - 1):
        sine, cosine = sin_cos(angle)
        double = 2.0 * cosine
        stride = double * double - 2.0
        waves = [-sine, jnp.zeros_like(sine), sine, double * sine]
        for k in range(3, KMOM):
            waves.append(stride * waves[k - 1] - waves[k - 3])
        angle = start - (2.0 / math.pi) * tree([
            coefficient[k - 1] * (waves[k + 1] * (1.0 / k)) for k in range(1, KMOM)])
    return 0.5 * (1.0 + sin_cos(angle)[1])


def rebase(moments, ratio):
    shift = ratio - 1.0
    before = moments
    current = [
        0.5 * ratio * (before[j + 1] + before[abs(j - 1)]) + shift * before[j]
        for j in range(KMOM - 1)
    ]
    out = [current[0]]
    twice = 2.0 * shift
    for k in range(1, KMOM - 1):
        following = [
            ratio * (current[j + 1] + current[abs(j - 1)]) + twice * current[j] - before[j]
            for j in range(KMOM - 1 - k)
        ]
        before, current = current, following
        out.append(current[0])
    return out


def cuts(total, sizes):
    edges = [0]
    for size in sizes:
        edges.append(edges[-1] + size)
    return [(i, j - i) for i, j in zip(edges, edges[1:])]


def chunk_sizes(depth):
    units = depth // UNIT - DIRECT // UNIT
    middle, odd = divmod(units - 2, 2)
    return [UNIT] + [2 * UNIT] * middle + [UNIT] * odd + [UNIT, DIRECT]


def groups_of(count, parts):
    edges = [count * i // parts for i in range(parts + 1)]
    return list(zip(edges, edges[1:]))


def kernel(
    devices, replicas, chunks, token_parts, weight_parts,
    tok, rt, wg, wu, out,
    T, RT, SEL, Y, X, W, AG, AU, H, HIN, CS, CN, SK, Q, F, CT, CE, LV,
    rt_sem, tok_sem, w_sem,
    x_send, d_send, x_recv, f_send, f_recv,
    n_send, n_recv, q_send, q_recv, z_send, z_recv, c_recv, h_send, h_recv, l_send, l_recv, ready, go,
):
    groups = devices // HSPLIT
    half = devices // 2 * CAP
    width = W.shape[2]
    tiles = width // LANES
    rows = devices * CAP
    me = lax.axis_index("expert")
    z = lax.axis_index("replica")
    c = me % 2
    p = (me // 2) % 2
    a = me // HSPLIT
    partner = me + 1 - 2 * c
    lead = me + 1 - c
    last = len(chunks) - 1

    def pos(j):
        return (j % 2) * (devices // 2) + j // 2

    def other(dg, dp, dc):
        return HSPLIT * ((a + dg) % groups) + 2 * ((p + dp) % 2) + (c + dc) % 2

    combos = [(dg, dp) for dg in range(groups) for dp in range(2) if (dg, dp) != (0, 0)]
    combos = combos[::-1]
    alls = [
        (dg, dp, dc)
        for dg in range(groups) for dp in range(2) for dc in range(2)
        if (dg, dp, dc) != (0, 0, 0)
    ][::-1]
    peers = []
    for i in range(replicas - 1):
        up, down = i + (i >= z), replicas - 1 - i - (replicas - 1 - i <= z)
        peers.append(jnp.where(z < replicas // 2, down, up))

    def block(j):
        return pl.ds(pl.multiple_of(pos(j) * CAP, CAP), CAP)

    def columns(ch):
        return pl.ds(chunks[ch][0], chunks[ch][1])

    def span(first, end):
        return pl.ds(chunks[first][0], chunks[end - 1][0] + chunks[end - 1][1] - chunks[first][0])

    def remote(src, dst, send_sem, recv_sem, device):
        return pltpu.make_async_remote_copy(
            src_ref=src, dst_ref=dst, send_sem=send_sem, recv_sem=recv_sem,
            device_id=device, device_id_type=MESH)

    def settle(ref, sem):
        pltpu.make_async_copy(ref, ref, sem).wait()

    def load_tokens(i):
        part = span(*token_parts[i])
        return pltpu.make_async_copy(tok.at[:, part], T.at[:, part], tok_sem.at[i])

    def load_weights(i):
        part = span(*weight_parts[i])
        return [
            pltpu.make_async_copy(w.at[part], W.at[k, part], w_sem.at[i])
            for k, w in enumerate((wg, wu))
        ]

    load_routes = pltpu.make_async_copy(rt, RT, rt_sem)
    load_routes.start()
    load_tokens(0).start()

    barrier = pltpu.get_barrier_semaphore()
    for combo in alls:
        pl.semaphore_signal(barrier, inc=1, device_id=(other(*combo), z), device_id_type=MESH)

    @pl.when(me == 0)
    def _():
        for peer in peers:
            pl.semaphore_signal(barrier, inc=1, device_id=(me, peer), device_id_type=MESH)

    for i in range(1, len(token_parts)):
        load_tokens(i).start()

    load_routes.wait()
    routes = RT[...]
    count = routes.shape[1]
    t_from = lax.broadcasted_iota(jnp.int32, (count, count), 0)
    t_to = lax.broadcasted_iota(jnp.int32, (count, count), 1)
    earlier = jnp.where(t_from < t_to, 1.0, 0.0).astype(jnp.bfloat16)
    named = [
        jnp.sum(jnp.where(routes == (a + dg) % groups, 1.0, 0.0), axis=0, keepdims=True)
        for dg in range(groups)
    ]
    table = jnp.concatenate(
        [jnp.broadcast_to(n, (CAP, count)) for n in named], axis=0)
    before = jnp.dot(table.astype(jnp.bfloat16), earlier, preferred_element_type=jnp.float32)
    slot = (lax.broadcasted_iota(jnp.int32, (groups * CAP, count), 0) % CAP).astype(jnp.float32)
    picks = jnp.where(before == slot, table, 0.0)
    SEL[...] = picks.astype(jnp.bfloat16)

    def gather(ch):
        part = columns(ch)
        picked = jnp.dot(
            SEL[...], T[:, part], preferred_element_type=jnp.float32).astype(jnp.bfloat16)
        Y[:, part] = picked
        X[block(me), part] = picked[:CAP]

    def send_rows(ch):
        part = columns(ch)
        if ch == last:
            for dg, dp, dc in alls:
                remote(
                    Y.at[pl.ds(dg * CAP, CAP), part], X.at[block(me), part],
                    d_send, x_recv.at[ch], (other(dg, dp, dc), z)).start()
            return
        for dg, dp in combos:
            remote(
                Y.at[pl.ds(dg * CAP, CAP), part], X.at[block(me), part],
                x_send, x_recv.at[ch], (other(dg, dp, 0), z)).start()

    load_tokens(0).wait()
    gather(0)
    for i in range(len(weight_parts)):
        for copy in load_weights(i):
            copy.start()
    pl.semaphore_wait(barrier, len(alls) + jnp.where(me == 0, len(peers), 0))
    send_rows(0)

    filled = jnp.sum(picks, axis=1, keepdims=True)
    for dg in range(groups):
        total = jnp.sum(filled[dg * CAP:(dg + 1) * CAP], axis=0, keepdims=True)
        CS[dg] = jnp.broadcast_to(total, (8, LANES))
    CN[me] = CS[0]
    for dg, dp, dc in alls:
        remote(CS.at[dg], CN.at[me], n_send, n_recv, (other(dg, dp, dc), z)).start()

    for i, (first, end) in enumerate(token_parts):
        if i:
            load_tokens(i).wait()
        for ch in range(max(first, 1), end):
            gather(ch)
            send_rows(ch)

    @pl.when(me == 0)
    def _():
        for peer in peers:
            pl.semaphore_signal(ready, inc=1, device_id=(me, peer), device_id_type=MESH)

    own = pl.ds(pl.multiple_of(c * half, half), half)

    def collect(ch):
        part = columns(ch)
        settle(X.at[pl.ds(0, len(combos) * CAP), part], x_recv.at[ch])
        remote(
            X.at[own, part], X.at[own, part], f_send, f_recv.at[ch], (partner, z)).start()

    def arrive(ch):
        part = columns(ch)
        if ch < last:
            settle(X.at[pl.ds(0, half), part], f_recv.at[ch])
        else:
            settle(X.at[pl.ds(0, len(alls) * CAP), part], x_recv.at[ch])
        for i, (first, end) in enumerate(weight_parts):
            if first == ch:
                settle(W.at[:, span(first, end)], w_sem.at[i])

    def multiply(ch):
        arrive(ch)
        part = columns(ch)
        x = X[:, part]
        for k, A in enumerate((AG, AU)):
            product = jnp.dot(x, W[k, part, :], preferred_element_type=jnp.float32)
            A[...] = A[...] + product if ch else product

    def release():
        @pl.when(me == 0)
        def _():
            pl.semaphore_wait(ready, len(peers))
            for combo in alls:
                pl.semaphore_signal(go, inc=1, device_id=(other(*combo), z), device_id_type=MESH)

    def share_count():
        settle(CN.at[pl.ds(0, len(alls))], n_recv)
        total = functools.reduce(jnp.add, [CN[j] for j in range(devices)])
        CT[z] = total

        @pl.when(me != 0)
        def _():
            pl.semaphore_wait(go, 1)

        @pl.when(c == 1)
        def _():
            for peer in peers:
                remote(CT.at[z], CT.at[z], n_send, c_recv, (me, peer)).start()

    collect(0)
    for ch in range(1, last):
        collect(ch)
        multiply(ch - 1)
        if ch == last // 2 - 1:
            release()
        if ch == last - 1:
            share_count()
    arrive(last - 1)
    arrive(last)
    part = span(last - 1, last + 1)
    x = X[:, part]
    strip = min(2 * LANES, width)
    tops = []
    for n in range(0, width, strip):
        lanes = slice(n, n + strip)
        g, u = (
            A[:, lanes] + jnp.dot(x, W[k, part, lanes], preferred_element_type=jnp.float32)
            for k, A in enumerate((AG, AU)))
        h = g / (1.0 + jnp.exp(-g)) * u
        H[:, lanes] = h
        tops.append(jnp.max(jnp.abs(h), axis=0, keepdims=True))

    ceiling = jnp.concatenate(tops, axis=1) + EPSILON
    mine = c * replicas + z
    for l in range(tiles):
        CE[mine, l:l + 1, :] = ceiling[:, l * LANES:(l + 1) * LANES]

    def share(ref, send_sem, recv_sem, targets):
        for peer in targets:
            remote(ref, ref, send_sem, recv_sem, (lead, peer)).start()

    def share_here(ref, send_sem, recv_sem):
        @pl.when(c == 0)
        def _():
            remote(ref, ref, send_sem, recv_sem, (lead, z)).start()

    share(CE.at[mine], z_send, z_recv, peers)
    share_here(CE.at[mine], z_send, z_recv)
    scale = 2.0 / ceiling
    here = CT[z, 0:1, :]
    empty = float(rows) - here
    stretch = STEPS / jnp.maximum(here, 1.0)
    even = lax.broadcasted_iota(jnp.int32, (SKETCH * tiles, LANES), 0) % 2 == 0
    bounds = [SKETCH * tiles * 2 // 3 // 16 * 16, SKETCH * tiles]
    sent = 0

    for l in range(tiles):
        lanes = slice(l * LANES, (l + 1) * LANES)
        scale_l = scale[:, lanes]

        def sketch(i, sums):
            part = pl.ds(pl.multiple_of(i * BATCH, BATCH), BATCH)
            scaled = jnp.abs(H[part, lanes]) * scale_l - 1.0
            double = 2.0 * scaled
            previous, current = jnp.ones_like(scaled), scaled
            new = []
            for k in range(KMOM - 1):
                new.append(sums[k] + jnp.sum(current.reshape(BATCH // 8, 8, LANES), axis=0))
                previous, current = current, double * current - previous
            return tuple(new)

        zero = jnp.zeros((8, LANES), jnp.float32)
        sums = lax.fori_loop(0, rows // BATCH, sketch, (zero,) * (KMOM - 1), unroll=True)
        SK[l * SKETCH:l * SKETCH + 1, :] = jnp.zeros((1, LANES), jnp.float32)
        for k in range(1, KMOM):
            SK[l * SKETCH + k:l * SKETCH + k + 1, :] = jnp.sum(
                sums[k - 1], axis=0, keepdims=True)
        while bounds and bounds[0] <= (l + 1) * SKETCH:
            part = slice(sent, bounds[0])
            held = SK[part, :] + jnp.where(even[part], -empty, empty)
            code = jnp.minimum(jnp.maximum(held * stretch, -STEPS), STEPS)
            Q[mine, part, :] = jnp.floor(code + 0.5).astype(jnp.int32).astype(jnp.int16)
            share(Q.at[mine, part, :], q_send, q_recv, peers[:1])
            sent = bounds.pop(0)
    share(Q.at[mine], q_send, q_recv, peers[1:])
    share_here(Q.at[mine], q_send, q_recv)
    for dg, dp, dc in alls:
        j = other(dg, dp, dc)
        remote(H.at[block(j), :], HIN.at[me], h_send, h_recv, (j, z)).start()

    HIN[me] = H[block(me), :]
    def calibrate():
        settle(CT.at[pl.ds(0, len(peers))], c_recv)
        settle(CE.at[pl.ds(0, 2 * replicas - 1)], z_recv)
        local = [CE[i, 0:tiles, :] for i in range(2 * replicas)]
        common = [
            functools.reduce(jnp.maximum, local[k * replicas:(k + 1) * replicas])
            for k in range(2)
        ]
        ratio = jnp.concatenate(
            [value / common[i // replicas] for i, value in enumerate(local)], axis=0)
        here = [CT[r, 0:tiles, :] for r in range(replicas)]
        total = functools.reduce(jnp.add, here)
        part = jnp.concatenate([value / total for value in here] * 2, axis=0)

        def added(value):
            value = value * part
            value = [value[i * tiles:(i + 1) * tiles] for i in range(2 * replicas)]
            return jnp.concatenate([
                functools.reduce(jnp.add, value[k * replicas:(k + 1) * replicas])
                for k in range(2)
            ], axis=0)

        settle(Q.at[pl.ds(0, 2 * replicas - 1)], q_recv)
        for i in range(2 * replicas):
            F[i * SKETCH * tiles:(i + 1) * SKETCH * tiles, :] = (
                Q[i].astype(jnp.int32).astype(jnp.float32) * (1.0 / STEPS))
        moments = [jnp.ones_like(ratio)]
        moments += [
            F[pl.ds(k, 2 * replicas * tiles, stride=SKETCH), :] for k in range(1, KMOM)]
        level = clip_fraction([added(value) for value in rebase(moments, ratio)])
        for k in range(2):
            LV[me - 1 + k] = jnp.concatenate(
                [common[k] * level[k * tiles:(k + 1) * tiles], 1.0 / common[k]], axis=0)
        pair = LV.at[pl.ds(me - 1, 2)]
        for dg, dp, dc in alls:
            remote(pair, pair, l_send, l_recv, (other(dg, dp, dc), z)).start()

    @pl.when(c == 1)
    def _():
        calibrate()

    settle(X.at[pl.ds(0, len(combos) * CAP), span(0, last)], x_send)
    settle(X.at[pl.ds(0, len(alls) * CAP), columns(last)], d_send)
    settle(X.at[pl.ds(0, half), span(0, last)], f_send)
    settle(CN.at[pl.ds(0, len(alls))], n_send)

    @pl.when(c == 0)
    def _():
        settle(Q.at[pl.ds(0, len(peers) + 1)], q_send)
        settle(CE.at[pl.ds(0, len(peers) + 1)], z_send)

    @pl.when(c == 1)
    def _():
        settle(CT.at[pl.ds(0, len(peers))], n_send)
        settle(Q.at[pl.ds(0, len(peers))], q_send)
        settle(CE.at[pl.ds(0, len(peers))], z_send)
        settle(X.at[pl.ds(0, 2 * CAP), pl.ds(0, len(alls) * LANES)], l_send)

    settle(HIN.at[pl.ds(0, len(alls))], h_send)
    settle(HIN.at[pl.ds(0, len(alls))], h_recv)
    @pl.when(c == 0)
    def _():
        settle(LV.at[pl.ds(0, devices)], l_recv)

    @pl.when(c == 1)
    def _():
        settle(LV.at[pl.ds(0, devices - 2)], l_recv)

    def finish(i, _):
        for k in range(HSPLIT):
            e = i * HSPLIT + k
            for l in range(tiles):
                bound = LV[e, l:l + 1, :]
                factor = LV[e, tiles + l:tiles + l + 1, :]
                h = HIN[e, :, l * LANES:(l + 1) * LANES]
                h = jnp.minimum(jnp.maximum(h, -bound), bound) * factor
                lanes = pl.ds(pl.multiple_of(e * width + l * LANES, LANES), LANES)
                out[:, lanes] = h.astype(jnp.bfloat16)
        return 0

    lax.fori_loop(0, groups, finish, 0)


def shards(tokens, routes, gate_weight, up_weight):
    devices = lax.axis_size("expert")
    replicas = lax.axis_size("replica")
    groups = devices // HSPLIT
    count, depth = tokens.shape
    width = gate_weight.shape[1]
    chunks = cuts(depth, chunk_sizes(depth))
    token_parts = [(0, 1), (1, 3), (3, len(chunks))]
    weight_parts = groups_of(len(chunks), 4)
    rows = devices * CAP
    tiles = width // LANES
    bf16, f32 = jnp.bfloat16, jnp.float32
    dma = pltpu.SemaphoreType.DMA
    anywhere = pl.BlockSpec(memory_space=pl.ANY)
    return pl.pallas_call(
        functools.partial(kernel, devices, replicas, chunks, token_parts, weight_parts),
        out_shape=pltpu.VMEM((CAP, devices * width), bf16),
        in_specs=[anywhere] * 4,
        out_specs=pl.BlockSpec(memory_space=pltpu.VMEM),
        scratch_shapes=[
            pltpu.VMEM((count, depth), bf16),
            pltpu.VMEM((routes.shape[1], count), jnp.int32),
            pltpu.VMEM((groups * CAP, count), bf16),
            pltpu.VMEM((groups * CAP, depth), bf16),
            pltpu.VMEM((rows, depth), bf16),
            pltpu.VMEM((2, depth, width), bf16),
            pltpu.VMEM((rows, width), f32),
            pltpu.VMEM((rows, width), f32),
            pltpu.VMEM((rows, width), f32),
            pltpu.VMEM((devices, CAP, width), f32),
            pltpu.VMEM((groups, 8, LANES), f32),
            pltpu.VMEM((devices, 8, LANES), f32),
            pltpu.VMEM((SKETCH * tiles, LANES), f32),
            pltpu.VMEM((2 * replicas, SKETCH * tiles, LANES), jnp.int16),
            pltpu.VMEM((2 * replicas * SKETCH * tiles, LANES), f32),
            pltpu.VMEM((replicas, 8, LANES), f32),
            pltpu.VMEM((2 * replicas, 8, LANES), f32),
            pltpu.VMEM((devices, 2 * tiles, LANES), f32),
            dma(()), dma((len(token_parts),)), dma((len(weight_parts),)),
            dma(()), dma(()), dma((len(chunks),)), dma(()), dma((len(chunks) - 1,)),
            dma(()), dma(()), dma(()), dma(()), dma(()), dma(()), dma(()), dma(()), dma(()), dma(()), dma(()),
            pltpu.SemaphoreType.REGULAR, pltpu.SemaphoreType.REGULAR,
        ],
        compiler_params=pltpu.CompilerParams(
            collective_id=0, has_side_effects=True, vmem_limit_bytes=56 * 1024 * 1024),
    )(tokens, pltpu.with_memory_space_constraint(routes.T, pltpu.HBM), gate_weight, up_weight)


def solution(mesh):
    in_specs = (
        P(("expert", "replica"), None),
        P(("expert", "replica"), None),
        P(None, "expert"),
        P(None, "expert"),
    )
    out_specs = P(("expert", "replica"), None)
    return jax.shard_map(shards, mesh=mesh, in_specs=in_specs, out_specs=out_specs, check_vma=False)
```

```python
import functools
import math

import jax
import jax.numpy as jnp
from jax import lax
from jax.experimental import pallas as pl
from jax.experimental.pallas import tpu as pltpu
from jax.sharding import PartitionSpec as P

HSPLIT = 4
CAP = 16
KMOM = 12
QITERS = 4
LANES = 128
UNIT = 512
TAIL = 256
WIDEST = 2
ROWS = 32
BATCH = 64
SKETCH = 12
STEPS = 32767.0

QUANTILE_LEVEL = 0.99
EPSILON = 1e-06
MESH = pl.DeviceIdType.MESH

SIN_TERMS = [(-1.0) ** i / math.factorial(2 * i + 1) for i in range(7)]
COS_TERMS = [(-1.0) ** i / math.factorial(2 * i) for i in range(8)]


def polynomial(x, terms):
    terms = [jnp.full_like(x, term) for term in terms]
    while len(terms) > 1:
        pairs = [terms[i] + terms[i + 1] * x for i in range(0, len(terms) - 1, 2)]
        terms = pairs + terms[2 * len(pairs):]
        x = x * x
    return terms[0]


def sin_cos(half_turns):
    turns = jnp.floor(half_turns + 0.5)
    rest = (half_turns - turns) * math.pi
    sign = 1.0 - 2.0 * (turns - 2.0 * jnp.floor(turns * 0.5))
    square = rest * rest
    return sign * rest * polynomial(square, SIN_TERMS), sign * polynomial(square, COS_TERMS)


def tree(terms):
    while len(terms) > 1:
        terms = [functools.reduce(jnp.add, terms[i:i + 2]) for i in range(0, len(terms), 2)]
    return terms[0]


def clip_fraction(coefficient):
    start = 1.0 - QUANTILE_LEVEL
    total = jnp.zeros_like(coefficient[0])
    for k in range(1, KMOM, 2):
        total = total + coefficient[k - 1] * ((1.0 if k % 4 == 1 else -1.0) / k)
    angle = start - (2.0 / math.pi) * total
    for _ in range(QITERS - 1):
        sine, cosine = sin_cos(angle)
        double = 2.0 * cosine
        stride = double * double - 2.0
        waves = [-sine, jnp.zeros_like(sine), sine, double * sine]
        for k in range(3, KMOM):
            waves.append(stride * waves[k - 1] - waves[k - 3])
        angle = start - (2.0 / math.pi) * tree([
            coefficient[k - 1] * (waves[k + 1] * (1.0 / k)) for k in range(1, KMOM)])
    return 0.5 * (1.0 + sin_cos(angle)[1])


def rebase(moments, ratio):
    shift = ratio - 1.0
    before = moments
    current = [
        0.5 * ratio * (before[j + 1] + before[abs(j - 1)]) + shift * before[j]
        for j in range(KMOM - 1)
    ]
    out = [current[0]]
    twice = 2.0 * shift
    for k in range(1, KMOM - 1):
        following = [
            ratio * (current[j + 1] + current[abs(j - 1)]) + twice * current[j] - before[j]
            for j in range(KMOM - 1 - k)
        ]
        before, current = current, following
        out.append(current[0])
    return out


def cuts(total, sizes):
    edges = [0]
    for size in sizes:
        edges.append(edges[-1] + size)
    return [(i, j - i) for i, j in zip(edges, edges[1:])]


def chunk_sizes(depth):
    ends = [UNIT, UNIT, UNIT]
    units = (depth - sum(ends)) // UNIT - 1
    middle, odd = divmod(units, 2)
    first = depth - sum(ends) - UNIT * units
    return [first] + [2 * UNIT] * middle + [UNIT] * odd + ends


def groups_of(count, parts):
    edges = [count * i // parts for i in range(parts + 1)]
    return list(zip(edges, edges[1:]))


def kernel(
    devices, replicas, chunks, token_parts, weight_parts,
    tok, rt, wg, wu, out,
    T, RT, SEL, Y, X, W, AG, AU, H, HIN, CS, CN, SK, Q, F, CT, CE, LV,
    rt_sem, tok_sem, w_sem, sent_sem, x_recv, f_recv, e_recv,
    n_recv, q_recv, z_recv, c_recv, h_recv, l_recv, ready, go,
):
    groups = devices // HSPLIT
    half = devices // 2 * CAP
    width = W.shape[2]
    tiles = width // LANES
    rows = devices * CAP
    me = lax.axis_index("expert")
    z = lax.axis_index("replica")
    c = me % 2
    p = (me // 2) % 2
    a = me // HSPLIT
    partner = me + 1 - 2 * c
    lead = me + 1 - c
    last = len(chunks) - 1

    def pos(j):
        return (j % 2) * (devices // 2) + j // 2

    def other(dg, dp, dc):
        return HSPLIT * ((a + dg) % groups) + 2 * ((p + dp) % 2) + (c + dc) % 2

    combos = [(dg, dp) for dg in range(groups) for dp in range(2) if (dg, dp) != (0, 0)]
    combos = combos[::-1]
    alls = [
        (dg, dp, dc)
        for dg in range(groups) for dp in range(2) for dc in range(2)
        if (dg, dp, dc) != (0, 0, 0)
    ][::-1]
    peers = []
    for i in range(replicas - 1):
        up, down = i + (i >= z), replicas - 1 - i - (replicas - 1 - i <= z)
        peers.append(jnp.where(z < replicas // 2, down, up))

    def block(j):
        return pl.ds(pl.multiple_of(pos(j) * CAP, CAP), CAP)

    def columns(ch):
        return pl.ds(chunks[ch][0], chunks[ch][1])

    def span(first, end):
        return pl.ds(chunks[first][0], chunks[end - 1][0] + chunks[end - 1][1] - chunks[first][0])

    def remote(src, dst, send_sem, recv_sem, device):
        return pltpu.make_async_remote_copy(
            src_ref=src, dst_ref=dst, send_sem=send_sem, recv_sem=recv_sem,
            device_id=device, device_id_type=MESH)

    def settle(ref, sem):
        pltpu.make_async_copy(ref, ref, sem).wait()

    def load_tokens(i):
        part = span(*token_parts[i])
        return pltpu.make_async_copy(tok.at[:, part], T.at[:, part], tok_sem.at[i])

    def load_weights(i):
        part = span(*weight_parts[i])
        return [
            pltpu.make_async_copy(w.at[part], W.at[k, part], w_sem.at[i])
            for k, w in enumerate((wg, wu))
        ]

    load_routes = pltpu.make_async_copy(rt, RT, rt_sem)
    load_routes.start()
    load_tokens(0).start()

    barrier = pltpu.get_barrier_semaphore()
    for combo in alls:
        pl.semaphore_signal(barrier, inc=1, device_id=(other(*combo), z), device_id_type=MESH)

    @pl.when(me == 0)
    def _():
        for peer in peers:
            pl.semaphore_signal(barrier, inc=1, device_id=(me, peer), device_id_type=MESH)

    for i in range(1, len(token_parts)):
        load_tokens(i).start()

    load_routes.wait()
    routes = RT[...]
    count = routes.shape[1]
    t_from = lax.broadcasted_iota(jnp.int32, (count, count), 0)
    t_to = lax.broadcasted_iota(jnp.int32, (count, count), 1)
    earlier = jnp.where(t_from < t_to, 1.0, 0.0).astype(jnp.bfloat16)
    named = [
        jnp.sum(jnp.where(routes == (a + dg) % groups, 1.0, 0.0), axis=0, keepdims=True)
        for dg in range(groups)
    ]
    table = jnp.concatenate(
        [jnp.broadcast_to(n, (CAP, count)) for n in named], axis=0)
    before = jnp.dot(table.astype(jnp.bfloat16), earlier, preferred_element_type=jnp.float32)
    slot = (lax.broadcasted_iota(jnp.int32, (groups * CAP, count), 0) % CAP).astype(jnp.float32)
    picks = jnp.where(before == slot, table, 0.0)
    SEL[...] = picks.astype(jnp.bfloat16)

    def gather(ch):
        part = columns(ch)
        picked = jnp.dot(
            SEL[...], T[:, part], preferred_element_type=jnp.float32).astype(jnp.bfloat16)
        Y[:, part] = picked

        X[block(me), part] = picked[:CAP]

    def send_rows(ch, pairs):
        part = columns(ch)
        for dg, dp in pairs:
            remote(
                Y.at[pl.ds(dg * CAP, CAP), part], X.at[block(me), part],
                sent_sem, x_recv.at[ch], (other(dg, dp, 0), z)).start()

    def send_across(pairs):
        part = columns(last)

        @pl.when(c == 0)
        def _():
            for dg, dp in pairs:
                remote(
                    Y.at[pl.ds(dg * CAP, CAP), part], X.at[block(me), part],
                    sent_sem, e_recv, (other(dg, dp, 1), z)).start()

    load_tokens(0).wait()
    gather(0)
    for i in range(len(weight_parts)):
        for copy in load_weights(i):
            copy.start()
    pl.semaphore_wait(barrier, len(alls) + jnp.where(me == 0, len(peers), 0))
    send_rows(0, combos)

    filled = jnp.sum(picks, axis=1, keepdims=True)
    for dg in range(groups):
        total = jnp.sum(filled[dg * CAP:(dg + 1) * CAP], axis=0, keepdims=True)
        CS[dg] = jnp.broadcast_to(total, (8, LANES))
    CN[me] = CS[0]
    for dg, dp, dc in alls:
        remote(CS.at[dg], CN.at[me], sent_sem, n_recv, (other(dg, dp, dc), z)).start()

    for i, (first, end) in enumerate(token_parts):
        if i:
            load_tokens(i).wait()
        for ch in range(max(first, 1), end):
            gather(ch)
            if ch < last - 1:
                send_rows(ch, combos)
    far = [pair for pair in combos if 0 not in pair]
    near = [pair for pair in combos if 0 in pair]
    for pairs in (far, near):
        for ch in (last - 1, last):
            send_rows(ch, pairs)
        send_across(pairs)
    send_across([(0, 0)])

    @pl.when(me == 0)
    def _():
        for peer in peers:
            pl.semaphore_signal(ready, inc=1, device_id=(me, peer), device_id_type=MESH)

    own = pl.ds(pl.multiple_of(c * half, half), half)

    def receive(ch):
        settle(X.at[pl.ds(0, len(combos) * CAP), columns(ch)], x_recv.at[ch])

    def forward(ch):
        part = columns(ch)
        remote(
            X.at[own, part], X.at[own, part], sent_sem, f_recv.at[ch], (partner, z)).start()

    def collect(ch):
        receive(ch)
        forward(ch)

    def arrive(ch):
        part = columns(ch)
        if ch < last:
            settle(X.at[pl.ds(0, half), part], f_recv.at[ch])
        else:
            @pl.when(c == 0)
            def _():
                receive(ch)
                settle(X.at[pl.ds(0, half), part], f_recv.at[ch])

            @pl.when(c == 1)
            def _():
                settle(X.at[pl.ds(0, (len(combos) + 1) * CAP), part], e_recv)

        for i, (first, end) in enumerate(weight_parts):
            if first == ch:
                settle(W.at[:, span(first, end)], w_sem.at[i])

    def multiply(ch):
        arrive(ch)
        part = columns(ch)
        x = X[:, part]
        for k, A in enumerate((AG, AU)):
            product = jnp.dot(x, W[k, part, :], preferred_element_type=jnp.float32)
            A[...] = A[...] + product if ch else product

    def release():
        @pl.when(me == 0)
        def _():
            pl.semaphore_wait(ready, len(peers))
            for combo in alls:
                pl.semaphore_signal(go, inc=1, device_id=(other(*combo), z), device_id_type=MESH)

    def share_count():
        settle(CN.at[pl.ds(0, len(alls))], n_recv)
        total = functools.reduce(jnp.add, [CN[j] for j in range(devices)])
        CT[z] = total

        @pl.when(me != 0)
        def _():
            pl.semaphore_wait(go, 1)

        @pl.when(c == 1)
        def _():
            for peer in peers:
                remote(CT.at[z], CT.at[z], sent_sem, c_recv, (me, peer)).start()

    collect(0)
    steady = last - 4
    for ch in range(1, steady + 1):
        collect(ch)
        multiply(ch - 1)
        if ch == 2:
            release()
        if ch == steady:
            share_count()

    @pl.when(c == 0)
    def _():
        multiply(steady)
        for ch in range(steady + 1, last - 1):
            collect(ch)
            multiply(ch)
        collect(last - 1)

    @pl.when(c == 1)
    def _():
        collect(steady + 1)
        collect(steady + 2)
        multiply(steady)
        collect(last - 1)
        collect(last)
        for ch in range(steady + 1, last - 1):
            multiply(ch)

    arrive(last - 1)
    arrive(last)
    part = span(last - 1, last + 1)
    x = X[:, part]
    strip = min(2 * LANES, width)
    tops = []
    for n in range(0, width, strip):
        lanes = slice(n, n + strip)
        g, u = (
            A[:, lanes] + jnp.dot(x, W[k, part, lanes], preferred_element_type=jnp.float32)
            for k, A in enumerate((AG, AU)))
        h = g / (1.0 + jnp.exp(-g)) * u
        H[:, lanes] = h
        tops.append(jnp.max(jnp.abs(h), axis=0, keepdims=True))

    ceiling = jnp.concatenate(tops, axis=1) + EPSILON
    mine = c * replicas + z
    for l in range(tiles):
        CE[mine, l:l + 1, :] = ceiling[:, l * LANES:(l + 1) * LANES]

    def share(ref, send_sem, recv_sem, targets):
        for peer in targets:
            remote(ref, ref, send_sem, recv_sem, (lead, peer)).start()

    def share_here(ref, send_sem, recv_sem):
        @pl.when(c == 0)
        def _():
            remote(ref, ref, send_sem, recv_sem, (lead, z)).start()

    share(CE.at[mine], sent_sem, z_recv, peers)
    share_here(CE.at[mine], sent_sem, z_recv)
    scale = 2.0 / ceiling
    here = CT[z, 0:1, :]
    empty = float(rows) - here
    stretch = STEPS / jnp.maximum(here, 1.0)
    even = lax.broadcasted_iota(jnp.int32, (SKETCH * tiles, LANES), 0) % 2 == 0
    bounds = [SKETCH * tiles * 2 // 3 // 16 * 16, SKETCH * tiles]
    sent = 0

    for l in range(tiles):
        lanes = slice(l * LANES, (l + 1) * LANES)
        scale_l = scale[:, lanes]

        def sketch(i, sums):
            part = pl.ds(pl.multiple_of(i * BATCH, BATCH), BATCH)
            scaled = jnp.abs(H[part, lanes]) * scale_l - 1.0
            double = 2.0 * scaled
            previous, current = jnp.ones_like(scaled), scaled
            new = []
            for k in range(KMOM - 1):
                new.append(sums[k] + jnp.sum(current.reshape(BATCH // 8, 8, LANES), axis=0))
                previous, current = current, double * current - previous
            return tuple(new)

        zero = jnp.zeros((8, LANES), jnp.float32)
        sums = lax.fori_loop(0, rows // BATCH, sketch, (zero,) * (KMOM - 1), unroll=True)
        SK[l * SKETCH:l * SKETCH + 1, :] = jnp.zeros((1, LANES), jnp.float32)
        for k in range(1, KMOM):
            SK[l * SKETCH + k:l * SKETCH + k + 1, :] = jnp.sum(
                sums[k - 1], axis=0, keepdims=True)
        while bounds and bounds[0] <= (l + 1) * SKETCH:
            part = slice(sent, bounds[0])
            held = SK[part, :] + jnp.where(even[part], -empty, empty)
            code = jnp.minimum(jnp.maximum(held * stretch, -STEPS), STEPS)
            Q[mine, part, :] = jnp.floor(code + 0.5).astype(jnp.int32).astype(jnp.int16)
            share(Q.at[mine, part, :], sent_sem, q_recv, peers[:1])
            sent = bounds.pop(0)
    share(Q.at[mine], sent_sem, q_recv, peers[1:])
    share_here(Q.at[mine], sent_sem, q_recv)
    for dg, dp, dc in alls:
        j = other(dg, dp, dc)
        remote(H.at[block(j), :], HIN.at[me], sent_sem, h_recv, (j, z)).start()

    HIN[me] = H[block(me), :]
    def calibrate():
        settle(CT.at[pl.ds(0, len(peers))], c_recv)
        settle(CE.at[pl.ds(0, 2 * replicas - 1)], z_recv)
        local = [CE[i, 0:tiles, :] for i in range(2 * replicas)]
        common = [
            functools.reduce(jnp.maximum, local[k * replicas:(k + 1) * replicas])
            for k in range(2)
        ]
        ratio = jnp.concatenate(
            [value / common[i // replicas] for i, value in enumerate(local)], axis=0)
        here = [CT[r, 0:tiles, :] for r in range(replicas)]
        total = functools.reduce(jnp.add, here)
        part = jnp.concatenate([value / total for value in here] * 2, axis=0)

        def added(value):
            value = value * part
            value = [value[i * tiles:(i + 1) * tiles] for i in range(2 * replicas)]
            return jnp.concatenate([
                functools.reduce(jnp.add, value[k * replicas:(k + 1) * replicas])
                for k in range(2)
            ], axis=0)

        settle(Q.at[pl.ds(0, 2 * replicas - 1)], q_recv)
        for i in range(2 * replicas):
            F[i * SKETCH * tiles:(i + 1) * SKETCH * tiles, :] = (
                Q[i].astype(jnp.int32).astype(jnp.float32) * (1.0 / STEPS))
        moments = [jnp.ones_like(ratio)]
        moments += [
            F[pl.ds(k, 2 * replicas * tiles, stride=SKETCH), :] for k in range(1, KMOM)]
        level = clip_fraction([added(value) for value in rebase(moments, ratio)])
        for k in range(2):
            LV[me - 1 + k] = jnp.concatenate(
                [common[k] * level[k * tiles:(k + 1) * tiles], 1.0 / common[k]], axis=0)
        pair = LV.at[pl.ds(me - 1, 2)]
        for dg, dp, dc in alls:
            remote(pair, pair, sent_sem, l_recv, (other(dg, dp, dc), z)).start()

    @pl.when(c == 1)
    def _():
        calibrate()

    settle(X.at[pl.ds(0, len(combos) * CAP), :], sent_sem)
    settle(X.at[pl.ds(0, half), span(0, last)], sent_sem)
    settle(CN.at[pl.ds(0, len(alls))], sent_sem)
    settle(Q.at[pl.ds(0, len(peers))], sent_sem)
    settle(CE.at[pl.ds(0, len(peers))], sent_sem)

    @pl.when(c == 0)
    def _():
        settle(X.at[pl.ds(0, (len(combos) + 1) * CAP), columns(last)], sent_sem)
        settle(Q.at[0], sent_sem)
        settle(CE.at[0], sent_sem)

    @pl.when(c == 1)
    def _():
        settle(X.at[pl.ds(0, half), columns(last)], sent_sem)
        settle(CT.at[pl.ds(0, len(peers))], sent_sem)
        settle(X.at[pl.ds(0, 2 * CAP), pl.ds(0, len(alls) * LANES)], sent_sem)

    settle(HIN.at[pl.ds(0, len(alls))], sent_sem)
    settle(HIN.at[pl.ds(0, len(alls))], h_recv)
    @pl.when(c == 0)
    def _():
        settle(LV.at[pl.ds(0, devices)], l_recv)

    @pl.when(c == 1)
    def _():
        settle(LV.at[pl.ds(0, devices - 2)], l_recv)

    def finish(i, _):
        for k in range(HSPLIT):
            e = i * HSPLIT + k
            for l in range(tiles):
                bound = LV[e, l:l + 1, :]
                factor = LV[e, tiles + l:tiles + l + 1, :]
                h = HIN[e, :, l * LANES:(l + 1) * LANES]
                h = jnp.minimum(jnp.maximum(h, -bound), bound) * factor
                lanes = pl.ds(pl.multiple_of(e * width + l * LANES, LANES), LANES)
                out[:, lanes] = h.astype(jnp.bfloat16)
        return 0

    lax.fori_loop(0, groups, finish, 0)


def shards(tokens, routes, gate_weight, up_weight):
    devices = lax.axis_size("expert")
    replicas = lax.axis_size("replica")
    groups = devices // HSPLIT
    count, depth = tokens.shape
    width = gate_weight.shape[1]
    chunks = cuts(depth, chunk_sizes(depth))
    token_parts = [(0, 1), (1, len(chunks))]
    weight_parts = groups_of(len(chunks), 3)
    rows = devices * CAP
    tiles = width // LANES
    bf16, f32 = jnp.bfloat16, jnp.float32
    dma = pltpu.SemaphoreType.DMA
    anywhere = pl.BlockSpec(memory_space=pl.ANY)
    return pl.pallas_call(
        functools.partial(kernel, devices, replicas, chunks, token_parts, weight_parts),
        out_shape=pltpu.VMEM((CAP, devices * width), bf16),
        in_specs=[anywhere] * 4,
        out_specs=pl.BlockSpec(memory_space=pltpu.VMEM),
        scratch_shapes=[
            pltpu.VMEM((count, depth), bf16),
            pltpu.VMEM((routes.shape[1], count), jnp.int32),
            pltpu.VMEM((groups * CAP, count), bf16),
            pltpu.VMEM((groups * CAP, depth), bf16),
            pltpu.VMEM((rows, depth), bf16),
            pltpu.VMEM((2, depth, width), bf16),
            pltpu.VMEM((rows, width), f32),
            pltpu.VMEM((rows, width), f32),
            pltpu.VMEM((rows, width), f32),
            pltpu.VMEM((devices, CAP, width), f32),
            pltpu.VMEM((groups, 8, LANES), f32),
            pltpu.VMEM((devices, 8, LANES), f32),
            pltpu.VMEM((SKETCH * tiles, LANES), f32),
            pltpu.VMEM((2 * replicas, SKETCH * tiles, LANES), jnp.int16),
            pltpu.VMEM((2 * replicas * SKETCH * tiles, LANES), f32),
            pltpu.VMEM((replicas, 8, LANES), f32),
            pltpu.VMEM((2 * replicas, 8, LANES), f32),
            pltpu.VMEM((devices, 2 * tiles, LANES), f32),
            dma(()), dma((len(token_parts),)), dma((len(weight_parts),)), dma(()),
            dma((len(chunks),)), dma((len(chunks),)), dma(()),
            dma(()), dma(()), dma(()), dma(()), dma(()), dma(()),
            pltpu.SemaphoreType.REGULAR, pltpu.SemaphoreType.REGULAR,
        ],
        compiler_params=pltpu.CompilerParams(
            collective_id=0, has_side_effects=True, vmem_limit_bytes=56 * 1024 * 1024),
    )(tokens, pltpu.with_memory_space_constraint(routes.T, pltpu.HBM), gate_weight, up_weight)


def solution(mesh):
    in_specs = (
        P(("expert", "replica"), None),
        P(("expert", "replica"), None),
        P(None, "expert"),
        P(None, "expert"),
    )
    out_specs = P(("expert", "replica"), None)
    return jax.shard_map(shards, mesh=mesh, in_specs=in_specs, out_specs=out_specs, check_vma=False)
```

```python
import functools
import math

import jax
import jax.numpy as jnp
from jax import lax
from jax.experimental import pallas as pl
from jax.experimental.pallas import tpu as pltpu
from jax.sharding import PartitionSpec as P

HSPLIT = 4
CAP = 16
KMOM = 12
QITERS = 4
LANES = 128
UNIT = 512
TAIL = 256
WIDEST = 2
ROWS = 32
BATCH = 64
SKETCH = 12
STEPS = 32767.0

QUANTILE_LEVEL = 0.99
EPSILON = 1e-06
MESH = pl.DeviceIdType.MESH

SIN_TERMS = [(-1.0) ** i / math.factorial(2 * i + 1) for i in range(7)]
COS_TERMS = [(-1.0) ** i / math.factorial(2 * i) for i in range(8)]


def polynomial(x, terms):
    terms = [jnp.full_like(x, term) for term in terms]
    while len(terms) > 1:
        pairs = [terms[i] + terms[i + 1] * x for i in range(0, len(terms) - 1, 2)]
        terms = pairs + terms[2 * len(pairs):]
        x = x * x
    return terms[0]


def sin_cos(half_turns):
    turns = jnp.floor(half_turns + 0.5)
    rest = (half_turns - turns) * math.pi
    sign = 1.0 - 2.0 * (turns - 2.0 * jnp.floor(turns * 0.5))
    square = rest * rest
    return sign * rest * polynomial(square, SIN_TERMS), sign * polynomial(square, COS_TERMS)


def tree(terms):
    while len(terms) > 1:
        terms = [functools.reduce(jnp.add, terms[i:i + 2]) for i in range(0, len(terms), 2)]
    return terms[0]


def clip_fraction(coefficient):
    start = 1.0 - QUANTILE_LEVEL
    total = jnp.zeros_like(coefficient[0])
    for k in range(1, KMOM, 2):
        total = total + coefficient[k - 1] * ((1.0 if k % 4 == 1 else -1.0) / k)
    angle = start - (2.0 / math.pi) * total
    for _ in range(QITERS - 1):
        sine, cosine = sin_cos(angle)
        double = 2.0 * cosine
        stride = double * double - 2.0
        waves = [-sine, jnp.zeros_like(sine), sine, double * sine]
        for k in range(3, KMOM):
            waves.append(stride * waves[k - 1] - waves[k - 3])
        angle = start - (2.0 / math.pi) * tree([
            coefficient[k - 1] * (waves[k + 1] * (1.0 / k)) for k in range(1, KMOM)])
    return 0.5 * (1.0 + sin_cos(angle)[1])


def rebased(ratio):
    shift = ratio - 1.0
    twice = 2.0 * shift
    zero = jnp.zeros_like(ratio)
    before, current = [jnp.ones_like(ratio)], [shift, ratio]
    rows = [current]
    for k in range(2, KMOM):
        padded = current + [zero, zero]
        following = [ratio * current[1] + twice * current[0] - before[0]]
        for m in range(1, k + 1):
            left = current[m - 1] if m > 1 else 2.0 * current[0]
            value = ratio * (left + padded[m + 1]) if m < k - 1 else ratio * left
            if m < k:
                value = value + twice * current[m]
            if m < k - 1:
                value = value - before[m]
            following.append(value)
        before, current = current, following
        rows.append(current)
    return rows


def cuts(total, sizes):
    edges = [0]
    for size in sizes:
        edges.append(edges[-1] + size)
    return [(i, j - i) for i, j in zip(edges, edges[1:])]


def chunk_sizes(depth):
    ends = [UNIT, UNIT, UNIT]
    units = (depth - sum(ends)) // UNIT - 1
    middle, odd = divmod(units, 2)
    first = depth - sum(ends) - UNIT * units
    return [first] + [2 * UNIT] * middle + [UNIT] * odd + ends


def groups_of(count, parts):
    edges = [count * i // parts for i in range(parts + 1)]
    return list(zip(edges, edges[1:]))


def kernel(
    devices, replicas, chunks, token_parts, weight_parts,
    tok, rt, wg, wu, out,
    T, RT, SEL, Y, X, W, AG, AU, H, HIN, CS, CN, SK, Q, F, B, CT, CE, LV,
    rt_sem, tok_sem, w_sem, sent_sem, x_recv, f_recv, e_recv,
    n_recv, q_recv, z_recv, c_recv, h_recv, l_recv, ready, go,
):
    groups = devices // HSPLIT
    half = devices // 2 * CAP
    width = W.shape[2]
    tiles = width // LANES
    rows = devices * CAP
    me = lax.axis_index("expert")
    z = lax.axis_index("replica")
    c = me % 2
    p = (me // 2) % 2
    a = me // HSPLIT
    partner = me + 1 - 2 * c
    lead = me + 1 - c
    last = len(chunks) - 1

    def pos(j):
        return (j % 2) * (devices // 2) + j // 2

    def other(dg, dp, dc):
        return HSPLIT * ((a + dg) % groups) + 2 * ((p + dp) % 2) + (c + dc) % 2

    combos = [(dg, dp) for dg in range(groups) for dp in range(2) if (dg, dp) != (0, 0)]
    combos = combos[::-1]
    alls = [
        (dg, dp, dc)
        for dg in range(groups) for dp in range(2) for dc in range(2)
        if (dg, dp, dc) != (0, 0, 0)
    ][::-1]
    peers = []
    for i in range(replicas - 1):
        up, down = i + (i >= z), replicas - 1 - i - (replicas - 1 - i <= z)
        peers.append(jnp.where(z < replicas // 2, down, up))

    def block(j):
        return pl.ds(pl.multiple_of(pos(j) * CAP, CAP), CAP)

    def columns(ch):
        return pl.ds(chunks[ch][0], chunks[ch][1])

    def span(first, end):
        return pl.ds(chunks[first][0], chunks[end - 1][0] + chunks[end - 1][1] - chunks[first][0])

    def remote(src, dst, send_sem, recv_sem, device):
        return pltpu.make_async_remote_copy(
            src_ref=src, dst_ref=dst, send_sem=send_sem, recv_sem=recv_sem,
            device_id=device, device_id_type=MESH)

    def settle(ref, sem):
        pltpu.make_async_copy(ref, ref, sem).wait()

    def load_tokens(i):
        part = span(*token_parts[i])
        return pltpu.make_async_copy(tok.at[:, part], T.at[:, part], tok_sem.at[i])

    def load_weights(i):
        part = span(*weight_parts[i])
        return [
            pltpu.make_async_copy(w.at[part], W.at[k, part], w_sem.at[i])
            for k, w in enumerate((wg, wu))
        ]

    load_routes = pltpu.make_async_copy(rt, RT, rt_sem)
    load_routes.start()
    load_tokens(0).start()

    barrier = pltpu.get_barrier_semaphore()
    for combo in alls:
        pl.semaphore_signal(barrier, inc=1, device_id=(other(*combo), z), device_id_type=MESH)

    @pl.when(me == 0)
    def _():
        for peer in peers:
            pl.semaphore_signal(barrier, inc=1, device_id=(me, peer), device_id_type=MESH)

    for i in range(1, len(token_parts)):
        load_tokens(i).start()

    load_routes.wait()
    routes = RT[...]
    count = routes.shape[1]
    t_from = lax.broadcasted_iota(jnp.int32, (count, count), 0)
    t_to = lax.broadcasted_iota(jnp.int32, (count, count), 1)
    earlier = jnp.where(t_from < t_to, 1.0, 0.0).astype(jnp.bfloat16)
    named = [
        jnp.sum(jnp.where(routes == (a + dg) % groups, 1.0, 0.0), axis=0, keepdims=True)
        for dg in range(groups)
    ]
    table = jnp.concatenate(
        [jnp.broadcast_to(n, (CAP, count)) for n in named], axis=0)
    before = jnp.dot(table.astype(jnp.bfloat16), earlier, preferred_element_type=jnp.float32)
    slot = (lax.broadcasted_iota(jnp.int32, (groups * CAP, count), 0) % CAP).astype(jnp.float32)
    picks = jnp.where(before == slot, table, 0.0)
    SEL[...] = picks.astype(jnp.bfloat16)

    def gather(ch):
        part = columns(ch)
        picked = jnp.dot(
            SEL[...], T[:, part], preferred_element_type=jnp.float32).astype(jnp.bfloat16)
        Y[:, part] = picked

        X[block(me), part] = picked[:CAP]

    def send_rows(ch, pairs):
        part = columns(ch)
        for dg, dp in pairs:
            remote(
                Y.at[pl.ds(dg * CAP, CAP), part], X.at[block(me), part],
                sent_sem, x_recv.at[ch], (other(dg, dp, 0), z)).start()

    def send_across(pairs):
        part = columns(last)

        @pl.when(c == 0)
        def _():
            for dg, dp in pairs:
                remote(
                    Y.at[pl.ds(dg * CAP, CAP), part], X.at[block(me), part],
                    sent_sem, e_recv, (other(dg, dp, 1), z)).start()

    load_tokens(0).wait()
    gather(0)
    for i in range(len(weight_parts)):
        for copy in load_weights(i):
            copy.start()
    pl.semaphore_wait(barrier, len(alls) + jnp.where(me == 0, len(peers), 0))
    send_rows(0, combos)

    filled = jnp.sum(picks, axis=1, keepdims=True)
    for dg in range(groups):
        total = jnp.sum(filled[dg * CAP:(dg + 1) * CAP], axis=0, keepdims=True)
        CS[dg] = jnp.broadcast_to(total, (8, LANES))
    CN[me] = CS[0]
    for dg, dp, dc in alls:
        remote(CS.at[dg], CN.at[me], sent_sem, n_recv, (other(dg, dp, dc), z)).start()

    for i, (first, end) in enumerate(token_parts):
        if i:
            load_tokens(i).wait()
        for ch in range(max(first, 1), end):
            gather(ch)
            if ch < last - 1:
                send_rows(ch, combos)
    far = [pair for pair in combos if 0 not in pair]
    near = [pair for pair in combos if 0 in pair]
    for pairs in (far, near):
        for ch in (last - 1, last):
            send_rows(ch, pairs)
        send_across(pairs)
    send_across([(0, 0)])

    @pl.when(me == 0)
    def _():
        for peer in peers:
            pl.semaphore_signal(ready, inc=1, device_id=(me, peer), device_id_type=MESH)

    own = pl.ds(pl.multiple_of(c * half, half), half)

    def receive(ch):
        settle(X.at[pl.ds(0, len(combos) * CAP), columns(ch)], x_recv.at[ch])

    def forward(ch):
        part = columns(ch)
        remote(
            X.at[own, part], X.at[own, part], sent_sem, f_recv.at[ch], (partner, z)).start()

    def collect(ch):
        receive(ch)
        forward(ch)

    def arrive(ch):
        part = columns(ch)
        if ch < last:
            settle(X.at[pl.ds(0, half), part], f_recv.at[ch])
        else:
            @pl.when(c == 0)
            def _():
                receive(ch)
                settle(X.at[pl.ds(0, half), part], f_recv.at[ch])

            @pl.when(c == 1)
            def _():
                settle(X.at[pl.ds(0, (len(combos) + 1) * CAP), part], e_recv)

        for i, (first, end) in enumerate(weight_parts):
            if first == ch:
                settle(W.at[:, span(first, end)], w_sem.at[i])

    def multiply(ch):
        arrive(ch)
        part = columns(ch)
        x = X[:, part]
        for k, A in enumerate((AG, AU)):
            product = jnp.dot(x, W[k, part, :], preferred_element_type=jnp.float32)
            A[...] = A[...] + product if ch else product

    def release():
        @pl.when(me == 0)
        def _():
            pl.semaphore_wait(ready, len(peers))
            for combo in alls:
                pl.semaphore_signal(go, inc=1, device_id=(other(*combo), z), device_id_type=MESH)

    def share_count():
        settle(CN.at[pl.ds(0, len(alls))], n_recv)
        total = functools.reduce(jnp.add, [CN[j] for j in range(devices)])
        CT[z] = total

        @pl.when(me != 0)
        def _():
            pl.semaphore_wait(go, 1)

        @pl.when(c == 1)
        def _():
            for peer in peers:
                remote(CT.at[z], CT.at[z], sent_sem, c_recv, (me, peer)).start()

    collect(0)
    steady = last - 4
    for ch in range(1, steady + 1):
        collect(ch)
        multiply(ch - 1)
        if ch == 2:
            release()
        if ch == steady:
            share_count()

    @pl.when(c == 0)
    def _():
        multiply(steady)
        for ch in range(steady + 1, last - 1):
            collect(ch)
            multiply(ch)
        collect(last - 1)

    @pl.when(c == 1)
    def _():
        collect(steady + 1)
        collect(steady + 2)
        multiply(steady)
        collect(last - 1)
        collect(last)
        for ch in range(steady + 1, last - 1):
            multiply(ch)

    arrive(last - 1)
    arrive(last)
    part = span(last - 1, last + 1)
    x = X[:, part]
    strip = min(2 * LANES, width)
    tops = []
    for n in range(0, width, strip):
        lanes = slice(n, n + strip)
        g, u = (
            A[:, lanes] + jnp.dot(x, W[k, part, lanes], preferred_element_type=jnp.float32)
            for k, A in enumerate((AG, AU)))
        h = g / (1.0 + jnp.exp(-g)) * u
        H[:, lanes] = h
        tops.append(jnp.max(jnp.abs(h), axis=0, keepdims=True))

    ceiling = jnp.concatenate(tops, axis=1) + EPSILON
    mine = c * replicas + z
    for l in range(tiles):
        CE[mine, l:l + 1, :] = ceiling[:, l * LANES:(l + 1) * LANES]

    def share(ref, send_sem, recv_sem, targets):
        for peer in targets:
            remote(ref, ref, send_sem, recv_sem, (lead, peer)).start()

    def share_here(ref, send_sem, recv_sem):
        @pl.when(c == 0)
        def _():
            remote(ref, ref, send_sem, recv_sem, (lead, z)).start()

    share(CE.at[mine], sent_sem, z_recv, peers)
    share_here(CE.at[mine], sent_sem, z_recv)
    scale = 2.0 / ceiling
    here = CT[z, 0:1, :]
    empty = float(rows) - here
    stretch = STEPS / jnp.maximum(here, 1.0)
    even = lax.broadcasted_iota(jnp.int32, (SKETCH * tiles, LANES), 0) % 2 == 0
    bounds = [SKETCH * tiles * 2 // 3 // 16 * 16, SKETCH * tiles]
    sent = 0

    for l in range(tiles):
        lanes = slice(l * LANES, (l + 1) * LANES)
        scale_l = scale[:, lanes]

        def sketch(i, sums):
            part = pl.ds(pl.multiple_of(i * BATCH, BATCH), BATCH)
            scaled = jnp.abs(H[part, lanes]) * scale_l - 1.0
            double = 2.0 * scaled
            previous, current = jnp.ones_like(scaled), scaled
            new = []
            for k in range(KMOM - 1):
                new.append(sums[k] + jnp.sum(current.reshape(BATCH // 8, 8, LANES), axis=0))
                previous, current = current, double * current - previous
            return tuple(new)

        zero = jnp.zeros((8, LANES), jnp.float32)
        sums = lax.fori_loop(0, rows // BATCH, sketch, (zero,) * (KMOM - 1), unroll=True)
        SK[l * SKETCH:l * SKETCH + 1, :] = jnp.zeros((1, LANES), jnp.float32)
        for k in range(1, KMOM):
            SK[l * SKETCH + k:l * SKETCH + k + 1, :] = jnp.sum(
                sums[k - 1], axis=0, keepdims=True)
        while bounds and bounds[0] <= (l + 1) * SKETCH:
            part = slice(sent, bounds[0])
            held = SK[part, :] + jnp.where(even[part], -empty, empty)
            code = jnp.minimum(jnp.maximum(held * stretch, -STEPS), STEPS)
            Q[mine, part, :] = jnp.floor(code + 0.5).astype(jnp.int32).astype(jnp.int16)
            share(Q.at[mine, part, :], sent_sem, q_recv, peers[:1])
            sent = bounds.pop(0)
    share(Q.at[mine], sent_sem, q_recv, peers[1:])
    share_here(Q.at[mine], sent_sem, q_recv)
    for dg, dp, dc in alls:
        j = other(dg, dp, dc)
        remote(H.at[block(j), :], HIN.at[me], sent_sem, h_recv, (j, z)).start()

    HIN[me] = H[block(me), :]
    def calibrate():
        settle(CT.at[pl.ds(0, len(peers))], c_recv)
        settle(CE.at[pl.ds(0, 2 * replicas - 1)], z_recv)
        local = [CE[i, 0:tiles, :] for i in range(2 * replicas)]
        common = [
            functools.reduce(jnp.maximum, local[k * replicas:(k + 1) * replicas])
            for k in range(2)
        ]
        ratio = jnp.concatenate(
            [value / common[i // replicas] for i, value in enumerate(local)], axis=0)
        here = [CT[r, 0:tiles, :] for r in range(replicas)]
        total = functools.reduce(jnp.add, here)
        part = jnp.concatenate([value / total for value in here] * 2, axis=0)

        def added(value):
            value = [value[i * tiles:(i + 1) * tiles] for i in range(2 * replicas)]
            return jnp.concatenate([
                functools.reduce(jnp.add, value[k * replicas:(k + 1) * replicas])
                for k in range(2)
            ], axis=0)

        scaled = part * (1.0 / STEPS)
        starts = []
        for k, row in enumerate(rebased(ratio)):
            starts.append(k * (k + 3) // 2)
            for m, value in enumerate(row):
                B[starts[k] + m] = value * (scaled if m else part)
        settle(Q.at[pl.ds(0, 2 * replicas - 1)], q_recv)
        for i in range(2 * replicas):
            F[i * SKETCH * tiles:(i + 1) * SKETCH * tiles, :] = (
                Q[i].astype(jnp.int32).astype(jnp.float32))
        codes = [
            F[pl.ds(k, 2 * replicas * tiles, stride=SKETCH), :] for k in range(1, KMOM)]
        level = clip_fraction([
            added(tree([B[starts[k]]] + [
                B[starts[k] + m + 1] * codes[m] for m in range(k + 1)]))
            for k in range(KMOM - 1)
        ])
        for k in range(2):
            LV[me - 1 + k] = jnp.concatenate(
                [common[k] * level[k * tiles:(k + 1) * tiles], 1.0 / common[k]], axis=0)
        pair = LV.at[pl.ds(me - 1, 2)]
        for dg, dp, dc in alls:
            remote(pair, pair, sent_sem, l_recv, (other(dg, dp, dc), z)).start()

    @pl.when(c == 1)
    def _():
        calibrate()

    settle(X.at[pl.ds(0, len(combos) * CAP), :], sent_sem)
    settle(X.at[pl.ds(0, half), span(0, last)], sent_sem)
    settle(CN.at[pl.ds(0, len(alls))], sent_sem)
    settle(Q.at[pl.ds(0, len(peers))], sent_sem)
    settle(CE.at[pl.ds(0, len(peers))], sent_sem)

    @pl.when(c == 0)
    def _():
        settle(X.at[pl.ds(0, (len(combos) + 1) * CAP), columns(last)], sent_sem)
        settle(Q.at[0], sent_sem)
        settle(CE.at[0], sent_sem)

    @pl.when(c == 1)
    def _():
        settle(X.at[pl.ds(0, half), columns(last)], sent_sem)
        settle(CT.at[pl.ds(0, len(peers))], sent_sem)
        settle(X.at[pl.ds(0, 2 * CAP), pl.ds(0, len(alls) * LANES)], sent_sem)

    settle(HIN.at[pl.ds(0, len(alls))], sent_sem)
    settle(HIN.at[pl.ds(0, len(alls))], h_recv)
    @pl.when(c == 0)
    def _():
        settle(LV.at[pl.ds(0, devices)], l_recv)

    @pl.when(c == 1)
    def _():
        settle(LV.at[pl.ds(0, devices - 2)], l_recv)

    def finish(i, _):
        for k in range(HSPLIT):
            e = i * HSPLIT + k
            for l in range(tiles):
                bound = LV[e, l:l + 1, :]
                factor = LV[e, tiles + l:tiles + l + 1, :]
                h = HIN[e, :, l * LANES:(l + 1) * LANES]
                h = jnp.minimum(jnp.maximum(h, -bound), bound) * factor
                lanes = pl.ds(pl.multiple_of(e * width + l * LANES, LANES), LANES)
                out[:, lanes] = h.astype(jnp.bfloat16)
        return 0

    lax.fori_loop(0, groups, finish, 0)


def shards(tokens, routes, gate_weight, up_weight):
    devices = lax.axis_size("expert")
    replicas = lax.axis_size("replica")
    groups = devices // HSPLIT
    count, depth = tokens.shape
    width = gate_weight.shape[1]
    chunks = cuts(depth, chunk_sizes(depth))
    token_parts = [(0, 1), (1, len(chunks))]
    weight_parts = groups_of(len(chunks), 3)
    rows = devices * CAP
    tiles = width // LANES
    bf16, f32 = jnp.bfloat16, jnp.float32
    dma = pltpu.SemaphoreType.DMA
    anywhere = pl.BlockSpec(memory_space=pl.ANY)
    return pl.pallas_call(
        functools.partial(kernel, devices, replicas, chunks, token_parts, weight_parts),
        out_shape=pltpu.VMEM((CAP, devices * width), bf16),
        in_specs=[anywhere] * 4,
        out_specs=pl.BlockSpec(memory_space=pltpu.VMEM),
        scratch_shapes=[
            pltpu.VMEM((count, depth), bf16),
            pltpu.VMEM((routes.shape[1], count), jnp.int32),
            pltpu.VMEM((groups * CAP, count), bf16),
            pltpu.VMEM((groups * CAP, depth), bf16),
            pltpu.VMEM((rows, depth), bf16),
            pltpu.VMEM((2, depth, width), bf16),
            pltpu.VMEM((rows, width), f32),
            pltpu.VMEM((rows, width), f32),
            pltpu.VMEM((rows, width), f32),
            pltpu.VMEM((devices, CAP, width), f32),
            pltpu.VMEM((groups, 8, LANES), f32),
            pltpu.VMEM((devices, 8, LANES), f32),
            pltpu.VMEM((SKETCH * tiles, LANES), f32),
            pltpu.VMEM((2 * replicas, SKETCH * tiles, LANES), jnp.int16),
            pltpu.VMEM((2 * replicas * SKETCH * tiles, LANES), f32),
            pltpu.VMEM(((KMOM - 1) * (KMOM + 2) // 2, 2 * replicas * tiles, LANES), f32),
            pltpu.VMEM((replicas, 8, LANES), f32),
            pltpu.VMEM((2 * replicas, 8, LANES), f32),
            pltpu.VMEM((devices, 2 * tiles, LANES), f32),
            dma(()), dma((len(token_parts),)), dma((len(weight_parts),)), dma(()),
            dma((len(chunks),)), dma((len(chunks),)), dma(()),
            dma(()), dma(()), dma(()), dma(()), dma(()), dma(()),
            pltpu.SemaphoreType.REGULAR, pltpu.SemaphoreType.REGULAR,
        ],
        compiler_params=pltpu.CompilerParams(
            collective_id=0, has_side_effects=True, vmem_limit_bytes=56 * 1024 * 1024),
    )(tokens, pltpu.with_memory_space_constraint(routes.T, pltpu.HBM), gate_weight, up_weight)


def solution(mesh):
    in_specs = (
        P(("expert", "replica"), None),
        P(("expert", "replica"), None),
        P(None, "expert"),
        P(None, "expert"),
    )
    out_specs = P(("expert", "replica"), None)
    return jax.shard_map(shards, mesh=mesh, in_specs=in_specs, out_specs=out_specs, check_vma=False)
```

```python
import functools
import math

import jax
import jax.numpy as jnp
from jax import lax
from jax.experimental import pallas as pl
from jax.experimental.pallas import tpu as pltpu
from jax.sharding import PartitionSpec as P

HSPLIT = 4
CAP = 16
KMOM = 12
QITERS = 4
LANES = 128
UNIT = 512
TAIL = 256
WIDEST = 2
ROWS = 32
BATCH = 64
SKETCH = 12
STEPS = 32767.0

QUANTILE_LEVEL = 0.99
EPSILON = 1e-06
MESH = pl.DeviceIdType.MESH

SIN_TERMS = [(-1.0) ** i / math.factorial(2 * i + 1) for i in range(7)]
COS_TERMS = [(-1.0) ** i / math.factorial(2 * i) for i in range(8)]


def polynomial(x, terms):
    terms = [jnp.full_like(x, term) for term in terms]
    while len(terms) > 1:
        pairs = [terms[i] + terms[i + 1] * x for i in range(0, len(terms) - 1, 2)]
        terms = pairs + terms[2 * len(pairs):]
        x = x * x
    return terms[0]


def sin_cos(half_turns):
    turns = jnp.floor(half_turns + 0.5)
    rest = (half_turns - turns) * math.pi
    sign = 1.0 - 2.0 * (turns - 2.0 * jnp.floor(turns * 0.5))
    square = rest * rest
    return sign * rest * polynomial(square, SIN_TERMS), sign * polynomial(square, COS_TERMS)


def tree(terms):
    while len(terms) > 1:
        terms = [functools.reduce(jnp.add, terms[i:i + 2]) for i in range(0, len(terms), 2)]
    return terms[0]


def clip_fraction(coefficient):
    start = 1.0 - QUANTILE_LEVEL
    total = jnp.zeros_like(coefficient[0])
    for k in range(1, KMOM, 2):
        total = total + coefficient[k - 1] * ((1.0 if k % 4 == 1 else -1.0) / k)
    angle = start - (2.0 / math.pi) * total
    for _ in range(QITERS - 1):
        sine, cosine = sin_cos(angle)
        double = 2.0 * cosine
        stride = double * double - 2.0
        waves = [-sine, jnp.zeros_like(sine), sine, double * sine]
        for k in range(3, KMOM):
            waves.append(stride * waves[k - 1] - waves[k - 3])
        angle = start - (2.0 / math.pi) * tree([
            coefficient[k - 1] * (waves[k + 1] * (1.0 / k)) for k in range(1, KMOM)])
    return 0.5 * (1.0 + sin_cos(angle)[1])


def rebased(ratio):
    shift = ratio - 1.0
    twice = 2.0 * shift
    zero = jnp.zeros_like(ratio)
    before, current = [jnp.ones_like(ratio)], [shift, ratio]
    rows = [current]
    for k in range(2, KMOM):
        padded = current + [zero, zero]
        following = [ratio * current[1] + twice * current[0] - before[0]]
        for m in range(1, k + 1):
            left = current[m - 1] if m > 1 else 2.0 * current[0]
            value = ratio * (left + padded[m + 1]) if m < k - 1 else ratio * left
            if m < k:
                value = value + twice * current[m]
            if m < k - 1:
                value = value - before[m]
            following.append(value)
        before, current = current, following
        rows.append(current)
    return rows


def cuts(total, sizes):
    edges = [0]
    for size in sizes:
        edges.append(edges[-1] + size)
    return [(i, j - i) for i, j in zip(edges, edges[1:])]


def chunk_sizes(depth):
    ends = [UNIT, UNIT, UNIT]
    units = (depth - sum(ends)) // UNIT - 1
    middle, odd = divmod(units, 2)
    first = depth - sum(ends) - UNIT * units
    return [first] + [2 * UNIT] * middle + [UNIT] * odd + ends


def groups_of(count, parts):
    edges = [count * i // parts for i in range(parts + 1)]
    return list(zip(edges, edges[1:]))


def kernel(
    devices, replicas, chunks, token_parts, weight_parts,
    tok, rt, wg, wu, out,
    T, RT, SEL, Y, X, W, AG, AU, H, HIN, CS, CN, SK, Q, F, B, CT, CE, LV,
    rt_sem, tok_sem, w_sem, sent_sem, x_recv, f_recv, e_recv,
    n_recv, q_recv, z_recv, c_recv, h_recv, l_recv, ready, go,
):
    groups = devices // HSPLIT
    half = devices // 2 * CAP
    width = W.shape[2]
    tiles = width // LANES
    rows = devices * CAP
    me = lax.axis_index("expert")
    z = lax.axis_index("replica")
    c = me % 2
    p = (me // 2) % 2
    a = me // HSPLIT
    partner = me + 1 - 2 * c
    lead = me + 1 - c
    last = len(chunks) - 1

    def pos(j):
        return (j % 2) * (devices // 2) + j // 2

    def other(dg, dp, dc):
        return HSPLIT * ((a + dg) % groups) + 2 * ((p + dp) % 2) + (c + dc) % 2

    combos = [(dg, dp) for dg in range(groups) for dp in range(2) if (dg, dp) != (0, 0)]
    combos = combos[::-1]
    alls = [
        (dg, dp, dc)
        for dg in range(groups) for dp in range(2) for dc in range(2)
        if (dg, dp, dc) != (0, 0, 0)
    ][::-1]
    peers = []
    for i in range(replicas - 1):
        up, down = i + (i >= z), replicas - 1 - i - (replicas - 1 - i <= z)
        peers.append(jnp.where(z < replicas // 2, down, up))

    def block(j):
        return pl.ds(pl.multiple_of(pos(j) * CAP, CAP), CAP)

    def columns(ch):
        return pl.ds(chunks[ch][0], chunks[ch][1])

    def span(first, end):
        return pl.ds(chunks[first][0], chunks[end - 1][0] + chunks[end - 1][1] - chunks[first][0])

    def remote(src, dst, send_sem, recv_sem, device):
        return pltpu.make_async_remote_copy(
            src_ref=src, dst_ref=dst, send_sem=send_sem, recv_sem=recv_sem,
            device_id=device, device_id_type=MESH)

    def settle(ref, sem):
        pltpu.make_async_copy(ref, ref, sem).wait()

    def load_tokens(i):
        part = span(*token_parts[i])
        return pltpu.make_async_copy(tok.at[:, part], T.at[:, part], tok_sem.at[i])

    def load_weights(i):
        part = span(*weight_parts[i])
        return [
            pltpu.make_async_copy(w.at[part], W.at[k, part], w_sem.at[i])
            for k, w in enumerate((wg, wu))
        ]

    load_routes = pltpu.make_async_copy(rt, RT, rt_sem)
    load_tokens(0).start()
    load_routes.start()

    barrier = pltpu.get_barrier_semaphore()
    for combo in alls:
        pl.semaphore_signal(barrier, inc=1, device_id=(other(*combo), z), device_id_type=MESH)

    @pl.when(me == 0)
    def _():
        for peer in peers:
            pl.semaphore_signal(barrier, inc=1, device_id=(me, peer), device_id_type=MESH)

    for i in range(1, len(token_parts)):
        load_tokens(i).start()

    load_routes.wait()
    routes = RT[...]
    count = routes.shape[1]
    t_from = lax.broadcasted_iota(jnp.int32, (count, count), 0)
    t_to = lax.broadcasted_iota(jnp.int32, (count, count), 1)
    earlier = jnp.where(t_from < t_to, 1.0, 0.0).astype(jnp.bfloat16)
    named = [
        jnp.sum(jnp.where(routes == (a + dg) % groups, 1.0, 0.0), axis=0, keepdims=True)
        for dg in range(groups)
    ]
    table = jnp.concatenate(
        [jnp.broadcast_to(n, (CAP, count)) for n in named], axis=0)
    before = jnp.dot(table.astype(jnp.bfloat16), earlier, preferred_element_type=jnp.float32)
    slot = (lax.broadcasted_iota(jnp.int32, (groups * CAP, count), 0) % CAP).astype(jnp.float32)
    picks = jnp.where(before == slot, table, 0.0)
    SEL[...] = picks.astype(jnp.bfloat16)

    def gather(ch):
        part = columns(ch)
        picked = jnp.dot(
            SEL[...], T[:, part], preferred_element_type=jnp.float32).astype(jnp.bfloat16)
        Y[:, part] = picked

        X[block(me), part] = picked[:CAP]

    def send_rows(ch, pairs):
        part = columns(ch)
        for dg, dp in pairs:
            remote(
                Y.at[pl.ds(dg * CAP, CAP), part], X.at[block(me), part],
                sent_sem, x_recv.at[ch], (other(dg, dp, 0), z)).start()

    def send_across(pairs):
        part = columns(last)

        @pl.when(c == 0)
        def _():
            for dg, dp in pairs:
                remote(
                    Y.at[pl.ds(dg * CAP, CAP), part], X.at[block(me), part],
                    sent_sem, e_recv, (other(dg, dp, 1), z)).start()

    load_tokens(0).wait()
    gather(0)
    for i in range(len(weight_parts)):
        for copy in load_weights(i):
            copy.start()
    pl.semaphore_wait(barrier, len(alls) + jnp.where(me == 0, len(peers), 0))
    send_rows(0, combos)

    filled = jnp.sum(picks, axis=1, keepdims=True)
    for dg in range(groups):
        total = jnp.sum(filled[dg * CAP:(dg + 1) * CAP], axis=0, keepdims=True)
        CS[dg] = jnp.broadcast_to(total, (8, LANES))
    CN[me] = CS[0]
    for dg, dp, dc in alls:
        remote(CS.at[dg], CN.at[me], sent_sem, n_recv, (other(dg, dp, dc), z)).start()

    for i, (first, end) in enumerate(token_parts):
        if i:
            load_tokens(i).wait()
        for ch in range(max(first, 1), end):
            gather(ch)
            if ch < last - 1:
                send_rows(ch, combos)
    far = [pair for pair in combos if 0 not in pair]
    near = [pair for pair in combos if 0 in pair]
    for pairs in (far, near):
        for ch in (last - 1, last):
            send_rows(ch, pairs)
        send_across(pairs)
    send_across([(0, 0)])

    @pl.when(me == 0)
    def _():
        for peer in peers:
            pl.semaphore_signal(ready, inc=1, device_id=(me, peer), device_id_type=MESH)

    own = pl.ds(pl.multiple_of(c * half, half), half)

    def receive(ch):
        settle(X.at[pl.ds(0, len(combos) * CAP), columns(ch)], x_recv.at[ch])

    def forward(ch):
        part = columns(ch)
        remote(
            X.at[own, part], X.at[own, part], sent_sem, f_recv.at[ch], (partner, z)).start()

    def collect(ch):
        receive(ch)
        forward(ch)

    def arrive(ch):
        part = columns(ch)
        if ch < last:
            settle(X.at[pl.ds(0, half), part], f_recv.at[ch])
        else:
            @pl.when(c == 0)
            def _():
                receive(ch)
                settle(X.at[pl.ds(0, half), part], f_recv.at[ch])

            @pl.when(c == 1)
            def _():
                settle(X.at[pl.ds(0, (len(combos) + 1) * CAP), part], e_recv)

        for i, (first, end) in enumerate(weight_parts):
            if first == ch:
                settle(W.at[:, span(first, end)], w_sem.at[i])

    def multiply(ch):
        arrive(ch)
        part = columns(ch)
        x = X[:, part]
        for k, A in enumerate((AG, AU)):
            product = jnp.dot(x, W[k, part, :], preferred_element_type=jnp.float32)
            A[...] = A[...] + product if ch else product

    def release():
        @pl.when(me == 0)
        def _():
            pl.semaphore_wait(ready, len(peers))
            for combo in alls:
                pl.semaphore_signal(go, inc=1, device_id=(other(*combo), z), device_id_type=MESH)

    def share_count():
        settle(CN.at[pl.ds(0, len(alls))], n_recv)
        total = functools.reduce(jnp.add, [CN[j] for j in range(devices)])
        CT[z] = total

        @pl.when(me != 0)
        def _():
            pl.semaphore_wait(go, 1)

        @pl.when(c == 1)
        def _():
            for peer in peers:
                remote(CT.at[z], CT.at[z], sent_sem, c_recv, (me, peer)).start()

    collect(0)
    steady = last - 4
    for ch in range(1, steady + 1):
        collect(ch)
        multiply(ch - 1)
        if ch == 2:
            release()
        if ch == steady:
            share_count()

    @pl.when(c == 0)
    def _():
        multiply(steady)
        for ch in range(steady + 1, last - 1):
            collect(ch)
            multiply(ch)
        collect(last - 1)

    @pl.when(c == 1)
    def _():
        collect(steady + 1)
        collect(steady + 2)
        multiply(steady)
        collect(last - 1)
        collect(last)
        for ch in range(steady + 1, last - 1):
            multiply(ch)

    arrive(last - 1)
    arrive(last)
    part = span(last - 1, last + 1)
    x = X[:, part]
    strip = min(2 * LANES, width)
    tops = []
    for n in range(0, width, strip):
        lanes = slice(n, n + strip)
        g, u = (
            A[:, lanes] + jnp.dot(x, W[k, part, lanes], preferred_element_type=jnp.float32)
            for k, A in enumerate((AG, AU)))
        h = g / (1.0 + jnp.exp(-g)) * u
        H[:, lanes] = h
        tops.append(jnp.max(jnp.abs(h), axis=0, keepdims=True))

    ceiling = jnp.concatenate(tops, axis=1) + EPSILON
    mine = c * replicas + z
    for l in range(tiles):
        CE[mine, l:l + 1, :] = ceiling[:, l * LANES:(l + 1) * LANES]

    def share(ref, send_sem, recv_sem, targets):
        for peer in targets:
            remote(ref, ref, send_sem, recv_sem, (lead, peer)).start()

    def share_here(ref, send_sem, recv_sem):
        @pl.when(c == 0)
        def _():
            remote(ref, ref, send_sem, recv_sem, (lead, z)).start()

    share(CE.at[mine], sent_sem, z_recv, peers)
    share_here(CE.at[mine], sent_sem, z_recv)
    scale = 2.0 / ceiling
    here = CT[z, 0:1, :]
    empty = float(rows) - here
    stretch = STEPS / jnp.maximum(here, 1.0)
    even = lax.broadcasted_iota(jnp.int32, (SKETCH * tiles, LANES), 0) % 2 == 0
    bounds = [SKETCH * tiles * 2 // 3 // 16 * 16, SKETCH * tiles]
    sent = 0

    for l in range(tiles):
        lanes = slice(l * LANES, (l + 1) * LANES)
        scale_l = scale[:, lanes]

        def sketch(i, sums):
            part = pl.ds(pl.multiple_of(i * BATCH, BATCH), BATCH)
            scaled = jnp.abs(H[part, lanes]) * scale_l - 1.0
            double = 2.0 * scaled
            previous, current = jnp.ones_like(scaled), scaled
            waves = []
            for _ in range(KMOM // 2):
                waves.append(current)
                previous, current = current, double * current - previous
            waves += [wave * waves[-1] for wave in waves[:-1]]
            return tuple(
                total + jnp.sum(wave.reshape(BATCH // 8, 8, LANES), axis=0)
                for total, wave in zip(sums, waves))

        zero = jnp.zeros((8, LANES), jnp.float32)
        sums = lax.fori_loop(0, rows // BATCH, sketch, (zero,) * (KMOM - 1), unroll=True)
        SK[l * SKETCH:l * SKETCH + 1, :] = jnp.zeros((1, LANES), jnp.float32)
        half_order = KMOM // 2
        found = [jnp.sum(value, axis=0, keepdims=True) for value in sums]
        for k in range(half_order + 1, KMOM):
            found[k - 1] = 2.0 * found[k - 1] - found[2 * half_order - k - 1]
        for k in range(1, KMOM):
            SK[l * SKETCH + k:l * SKETCH + k + 1, :] = found[k - 1]
        while bounds and bounds[0] <= (l + 1) * SKETCH:
            part = slice(sent, bounds[0])
            held = SK[part, :] + jnp.where(even[part], -empty, empty)
            code = jnp.minimum(jnp.maximum(held * stretch, -STEPS), STEPS)
            Q[mine, part, :] = jnp.floor(code + 0.5).astype(jnp.int32).astype(jnp.int16)
            share(Q.at[mine, part, :], sent_sem, q_recv, peers[:1])
            sent = bounds.pop(0)
    share(Q.at[mine], sent_sem, q_recv, peers[1:])
    share_here(Q.at[mine], sent_sem, q_recv)
    for dg, dp, dc in alls:
        j = other(dg, dp, dc)
        remote(H.at[block(j), :], HIN.at[me], sent_sem, h_recv, (j, z)).start()

    HIN[me] = H[block(me), :]
    def calibrate():
        settle(CT.at[pl.ds(0, len(peers))], c_recv)
        settle(CE.at[pl.ds(0, 2 * replicas - 1)], z_recv)
        local = [CE[i, 0:tiles, :] for i in range(2 * replicas)]
        common = [
            functools.reduce(jnp.maximum, local[k * replicas:(k + 1) * replicas])
            for k in range(2)
        ]
        ratio = jnp.concatenate(
            [value / common[i // replicas] for i, value in enumerate(local)], axis=0)
        here = [CT[r, 0:tiles, :] for r in range(replicas)]
        total = functools.reduce(jnp.add, here)
        part = jnp.concatenate([value / total for value in here] * 2, axis=0)

        def added(value):
            value = [value[i * tiles:(i + 1) * tiles] for i in range(2 * replicas)]
            return jnp.concatenate([
                functools.reduce(jnp.add, value[k * replicas:(k + 1) * replicas])
                for k in range(2)
            ], axis=0)

        scaled = part * (1.0 / STEPS)
        starts = []
        for k, row in enumerate(rebased(ratio)):
            starts.append(k * (k + 3) // 2)
            for m, value in enumerate(row):
                B[starts[k] + m] = value * (scaled if m else part)
        settle(Q.at[pl.ds(0, 2 * replicas - 1)], q_recv)
        for i in range(2 * replicas):
            F[i * SKETCH * tiles:(i + 1) * SKETCH * tiles, :] = (
                Q[i].astype(jnp.int32).astype(jnp.float32))
        codes = [
            F[pl.ds(k, 2 * replicas * tiles, stride=SKETCH), :] for k in range(1, KMOM)]
        level = clip_fraction([
            added(tree([B[starts[k]]] + [
                B[starts[k] + m + 1] * codes[m] for m in range(k + 1)]))
            for k in range(KMOM - 1)
        ])
        for k in range(2):
            LV[me - 1 + k] = jnp.concatenate(
                [common[k] * level[k * tiles:(k + 1) * tiles], 1.0 / common[k]], axis=0)
        pair = LV.at[pl.ds(me - 1, 2)]
        for dg, dp, dc in alls:
            remote(pair, pair, sent_sem, l_recv, (other(dg, dp, dc), z)).start()

    @pl.when(c == 1)
    def _():
        calibrate()

    settle(X.at[pl.ds(0, len(combos) * CAP), :], sent_sem)
    settle(X.at[pl.ds(0, half), span(0, last)], sent_sem)
    settle(CN.at[pl.ds(0, len(alls))], sent_sem)
    settle(Q.at[pl.ds(0, len(peers))], sent_sem)
    settle(CE.at[pl.ds(0, len(peers))], sent_sem)

    @pl.when(c == 0)
    def _():
        settle(X.at[pl.ds(0, (len(combos) + 1) * CAP), columns(last)], sent_sem)
        settle(Q.at[0], sent_sem)
        settle(CE.at[0], sent_sem)

    @pl.when(c == 1)
    def _():
        settle(X.at[pl.ds(0, half), columns(last)], sent_sem)
        settle(CT.at[pl.ds(0, len(peers))], sent_sem)
        settle(X.at[pl.ds(0, 2 * CAP), pl.ds(0, len(alls) * LANES)], sent_sem)

    settle(HIN.at[pl.ds(0, len(alls))], sent_sem)
    settle(HIN.at[pl.ds(0, len(alls))], h_recv)
    @pl.when(c == 0)
    def _():
        settle(LV.at[pl.ds(0, devices)], l_recv)

    @pl.when(c == 1)
    def _():
        settle(LV.at[pl.ds(0, devices - 2)], l_recv)

    def finish(i, _):
        for k in range(HSPLIT):
            e = i * HSPLIT + k
            for l in range(tiles):
                bound = LV[e, l:l + 1, :]
                factor = LV[e, tiles + l:tiles + l + 1, :]
                h = HIN[e, :, l * LANES:(l + 1) * LANES]
                h = jnp.minimum(jnp.maximum(h, -bound), bound) * factor
                lanes = pl.ds(pl.multiple_of(e * width + l * LANES, LANES), LANES)
                out[:, lanes] = h.astype(jnp.bfloat16)
        return 0

    lax.fori_loop(0, groups, finish, 0)


def shards(tokens, routes, gate_weight, up_weight):
    devices = lax.axis_size("expert")
    replicas = lax.axis_size("replica")
    groups = devices // HSPLIT
    count, depth = tokens.shape
    width = gate_weight.shape[1]
    chunks = cuts(depth, chunk_sizes(depth))
    token_parts = [(0, 1), (1, len(chunks))]
    weight_parts = groups_of(len(chunks), 3)
    rows = devices * CAP
    tiles = width // LANES
    bf16, f32 = jnp.bfloat16, jnp.float32
    dma = pltpu.SemaphoreType.DMA
    anywhere = pl.BlockSpec(memory_space=pl.ANY)
    return pl.pallas_call(
        functools.partial(kernel, devices, replicas, chunks, token_parts, weight_parts),
        out_shape=pltpu.VMEM((CAP, devices * width), bf16),
        in_specs=[anywhere] * 4,
        out_specs=pl.BlockSpec(memory_space=pltpu.VMEM),
        scratch_shapes=[
            pltpu.VMEM((count, depth), bf16),
            pltpu.VMEM((routes.shape[1], count), jnp.int32),
            pltpu.VMEM((groups * CAP, count), bf16),
            pltpu.VMEM((groups * CAP, depth), bf16),
            pltpu.VMEM((rows, depth), bf16),
            pltpu.VMEM((2, depth, width), bf16),
            pltpu.VMEM((rows, width), f32),
            pltpu.VMEM((rows, width), f32),
            pltpu.VMEM((rows, width), f32),
            pltpu.VMEM((devices, CAP, width), f32),
            pltpu.VMEM((groups, 8, LANES), f32),
            pltpu.VMEM((devices, 8, LANES), f32),
            pltpu.VMEM((SKETCH * tiles, LANES), f32),
            pltpu.VMEM((2 * replicas, SKETCH * tiles, LANES), jnp.int16),
            pltpu.VMEM((2 * replicas * SKETCH * tiles, LANES), f32),
            pltpu.VMEM(((KMOM - 1) * (KMOM + 2) // 2, 2 * replicas * tiles, LANES), f32),
            pltpu.VMEM((replicas, 8, LANES), f32),
            pltpu.VMEM((2 * replicas, 8, LANES), f32),
            pltpu.VMEM((devices, 2 * tiles, LANES), f32),
            dma(()), dma((len(token_parts),)), dma((len(weight_parts),)), dma(()),
            dma((len(chunks),)), dma((len(chunks),)), dma(()),
            dma(()), dma(()), dma(()), dma(()), dma(()), dma(()),
            pltpu.SemaphoreType.REGULAR, pltpu.SemaphoreType.REGULAR,
        ],
        compiler_params=pltpu.CompilerParams(
            collective_id=0, has_side_effects=True, vmem_limit_bytes=56 * 1024 * 1024),
    )(tokens, pltpu.with_memory_space_constraint(routes.T, pltpu.HBM), gate_weight, up_weight)


def solution(mesh):
    in_specs = (
        P(("expert", "replica"), None),
        P(("expert", "replica"), None),
        P(None, "expert"),
        P(None, "expert"),
    )
    out_specs = P(("expert", "replica"), None)
    return jax.shard_map(shards, mesh=mesh, in_specs=in_specs, out_specs=out_specs, check_vma=False)
```

```python
import functools
import math

import jax
import jax.numpy as jnp
from jax import lax
from jax.experimental import pallas as pl
from jax.experimental.pallas import tpu as pltpu
from jax.sharding import PartitionSpec as P

HSPLIT = 4
CAP = 16
KMOM = 12
QITERS = 4
LANES = 128
UNIT = 512
TAIL = 256
WIDEST = 2
ROWS = 32
BATCH = 64
SKETCH = 12
STEPS = 32767.0

QUANTILE_LEVEL = 0.99
EPSILON = 1e-06
MESH = pl.DeviceIdType.MESH

SIN_TERMS = [(-1.0) ** i / math.factorial(2 * i + 1) for i in range(7)]
COS_TERMS = [(-1.0) ** i / math.factorial(2 * i) for i in range(8)]


def polynomial(x, terms):
    terms = [jnp.full_like(x, term) for term in terms]
    while len(terms) > 1:
        pairs = [terms[i] + terms[i + 1] * x for i in range(0, len(terms) - 1, 2)]
        terms = pairs + terms[2 * len(pairs):]
        x = x * x
    return terms[0]


def sin_cos(half_turns):
    turns = jnp.floor(half_turns + 0.5)
    rest = (half_turns - turns) * math.pi
    sign = 1.0 - 2.0 * (turns - 2.0 * jnp.floor(turns * 0.5))
    square = rest * rest
    return sign * rest * polynomial(square, SIN_TERMS), sign * polynomial(square, COS_TERMS)


def tree(terms):
    while len(terms) > 1:
        terms = [functools.reduce(jnp.add, terms[i:i + 2]) for i in range(0, len(terms), 2)]
    return terms[0]


def clip_fraction(coefficient):
    start = 1.0 - QUANTILE_LEVEL
    total = jnp.zeros_like(coefficient[0])
    for k in range(1, KMOM, 2):
        total = total + coefficient[k - 1] * ((1.0 if k % 4 == 1 else -1.0) / k)
    angle = start - (2.0 / math.pi) * total
    for _ in range(QITERS - 1):
        sine, cosine = sin_cos(angle)
        double = 2.0 * cosine
        stride = double * double - 2.0
        waves = [-sine, jnp.zeros_like(sine), sine, double * sine]
        for k in range(3, KMOM):
            waves.append(stride * waves[k - 1] - waves[k - 3])
        angle = start - (2.0 / math.pi) * tree([
            coefficient[k - 1] * (waves[k + 1] * (1.0 / k)) for k in range(1, KMOM)])
    return 0.5 * (1.0 + sin_cos(angle)[1])


def rebased(ratio):
    shift = ratio - 1.0
    twice = 2.0 * shift
    zero = jnp.zeros_like(ratio)
    before, current = [jnp.ones_like(ratio)], [shift, ratio]
    rows = [current]
    for k in range(2, KMOM):
        padded = current + [zero, zero]
        following = [ratio * current[1] + twice * current[0] - before[0]]
        for m in range(1, k + 1):
            left = current[m - 1] if m > 1 else 2.0 * current[0]
            value = ratio * (left + padded[m + 1]) if m < k - 1 else ratio * left
            if m < k:
                value = value + twice * current[m]
            if m < k - 1:
                value = value - before[m]
            following.append(value)
        before, current = current, following
        rows.append(current)
    return rows


def cuts(total, sizes):
    edges = [0]
    for size in sizes:
        edges.append(edges[-1] + size)
    return [(i, j - i) for i, j in zip(edges, edges[1:])]


def chunk_sizes(depth):
    ends = [UNIT, UNIT, UNIT]
    units = (depth - sum(ends)) // UNIT - 1
    middle, odd = divmod(units, 2)
    first = depth - sum(ends) - UNIT * units
    return [first] + [2 * UNIT] * middle + [UNIT] * odd + ends


def groups_of(count, parts):
    edges = [count * i // parts for i in range(parts + 1)]
    return list(zip(edges, edges[1:]))


def kernel(
    devices, replicas, chunks, token_parts, weight_parts,
    tok, rt, wg, wu, out,
    T, RT, SEL, Y, X, W, AG, AU, H, HIN, CS, CN, SK, Q, F, B, CT, CE, LV,
    rt_sem, tok_sem, w_sem, sent_sem, x_recv, f_recv, e_recv,
    n_recv, q_recv, z_recv, h_recv, l_recv, ready, go,
):
    groups = devices // HSPLIT
    half = devices // 2 * CAP
    width = W.shape[2]
    tiles = width // LANES
    rows = devices * CAP
    me = lax.axis_index("expert")
    z = lax.axis_index("replica")
    c = me % 2
    p = (me // 2) % 2
    a = me // HSPLIT
    partner = me + 1 - 2 * c
    lead = me + 1 - c
    last = len(chunks) - 1

    def pos(j):
        return (j % 2) * (devices // 2) + j // 2

    def other(dg, dp, dc):
        return HSPLIT * ((a + dg) % groups) + 2 * ((p + dp) % 2) + (c + dc) % 2

    combos = [(dg, dp) for dg in range(groups) for dp in range(2) if (dg, dp) != (0, 0)]
    combos = combos[::-1]
    alls = [
        (dg, dp, dc)
        for dg in range(groups) for dp in range(2) for dc in range(2)
        if (dg, dp, dc) != (0, 0, 0)
    ][::-1]
    peers = []
    for i in range(replicas - 1):
        up, down = i + (i >= z), replicas - 1 - i - (replicas - 1 - i <= z)
        peers.append(jnp.where(z < replicas // 2, down, up))

    def block(j):
        return pl.ds(pl.multiple_of(pos(j) * CAP, CAP), CAP)

    def columns(ch):
        return pl.ds(chunks[ch][0], chunks[ch][1])

    def span(first, end):
        return pl.ds(chunks[first][0], chunks[end - 1][0] + chunks[end - 1][1] - chunks[first][0])

    def remote(src, dst, send_sem, recv_sem, device):
        return pltpu.make_async_remote_copy(
            src_ref=src, dst_ref=dst, send_sem=send_sem, recv_sem=recv_sem,
            device_id=device, device_id_type=MESH)

    def settle(ref, sem):
        pltpu.make_async_copy(ref, ref, sem).wait()

    def load_tokens(i):
        part = span(*token_parts[i])
        return pltpu.make_async_copy(tok.at[:, part], T.at[:, part], tok_sem.at[i])

    def load_weights(i):
        part = span(*weight_parts[i])
        return [
            pltpu.make_async_copy(w.at[part], W.at[k, part], w_sem.at[i])
            for k, w in enumerate((wg, wu))
        ]

    load_routes = pltpu.make_async_copy(rt, RT, rt_sem)
    load_tokens(0).start()
    load_routes.start()

    barrier = pltpu.get_barrier_semaphore()
    for combo in alls:
        pl.semaphore_signal(barrier, inc=1, device_id=(other(*combo), z), device_id_type=MESH)

    @pl.when(me == 0)
    def _():
        for peer in peers:
            pl.semaphore_signal(barrier, inc=1, device_id=(me, peer), device_id_type=MESH)

    for i in range(1, len(token_parts)):
        load_tokens(i).start()

    load_routes.wait()
    routes = RT[...]
    count = routes.shape[1]
    t_from = lax.broadcasted_iota(jnp.int32, (count, count), 0)
    t_to = lax.broadcasted_iota(jnp.int32, (count, count), 1)
    earlier = jnp.where(t_from < t_to, 1.0, 0.0).astype(jnp.bfloat16)
    named = [
        jnp.sum(jnp.where(routes == (a + dg) % groups, 1.0, 0.0), axis=0, keepdims=True)
        for dg in range(groups)
    ]
    table = jnp.concatenate(
        [jnp.broadcast_to(n, (CAP, count)) for n in named], axis=0)
    before = jnp.dot(table.astype(jnp.bfloat16), earlier, preferred_element_type=jnp.float32)
    slot = (lax.broadcasted_iota(jnp.int32, (groups * CAP, count), 0) % CAP).astype(jnp.float32)
    picks = jnp.where(before == slot, table, 0.0)
    SEL[...] = picks.astype(jnp.bfloat16)

    def gather(ch):
        part = columns(ch)
        picked = jnp.dot(
            SEL[...], T[:, part], preferred_element_type=jnp.float32).astype(jnp.bfloat16)
        Y[:, part] = picked

        X[block(me), part] = picked[:CAP]

    def send_rows(ch, pairs):
        part = columns(ch)
        for dg, dp in pairs:
            remote(
                Y.at[pl.ds(dg * CAP, CAP), part], X.at[block(me), part],
                sent_sem, x_recv.at[ch], (other(dg, dp, 0), z)).start()

    def send_across(pairs):
        part = columns(last)

        @pl.when(c == 0)
        def _():
            for dg, dp in pairs:
                remote(
                    Y.at[pl.ds(dg * CAP, CAP), part], X.at[block(me), part],
                    sent_sem, e_recv, (other(dg, dp, 1), z)).start()

    load_tokens(0).wait()
    gather(0)
    for i in range(len(weight_parts)):
        for copy in load_weights(i):
            copy.start()
    pl.semaphore_wait(barrier, len(alls) + jnp.where(me == 0, len(peers), 0))
    send_rows(0, combos)

    filled = jnp.sum(picks, axis=1, keepdims=True)
    for dg in range(groups):
        total = jnp.sum(filled[dg * CAP:(dg + 1) * CAP], axis=0, keepdims=True)
        CS[dg] = jnp.broadcast_to(total, (8, LANES))
    CN[me] = CS[0]
    for dg, dp, dc in alls:
        remote(CS.at[dg], CN.at[me], sent_sem, n_recv, (other(dg, dp, dc), z)).start()

    for i, (first, end) in enumerate(token_parts):
        if i:
            load_tokens(i).wait()
        for ch in range(max(first, 1), end):
            gather(ch)
            if ch < last - 1:
                send_rows(ch, combos)
    far = [pair for pair in combos if 0 not in pair]
    near = [pair for pair in combos if 0 in pair]
    for pairs in (far, near):
        for ch in (last - 1, last):
            send_rows(ch, pairs)
        send_across(pairs)
    send_across([(0, 0)])

    @pl.when(me == 0)
    def _():
        for peer in peers:
            pl.semaphore_signal(ready, inc=1, device_id=(me, peer), device_id_type=MESH)

    own = pl.ds(pl.multiple_of(c * half, half), half)

    def receive(ch):
        settle(X.at[pl.ds(0, len(combos) * CAP), columns(ch)], x_recv.at[ch])

    def forward(ch):
        part = columns(ch)
        remote(
            X.at[own, part], X.at[own, part], sent_sem, f_recv.at[ch], (partner, z)).start()

    def collect(ch):
        receive(ch)
        forward(ch)

    def arrive(ch):
        part = columns(ch)
        if ch < last:
            settle(X.at[pl.ds(0, half), part], f_recv.at[ch])
        else:
            @pl.when(c == 0)
            def _():
                receive(ch)
                settle(X.at[pl.ds(0, half), part], f_recv.at[ch])

            @pl.when(c == 1)
            def _():
                settle(X.at[pl.ds(0, (len(combos) + 1) * CAP), part], e_recv)

        for i, (first, end) in enumerate(weight_parts):
            if first == ch:
                settle(W.at[:, span(first, end)], w_sem.at[i])

    def multiply(ch):
        arrive(ch)
        part = columns(ch)
        x = X[:, part]
        for k, A in enumerate((AG, AU)):
            product = jnp.dot(x, W[k, part, :], preferred_element_type=jnp.float32)
            A[...] = A[...] + product if ch else product

    def release():
        @pl.when(me == 0)
        def _():
            pl.semaphore_wait(ready, len(peers))
            for combo in alls:
                pl.semaphore_signal(go, inc=1, device_id=(other(*combo), z), device_id_type=MESH)

    def share_count():
        settle(CN.at[pl.ds(0, len(alls))], n_recv)
        total = functools.reduce(jnp.add, [CN[j] for j in range(devices)])
        CT[z] = total

        @pl.when(me != 0)
        def _():
            pl.semaphore_wait(go, 1)

        @pl.when(c == 1)
        def _():
            for peer in peers:
                remote(CT.at[z], CT.at[z], sent_sem, z_recv, (me, peer)).start()

    collect(0)
    steady = last - 4
    for ch in range(1, steady + 1):
        collect(ch)
        multiply(ch - 1)
        if ch == 2:
            release()
        if ch == steady:
            share_count()

    @pl.when(c == 0)
    def _():
        multiply(steady)
        for ch in range(steady + 1, last - 1):
            collect(ch)
            multiply(ch)
        collect(last - 1)

    @pl.when(c == 1)
    def _():
        collect(steady + 1)
        collect(steady + 2)
        multiply(steady)
        collect(last - 1)
        collect(last)
        for ch in range(steady + 1, last - 1):
            multiply(ch)

    arrive(last - 1)
    arrive(last)
    part = span(last - 1, last + 1)
    x = X[:, part]
    strip = min(2 * LANES, width)
    tops = []
    for n in range(0, width, strip):
        lanes = slice(n, n + strip)
        g, u = (
            A[:, lanes] + jnp.dot(x, W[k, part, lanes], preferred_element_type=jnp.float32)
            for k, A in enumerate((AG, AU)))
        h = g / (1.0 + jnp.exp(-g)) * u
        H[:, lanes] = h
        tops.append(jnp.max(jnp.abs(h), axis=0, keepdims=True))

    ceiling = jnp.concatenate(tops, axis=1) + EPSILON
    mine = c * replicas + z
    for l in range(tiles):
        CE[mine, l:l + 1, :] = ceiling[:, l * LANES:(l + 1) * LANES]

    def share(ref, send_sem, recv_sem, targets):
        for peer in targets:
            remote(ref, ref, send_sem, recv_sem, (lead, peer)).start()

    def share_here(ref, send_sem, recv_sem):
        @pl.when(c == 0)
        def _():
            remote(ref, ref, send_sem, recv_sem, (lead, z)).start()

    share(CE.at[mine], sent_sem, z_recv, peers)
    share_here(CE.at[mine], sent_sem, z_recv)
    scale = 2.0 / ceiling
    here = CT[z, 0:1, :]
    empty = float(rows) - here
    stretch = STEPS / jnp.maximum(here, 1.0)
    even = lax.broadcasted_iota(jnp.int32, (SKETCH * tiles, LANES), 0) % 2 == 0
    bounds = [SKETCH * tiles * 2 // 3 // 16 * 16, SKETCH * tiles]
    sent = 0

    for l in range(tiles):
        lanes = slice(l * LANES, (l + 1) * LANES)
        scale_l = scale[:, lanes]

        def sketch(i, sums):
            part = pl.ds(pl.multiple_of(i * BATCH, BATCH), BATCH)
            scaled = jnp.abs(H[part, lanes]) * scale_l - 1.0
            double = 2.0 * scaled
            previous, current = jnp.ones_like(scaled), scaled
            waves = []
            for _ in range(KMOM // 2):
                waves.append(current)
                previous, current = current, double * current - previous
            waves += [wave * waves[-1] for wave in waves[:-1]]
            return tuple(
                total + jnp.sum(wave.reshape(BATCH // 8, 8, LANES), axis=0)
                for total, wave in zip(sums, waves))

        zero = jnp.zeros((8, LANES), jnp.float32)
        sums = lax.fori_loop(0, rows // BATCH, sketch, (zero,) * (KMOM - 1), unroll=True)
        SK[l * SKETCH:l * SKETCH + 1, :] = jnp.zeros((1, LANES), jnp.float32)
        half_order = KMOM // 2
        found = [jnp.sum(value, axis=0, keepdims=True) for value in sums]
        for k in range(half_order + 1, KMOM):
            found[k - 1] = 2.0 * found[k - 1] - found[2 * half_order - k - 1]
        for k in range(1, KMOM):
            SK[l * SKETCH + k:l * SKETCH + k + 1, :] = found[k - 1]
        while bounds and bounds[0] <= (l + 1) * SKETCH:
            part = slice(sent, bounds[0])
            held = SK[part, :] + jnp.where(even[part], -empty, empty)
            code = jnp.minimum(jnp.maximum(held * stretch, -STEPS), STEPS)
            Q[mine, part, :] = jnp.floor(code + 0.5).astype(jnp.int32).astype(jnp.int16)
            share(Q.at[mine, part, :], sent_sem, q_recv, peers[:1])
            sent = bounds.pop(0)
    share(Q.at[mine], sent_sem, q_recv, peers[1:])
    share_here(Q.at[mine], sent_sem, q_recv)
    for dg, dp, dc in alls:
        j = other(dg, dp, dc)
        remote(H.at[block(j), :], HIN.at[me], sent_sem, h_recv, (j, z)).start()

    HIN[me] = H[block(me), :]
    def calibrate():
        settle(F.at[pl.ds(0, 8 * (len(peers) + 2 * replicas - 1)), :], z_recv)
        local = [CE[i, 0:tiles, :] for i in range(2 * replicas)]
        common = [
            functools.reduce(jnp.maximum, local[k * replicas:(k + 1) * replicas])
            for k in range(2)
        ]
        ratio = jnp.concatenate(
            [value / common[i // replicas] for i, value in enumerate(local)], axis=0)
        here = [CT[r, 0:tiles, :] for r in range(replicas)]
        total = functools.reduce(jnp.add, here)
        part = jnp.concatenate([value / total for value in here] * 2, axis=0)

        def added(value):
            value = [value[i * tiles:(i + 1) * tiles] for i in range(2 * replicas)]
            return jnp.concatenate([
                functools.reduce(jnp.add, value[k * replicas:(k + 1) * replicas])
                for k in range(2)
            ], axis=0)

        scaled = part * (1.0 / STEPS)
        starts = []
        for k, row in enumerate(rebased(ratio)):
            starts.append(k * (k + 3) // 2)
            for m, value in enumerate(row):
                B[starts[k] + m] = value * (scaled if m else part)
        settle(Q.at[pl.ds(0, 2 * replicas - 1)], q_recv)
        for i in range(2 * replicas):
            F[i * SKETCH * tiles:(i + 1) * SKETCH * tiles, :] = (
                Q[i].astype(jnp.int32).astype(jnp.float32))
        codes = [
            F[pl.ds(k, 2 * replicas * tiles, stride=SKETCH), :] for k in range(1, KMOM)]
        level = clip_fraction([
            added(tree([B[starts[k]]] + [
                B[starts[k] + m + 1] * codes[m] for m in range(k + 1)]))
            for k in range(KMOM - 1)
        ])
        for k in range(2):
            LV[me - 1 + k] = jnp.concatenate(
                [common[k] * level[k * tiles:(k + 1) * tiles], 1.0 / common[k]], axis=0)
        pair = LV.at[pl.ds(me - 1, 2)]
        for dg, dp, dc in alls:
            remote(pair, pair, sent_sem, l_recv, (other(dg, dp, dc), z)).start()

    @pl.when(c == 1)
    def _():
        calibrate()

    settle(X.at[pl.ds(0, len(combos) * CAP), :], sent_sem)
    settle(X.at[pl.ds(0, half), span(0, last)], sent_sem)
    settle(CN.at[pl.ds(0, len(alls))], sent_sem)
    settle(Q.at[pl.ds(0, len(peers))], sent_sem)
    settle(CE.at[pl.ds(0, len(peers))], sent_sem)

    @pl.when(c == 0)
    def _():
        settle(X.at[pl.ds(0, (len(combos) + 1) * CAP), columns(last)], sent_sem)
        settle(Q.at[0], sent_sem)
        settle(CE.at[0], sent_sem)

    @pl.when(c == 1)
    def _():
        settle(X.at[pl.ds(0, half), columns(last)], sent_sem)
        settle(CT.at[pl.ds(0, len(peers))], sent_sem)
        settle(X.at[pl.ds(0, 2 * CAP), pl.ds(0, len(alls) * LANES)], sent_sem)

    settle(HIN.at[pl.ds(0, len(alls))], sent_sem)
    settle(HIN.at[pl.ds(0, len(alls))], h_recv)
    @pl.when(c == 0)
    def _():
        settle(LV.at[pl.ds(0, devices)], l_recv)

    @pl.when(c == 1)
    def _():
        settle(LV.at[pl.ds(0, devices - 2)], l_recv)

    def finish(i, _):
        for k in range(HSPLIT):
            e = i * HSPLIT + k
            for l in range(tiles):
                bound = LV[e, l:l + 1, :]
                factor = LV[e, tiles + l:tiles + l + 1, :]
                h = HIN[e, :, l * LANES:(l + 1) * LANES]
                h = jnp.minimum(jnp.maximum(h, -bound), bound) * factor
                lanes = pl.ds(pl.multiple_of(e * width + l * LANES, LANES), LANES)
                out[:, lanes] = h.astype(jnp.bfloat16)
        return 0

    lax.fori_loop(0, groups, finish, 0)


def shards(tokens, routes, gate_weight, up_weight):
    devices = lax.axis_size("expert")
    replicas = lax.axis_size("replica")
    groups = devices // HSPLIT
    count, depth = tokens.shape
    width = gate_weight.shape[1]
    chunks = cuts(depth, chunk_sizes(depth))
    token_parts = [(0, 1), (1, len(chunks))]
    weight_parts = groups_of(len(chunks), 3)
    rows = devices * CAP
    tiles = width // LANES
    bf16, f32 = jnp.bfloat16, jnp.float32
    dma = pltpu.SemaphoreType.DMA
    anywhere = pl.BlockSpec(memory_space=pl.ANY)
    return pl.pallas_call(
        functools.partial(kernel, devices, replicas, chunks, token_parts, weight_parts),
        out_shape=pltpu.VMEM((CAP, devices * width), bf16),
        in_specs=[anywhere] * 4,
        out_specs=pl.BlockSpec(memory_space=pltpu.VMEM),
        scratch_shapes=[
            pltpu.VMEM((count, depth), bf16),
            pltpu.VMEM((routes.shape[1], count), jnp.int32),
            pltpu.VMEM((groups * CAP, count), bf16),
            pltpu.VMEM((groups * CAP, depth), bf16),
            pltpu.VMEM((rows, depth), bf16),
            pltpu.VMEM((2, depth, width), bf16),
            pltpu.VMEM((rows, width), f32),
            pltpu.VMEM((rows, width), f32),
            pltpu.VMEM((rows, width), f32),
            pltpu.VMEM((devices, CAP, width), f32),
            pltpu.VMEM((groups, 8, LANES), f32),
            pltpu.VMEM((devices, 8, LANES), f32),
            pltpu.VMEM((SKETCH * tiles, LANES), f32),
            pltpu.VMEM((2 * replicas, SKETCH * tiles, LANES), jnp.int16),
            pltpu.VMEM((2 * replicas * SKETCH * tiles, LANES), f32),
            pltpu.VMEM(((KMOM - 1) * (KMOM + 2) // 2, 2 * replicas * tiles, LANES), f32),
            pltpu.VMEM((replicas, 8, LANES), f32),
            pltpu.VMEM((2 * replicas, 8, LANES), f32),
            pltpu.VMEM((devices, 2 * tiles, LANES), f32),
            dma(()), dma((len(token_parts),)), dma((len(weight_parts),)), dma(()),
            dma((len(chunks),)), dma((len(chunks),)), dma(()),
            dma(()), dma(()), dma(()), dma(()), dma(()),
            pltpu.SemaphoreType.REGULAR, pltpu.SemaphoreType.REGULAR,
        ],
        compiler_params=pltpu.CompilerParams(
            collective_id=0, has_side_effects=True, vmem_limit_bytes=56 * 1024 * 1024),
    )(tokens, pltpu.with_memory_space_constraint(routes.T, pltpu.HBM), gate_weight, up_weight)


def solution(mesh):
    in_specs = (
        P(("expert", "replica"), None),
        P(("expert", "replica"), None),
        P(None, "expert"),
        P(None, "expert"),
    )
    out_specs = P(("expert", "replica"), None)
    return jax.shard_map(shards, mesh=mesh, in_specs=in_specs, out_specs=out_specs, check_vma=False)
```

```python
import functools
import math

import jax
import jax.numpy as jnp
from jax import lax
from jax.experimental import pallas as pl
from jax.experimental.pallas import tpu as pltpu
from jax.sharding import PartitionSpec as P

HSPLIT = 4
CAP = 16
KMOM = 12
QITERS = 4
LANES = 128
UNIT = 512
TAIL = 256
WIDEST = 2
ROWS = 32
BATCH = 64
SKETCH = 12
STEPS = 32767.0

QUANTILE_LEVEL = 0.99
EPSILON = 1e-06
MESH = pl.DeviceIdType.MESH

SIN_TERMS = [(-1.0) ** i / math.factorial(2 * i + 1) for i in range(7)]
COS_TERMS = [(-1.0) ** i / math.factorial(2 * i) for i in range(8)]


def polynomial(x, terms):
    terms = [jnp.full_like(x, term) for term in terms]
    while len(terms) > 1:
        pairs = [terms[i] + terms[i + 1] * x for i in range(0, len(terms) - 1, 2)]
        terms = pairs + terms[2 * len(pairs):]
        x = x * x
    return terms[0]


def sin_cos(half_turns):
    turns = jnp.floor(half_turns + 0.5)
    rest = (half_turns - turns) * math.pi
    sign = 1.0 - 2.0 * (turns - 2.0 * jnp.floor(turns * 0.5))
    square = rest * rest
    return sign * rest * polynomial(square, SIN_TERMS), sign * polynomial(square, COS_TERMS)


def tree(terms):
    while len(terms) > 1:
        terms = [functools.reduce(jnp.add, terms[i:i + 2]) for i in range(0, len(terms), 2)]
    return terms[0]


def clip_fraction(coefficient):
    start = 1.0 - QUANTILE_LEVEL
    total = jnp.zeros_like(coefficient[0])
    for k in range(1, KMOM, 2):
        total = total + coefficient[k - 1] * ((1.0 if k % 4 == 1 else -1.0) / k)
    angle = start - (2.0 / math.pi) * total
    for _ in range(QITERS - 1):
        sine, cosine = sin_cos(angle)
        double = 2.0 * cosine
        stride = double * double - 2.0
        waves = [-sine, jnp.zeros_like(sine), sine, double * sine]
        for k in range(3, KMOM):
            waves.append(stride * waves[k - 1] - waves[k - 3])
        angle = start - (2.0 / math.pi) * tree([
            coefficient[k - 1] * (waves[k + 1] * (1.0 / k)) for k in range(1, KMOM)])
    return 0.5 * (1.0 + sin_cos(angle)[1])


def rebased(ratio):
    shift = ratio - 1.0
    twice = 2.0 * shift
    zero = jnp.zeros_like(ratio)
    before, current = [jnp.ones_like(ratio)], [shift, ratio]
    rows = [current]
    for k in range(2, KMOM):
        padded = current + [zero, zero]
        following = [ratio * current[1] + twice * current[0] - before[0]]
        for m in range(1, k + 1):
            left = current[m - 1] if m > 1 else 2.0 * current[0]
            value = ratio * (left + padded[m + 1]) if m < k - 1 else ratio * left
            if m < k:
                value = value + twice * current[m]
            if m < k - 1:
                value = value - before[m]
            following.append(value)
        before, current = current, following
        rows.append(current)
    return rows


def cuts(total, sizes):
    edges = [0]
    for size in sizes:
        edges.append(edges[-1] + size)
    return [(i, j - i) for i, j in zip(edges, edges[1:])]


def chunk_sizes(depth):
    ends = [UNIT, UNIT, UNIT]
    units = (depth - sum(ends)) // UNIT - 1
    middle, odd = divmod(units, 2)
    first = depth - sum(ends) - UNIT * units
    return [first] + [2 * UNIT] * middle + [UNIT] * odd + ends


def groups_of(count, parts):
    edges = [count * i // parts for i in range(parts + 1)]
    return list(zip(edges, edges[1:]))


def kernel(
    devices, replicas, chunks, token_parts, weight_parts,
    tok, rt, wg, wu, out,
    T, RT, SEL, Y, X, W, AG, AU, H, HIN, CS, CN, SK, Q, F, B, CT, CE, LV,
    rt_sem, tok_sem, w_sem, sent_sem, x_recv, f_recv, e_recv,
    n_recv, q_recv, z_recv, h_recv, l_recv, go,
):
    groups = devices // HSPLIT
    half = devices // 2 * CAP
    width = W.shape[2]
    tiles = width // LANES
    rows = devices * CAP
    me = lax.axis_index("expert")
    z = lax.axis_index("replica")
    c = me % 2
    p = (me // 2) % 2
    a = me // HSPLIT
    partner = me + 1 - 2 * c
    lead = me + 1 - c
    last = len(chunks) - 1

    def pos(j):
        return (j % 2) * (devices // 2) + j // 2

    def other(dg, dp, dc):
        return HSPLIT * ((a + dg) % groups) + 2 * ((p + dp) % 2) + (c + dc) % 2

    combos = [(dg, dp) for dg in range(groups) for dp in range(2) if (dg, dp) != (0, 0)]
    combos = combos[::-1]
    alls = [
        (dg, dp, dc)
        for dg in range(groups) for dp in range(2) for dc in range(2)
        if (dg, dp, dc) != (0, 0, 0)
    ][::-1]
    peers = []
    for i in range(replicas - 1):
        up, down = i + (i >= z), replicas - 1 - i - (replicas - 1 - i <= z)
        peers.append(jnp.where(z < replicas // 2, down, up))

    def block(j):
        return pl.ds(pl.multiple_of(pos(j) * CAP, CAP), CAP)

    def columns(ch):
        return pl.ds(chunks[ch][0], chunks[ch][1])

    def span(first, end):
        return pl.ds(chunks[first][0], chunks[end - 1][0] + chunks[end - 1][1] - chunks[first][0])

    def remote(src, dst, send_sem, recv_sem, device):
        return pltpu.make_async_remote_copy(
            src_ref=src, dst_ref=dst, send_sem=send_sem, recv_sem=recv_sem,
            device_id=device, device_id_type=MESH)

    def settle(ref, sem):
        pltpu.make_async_copy(ref, ref, sem).wait()

    def load_tokens(i):
        part = span(*token_parts[i])
        return pltpu.make_async_copy(tok.at[:, part], T.at[:, part], tok_sem.at[i])

    def load_weights(i):
        part = span(*weight_parts[i])
        return [
            pltpu.make_async_copy(w.at[part], W.at[k, part], w_sem.at[i])
            for k, w in enumerate((wg, wu))
        ]

    load_routes = pltpu.make_async_copy(rt, RT, rt_sem)
    load_tokens(0).start()
    load_routes.start()

    barrier = pltpu.get_barrier_semaphore()
    for combo in alls:
        pl.semaphore_signal(barrier, inc=1, device_id=(other(*combo), z), device_id_type=MESH)

    @pl.when(me == 0)
    def _():
        for peer in peers:
            pl.semaphore_signal(barrier, inc=1, device_id=(me, peer), device_id_type=MESH)

    for i in range(1, len(token_parts)):
        load_tokens(i).start()

    load_routes.wait()
    routes = RT[...]
    count = routes.shape[1]
    t_from = lax.broadcasted_iota(jnp.int32, (count, count), 0)
    t_to = lax.broadcasted_iota(jnp.int32, (count, count), 1)
    earlier = jnp.where(t_from < t_to, 1.0, 0.0).astype(jnp.bfloat16)
    named = [
        jnp.sum(jnp.where(routes == (a + dg) % groups, 1.0, 0.0), axis=0, keepdims=True)
        for dg in range(groups)
    ]
    table = jnp.concatenate(
        [jnp.broadcast_to(n, (CAP, count)) for n in named], axis=0)
    before = jnp.dot(table.astype(jnp.bfloat16), earlier, preferred_element_type=jnp.float32)
    slot = (lax.broadcasted_iota(jnp.int32, (groups * CAP, count), 0) % CAP).astype(jnp.float32)
    picks = jnp.where(before == slot, table, 0.0)
    SEL[...] = picks.astype(jnp.bfloat16)

    def gather(ch):
        part = columns(ch)
        picked = jnp.dot(
            SEL[...], T[:, part], preferred_element_type=jnp.float32).astype(jnp.bfloat16)
        Y[:, part] = picked

        X[block(me), part] = picked[:CAP]

    def send_rows(ch, pairs):
        part = columns(ch)
        for dg, dp in pairs:
            remote(
                Y.at[pl.ds(dg * CAP, CAP), part], X.at[block(me), part],
                sent_sem, x_recv.at[ch], (other(dg, dp, 0), z)).start()

    def send_across(pairs):
        part = columns(last)

        @pl.when(c == 0)
        def _():
            for dg, dp in pairs:
                remote(
                    Y.at[pl.ds(dg * CAP, CAP), part], X.at[block(me), part],
                    sent_sem, e_recv, (other(dg, dp, 1), z)).start()

    load_tokens(0).wait()
    gather(0)
    for i in range(len(weight_parts)):
        for copy in load_weights(i):
            copy.start()
    pl.semaphore_wait(barrier, len(alls) + jnp.where(me == 0, len(peers), 0))
    send_rows(0, combos)

    filled = jnp.sum(picks, axis=1, keepdims=True)
    for dg in range(groups):
        total = jnp.sum(filled[dg * CAP:(dg + 1) * CAP], axis=0, keepdims=True)
        CS[dg] = jnp.broadcast_to(total, (8, LANES))
    CN[me] = CS[0]
    for dg, dp, dc in alls:
        remote(CS.at[dg], CN.at[me], sent_sem, n_recv, (other(dg, dp, dc), z)).start()

    for i, (first, end) in enumerate(token_parts):
        if i:
            load_tokens(i).wait()
        for ch in range(max(first, 1), end):
            gather(ch)
            if ch < last - 1:
                send_rows(ch, combos)
    far = [pair for pair in combos if 0 not in pair]
    near = [pair for pair in combos if 0 in pair]
    for pairs in (far, near):
        for ch in (last - 1, last):
            send_rows(ch, pairs)
        send_across(pairs)
    send_across([(0, 0)])

    @pl.when(me == 0)
    def _():
        for peer in peers:
            pl.semaphore_signal(go, inc=1, device_id=(me, peer), device_id_type=MESH)

    own = pl.ds(pl.multiple_of(c * half, half), half)

    def receive(ch):
        settle(X.at[pl.ds(0, len(combos) * CAP), columns(ch)], x_recv.at[ch])

    def forward(ch):
        part = columns(ch)
        remote(
            X.at[own, part], X.at[own, part], sent_sem, f_recv.at[ch], (partner, z)).start()

    def collect(ch):
        receive(ch)
        forward(ch)

    def arrive(ch):
        part = columns(ch)
        if ch < last:
            settle(X.at[pl.ds(0, half), part], f_recv.at[ch])
        else:
            @pl.when(c == 0)
            def _():
                receive(ch)
                settle(X.at[pl.ds(0, half), part], f_recv.at[ch])

            @pl.when(c == 1)
            def _():
                settle(X.at[pl.ds(0, (len(combos) + 1) * CAP), part], e_recv)

        for i, (first, end) in enumerate(weight_parts):
            if first == ch:
                settle(W.at[:, span(first, end)], w_sem.at[i])

    def multiply(ch):
        arrive(ch)
        part = columns(ch)
        x = X[:, part]
        for k, A in enumerate((AG, AU)):
            product = jnp.dot(x, W[k, part, :], preferred_element_type=jnp.float32)
            A[...] = A[...] + product if ch else product

    def release():
        @pl.when(me == 0)
        def _():
            pl.semaphore_wait(go, len(peers))
            for combo in alls:
                pl.semaphore_signal(go, inc=1, device_id=(other(*combo), z), device_id_type=MESH)

    def share_count():
        settle(CN.at[pl.ds(0, len(alls))], n_recv)
        total = functools.reduce(jnp.add, [CN[j] for j in range(devices)])
        CT[z] = total

        @pl.when(me != 0)
        def _():
            pl.semaphore_wait(go, 1)

        @pl.when(c == 1)
        def _():
            for peer in peers:
                remote(CT.at[z], CT.at[z], sent_sem, z_recv, (me, peer)).start()

    collect(0)
    steady = last - 4
    for ch in range(1, steady + 1):
        collect(ch)
        multiply(ch - 1)
        if ch == 2:
            release()
        if ch == steady:
            share_count()

    @pl.when(c == 0)
    def _():
        multiply(steady)
        for ch in range(steady + 1, last - 1):
            collect(ch)
            multiply(ch)
        collect(last - 1)

    @pl.when(c == 1)
    def _():
        collect(steady + 1)
        collect(steady + 2)
        multiply(steady)
        collect(last - 1)
        collect(last)
        for ch in range(steady + 1, last - 1):
            multiply(ch)

    arrive(last - 1)
    arrive(last)
    part = span(last - 1, last + 1)
    x = X[:, part]
    strip = min(2 * LANES, width)
    tops = []
    for n in range(0, width, strip):
        lanes = slice(n, n + strip)
        g, u = (
            A[:, lanes] + jnp.dot(x, W[k, part, lanes], preferred_element_type=jnp.float32)
            for k, A in enumerate((AG, AU)))
        h = g / (1.0 + jnp.exp(-g)) * u
        H[:, lanes] = h
        tops.append(jnp.max(jnp.abs(h), axis=0, keepdims=True))

    ceiling = jnp.concatenate(tops, axis=1) + EPSILON
    mine = c * replicas + z
    for l in range(tiles):
        CE[mine, l:l + 1, :] = ceiling[:, l * LANES:(l + 1) * LANES]

    def share(ref, send_sem, recv_sem, targets):
        for peer in targets:
            remote(ref, ref, send_sem, recv_sem, (lead, peer)).start()

    def share_here(ref, send_sem, recv_sem):
        @pl.when(c == 0)
        def _():
            remote(ref, ref, send_sem, recv_sem, (lead, z)).start()

    share(CE.at[mine], sent_sem, z_recv, peers)
    share_here(CE.at[mine], sent_sem, z_recv)
    scale = 2.0 / ceiling
    here = CT[z, 0:1, :]
    empty = float(rows) - here
    stretch = STEPS / jnp.maximum(here, 1.0)
    even = lax.broadcasted_iota(jnp.int32, (SKETCH * tiles, LANES), 0) % 2 == 0
    bounds = [SKETCH * tiles * 2 // 3 // 16 * 16, SKETCH * tiles]
    sent = 0

    for l in range(tiles):
        lanes = slice(l * LANES, (l + 1) * LANES)
        scale_l = scale[:, lanes]

        def sketch(i, sums):
            part = pl.ds(pl.multiple_of(i * BATCH, BATCH), BATCH)
            scaled = jnp.abs(H[part, lanes]) * scale_l - 1.0
            double = 2.0 * scaled
            previous, current = jnp.ones_like(scaled), scaled
            waves = []
            for _ in range(KMOM // 2):
                waves.append(current)
                previous, current = current, double * current - previous
            waves += [wave * waves[-1] for wave in waves[:-1]]
            return tuple(
                total + jnp.sum(wave.reshape(BATCH // 8, 8, LANES), axis=0)
                for total, wave in zip(sums, waves))

        zero = jnp.zeros((8, LANES), jnp.float32)
        sums = lax.fori_loop(0, rows // BATCH, sketch, (zero,) * (KMOM - 1), unroll=True)
        SK[l * SKETCH:l * SKETCH + 1, :] = jnp.zeros((1, LANES), jnp.float32)
        half_order = KMOM // 2
        found = [jnp.sum(value, axis=0, keepdims=True) for value in sums]
        for k in range(half_order + 1, KMOM):
            found[k - 1] = 2.0 * found[k - 1] - found[2 * half_order - k - 1]
        for k in range(1, KMOM):
            SK[l * SKETCH + k:l * SKETCH + k + 1, :] = found[k - 1]
        while bounds and bounds[0] <= (l + 1) * SKETCH:
            part = slice(sent, bounds[0])
            held = SK[part, :] + jnp.where(even[part], -empty, empty)
            code = jnp.minimum(jnp.maximum(held * stretch, -STEPS), STEPS)
            Q[mine, part, :] = jnp.floor(code + 0.5).astype(jnp.int32).astype(jnp.int16)
            share(Q.at[mine, part, :], sent_sem, q_recv, peers[:1])
            sent = bounds.pop(0)
    share(Q.at[mine], sent_sem, q_recv, peers[1:])
    share_here(Q.at[mine], sent_sem, q_recv)
    for dg, dp, dc in alls:
        j = other(dg, dp, dc)
        remote(H.at[block(j), :], HIN.at[me], sent_sem, h_recv, (j, z)).start()

    HIN[me] = H[block(me), :]
    def calibrate():
        settle(F.at[pl.ds(0, 8 * (len(peers) + 2 * replicas - 1)), :], z_recv)
        local = [CE[i, 0:tiles, :] for i in range(2 * replicas)]
        common = [
            functools.reduce(jnp.maximum, local[k * replicas:(k + 1) * replicas])
            for k in range(2)
        ]
        ratio = jnp.concatenate(
            [value / common[i // replicas] for i, value in enumerate(local)], axis=0)
        here = [CT[r, 0:tiles, :] for r in range(replicas)]
        total = functools.reduce(jnp.add, here)
        part = jnp.concatenate([value / total for value in here] * 2, axis=0)

        def added(value):
            value = [value[i * tiles:(i + 1) * tiles] for i in range(2 * replicas)]
            return jnp.concatenate([
                functools.reduce(jnp.add, value[k * replicas:(k + 1) * replicas])
                for k in range(2)
            ], axis=0)

        scaled = part * (1.0 / STEPS)
        starts = []
        for k, row in enumerate(rebased(ratio)):
            starts.append(k * (k + 3) // 2)
            for m, value in enumerate(row):
                B[starts[k] + m] = value * (scaled if m else part)
        settle(Q.at[pl.ds(0, 2 * replicas - 1)], q_recv)
        for i in range(2 * replicas):
            F[i * SKETCH * tiles:(i + 1) * SKETCH * tiles, :] = (
                Q[i].astype(jnp.int32).astype(jnp.float32))
        codes = [
            F[pl.ds(k, 2 * replicas * tiles, stride=SKETCH), :] for k in range(1, KMOM)]
        level = clip_fraction([
            added(tree([B[starts[k]]] + [
                B[starts[k] + m + 1] * codes[m] for m in range(k + 1)]))
            for k in range(KMOM - 1)
        ])
        for k in range(2):
            LV[me - 1 + k] = jnp.concatenate(
                [common[k] * level[k * tiles:(k + 1) * tiles], 1.0 / common[k]], axis=0)
        pair = LV.at[pl.ds(me - 1, 2)]
        for dg, dp, dc in alls:
            remote(pair, pair, sent_sem, l_recv, (other(dg, dp, dc), z)).start()

    @pl.when(c == 1)
    def _():
        calibrate()

    settle(X.at[pl.ds(0, len(combos) * CAP), :], sent_sem)
    settle(X.at[pl.ds(0, half), span(0, last)], sent_sem)
    settle(CN.at[pl.ds(0, len(alls))], sent_sem)
    settle(Q.at[pl.ds(0, len(peers))], sent_sem)
    settle(CE.at[pl.ds(0, len(peers))], sent_sem)

    @pl.when(c == 0)
    def _():
        settle(X.at[pl.ds(0, (len(combos) + 1) * CAP), columns(last)], sent_sem)
        settle(Q.at[0], sent_sem)
        settle(CE.at[0], sent_sem)

    @pl.when(c == 1)
    def _():
        settle(X.at[pl.ds(0, half), columns(last)], sent_sem)
        settle(CT.at[pl.ds(0, len(peers))], sent_sem)
        settle(X.at[pl.ds(0, 2 * CAP), pl.ds(0, len(alls) * LANES)], sent_sem)

    settle(HIN.at[pl.ds(0, len(alls))], sent_sem)
    settle(HIN.at[pl.ds(0, len(alls))], h_recv)
    @pl.when(c == 0)
    def _():
        settle(LV.at[pl.ds(0, devices)], l_recv)

    @pl.when(c == 1)
    def _():
        settle(LV.at[pl.ds(0, devices - 2)], l_recv)

    def finish(i, _):
        for k in range(HSPLIT):
            e = i * HSPLIT + k
            for l in range(tiles):
                bound = LV[e, l:l + 1, :]
                factor = LV[e, tiles + l:tiles + l + 1, :]
                h = HIN[e, :, l * LANES:(l + 1) * LANES]
                h = jnp.minimum(jnp.maximum(h, -bound), bound) * factor
                lanes = pl.ds(pl.multiple_of(e * width + l * LANES, LANES), LANES)
                out[:, lanes] = h.astype(jnp.bfloat16)
        return 0

    lax.fori_loop(0, groups, finish, 0)


def shards(tokens, routes, gate_weight, up_weight):
    devices = lax.axis_size("expert")
    replicas = lax.axis_size("replica")
    groups = devices // HSPLIT
    count, depth = tokens.shape
    width = gate_weight.shape[1]
    chunks = cuts(depth, chunk_sizes(depth))
    token_parts = [(0, 1), (1, len(chunks))]
    weight_parts = groups_of(len(chunks), 3)
    rows = devices * CAP
    tiles = width // LANES
    bf16, f32 = jnp.bfloat16, jnp.float32
    dma = pltpu.SemaphoreType.DMA
    anywhere = pl.BlockSpec(memory_space=pl.ANY)
    return pl.pallas_call(
        functools.partial(kernel, devices, replicas, chunks, token_parts, weight_parts),
        out_shape=pltpu.VMEM((CAP, devices * width), bf16),
        in_specs=[anywhere] * 4,
        out_specs=pl.BlockSpec(memory_space=pltpu.VMEM),
        scratch_shapes=[
            pltpu.VMEM((count, depth), bf16),
            pltpu.VMEM((routes.shape[1], count), jnp.int32),
            pltpu.VMEM((groups * CAP, count), bf16),
            pltpu.VMEM((groups * CAP, depth), bf16),
            pltpu.VMEM((rows, depth), bf16),
            pltpu.VMEM((2, depth, width), bf16),
            pltpu.VMEM((rows, width), f32),
            pltpu.VMEM((rows, width), f32),
            pltpu.VMEM((rows, width), f32),
            pltpu.VMEM((devices, CAP, width), f32),
            pltpu.VMEM((groups, 8, LANES), f32),
            pltpu.VMEM((devices, 8, LANES), f32),
            pltpu.VMEM((SKETCH * tiles, LANES), f32),
            pltpu.VMEM((2 * replicas, SKETCH * tiles, LANES), jnp.int16),
            pltpu.VMEM((2 * replicas * SKETCH * tiles, LANES), f32),
            pltpu.VMEM(((KMOM - 1) * (KMOM + 2) // 2, 2 * replicas * tiles, LANES), f32),
            pltpu.VMEM((replicas, 8, LANES), f32),
            pltpu.VMEM((2 * replicas, 8, LANES), f32),
            pltpu.VMEM((devices, 2 * tiles, LANES), f32),
            dma(()), dma((len(token_parts),)), dma((len(weight_parts),)), dma(()),
            dma((len(chunks),)), dma((len(chunks),)), dma(()),
            dma(()), dma(()), dma(()), dma(()), dma(()),
            pltpu.SemaphoreType.REGULAR,
        ],
        compiler_params=pltpu.CompilerParams(
            collective_id=0, has_side_effects=True, vmem_limit_bytes=56 * 1024 * 1024),
    )(tokens, pltpu.with_memory_space_constraint(routes.T, pltpu.HBM), gate_weight, up_weight)


def solution(mesh):
    in_specs = (
        P(("expert", "replica"), None),
        P(("expert", "replica"), None),
        P(None, "expert"),
        P(None, "expert"),
    )
    out_specs = P(("expert", "replica"), None)
    return jax.shard_map(shards, mesh=mesh, in_specs=in_specs, out_specs=out_specs, check_vma=False)
```
